32 devices in a mesh: dp: 4 (over x, core), seq: 2 (over y), tensor: 4 (over z).
Axes of the slice: x: 2, y: 2, z: 4, core: 2. Of those that a mesh axis runs over, the one named last changes fastest.
Arguments:
- history: bfloat16 [4, 8, 1024, 2048], P(None, 'dp', 'seq'), may hold values from -6 to 6
- positions: int32 [8, 1024], P('dp', 'seq'), may hold values from 0 to 2046, as said below
- lengths: int32 [8], P('dp'), may hold values from 256 to 1024, as said below
- cotangent: bfloat16 [8, 1024, 2048], P('dp', 'seq'), may hold values from -6 to 6
- mix_gain: float32 [2048], replicated, may hold values from 0.5 to 1.5
- mix_w1: bfloat16 [2048, 16], P(('dp', 'seq')), may hold values from -0.125 to 0.125
- mix_w2: float32 [16, 16], replicated, may hold values from -1.5 to 1.5
- ln_gain: float32 [4, 2048], replicated, may hold values from 0.5 to 1.5
- ln_bias: float32 [4, 2048], replicated, may hold values from -1.8 to 1.8
- qkv_weight: bfloat16 [3, 2048, 2048], P(None, ('dp', 'seq'), 'tensor'), may hold values from -0.125 to 0.125
- qkv_bias: float32 [3, 2048], P(None, 'tensor'), may hold values from -1.8 to 1.8
- out_weight: bfloat16 [2048, 2048], P(('dp', 'seq'), 'tensor'), may hold values from -2 to 2
- out_bias: float32 [2048], replicated, may hold values from -1.8 to 1.8
- up_weight: bfloat16 [2048, 8192], P(('dp', 'seq'), 'tensor'), may hold values from -0.125 to 0.125
- up_bias: float32 [8192], P('tensor'), may hold values from -1.8 to 1.8
- down_weight: bfloat16 [2048, 8192], P(('dp', 'seq'), 'tensor'), may hold values from -0.0625 to 0.0625
- down_bias: float32 [2048], replicated, may hold values from -1.8 to 1.8
Outputs:
- layer_out: bfloat16 [8, 1024, 2048], P('dp', 'seq')
- grad_history: float32 [4, 8, 1024, 2048], P(None, 'dp', 'seq')
- grad_mix_gain: float32 [2048], replicated
- grad_mix_w1: float32 [2048, 16], P(('dp', 'seq'))
- grad_mix_w2: float32 [16, 16], replicated
- grad_ln_gain: float32 [4, 2048], replicated
- grad_ln_bias: float32 [4, 2048], replicated
- grad_qkv_weight: float32 [3, 2048, 2048], P(None, ('dp', 'seq'), 'tensor')
- grad_qkv_bias: float32 [3, 2048], P(None, 'tensor')
- grad_out_weight: float32 [2048, 2048], P(('dp', 'seq'), 'tensor')
- grad_out_bias: float32 [2048], replicated
- grad_up_weight: float32 [2048, 8192], P(('dp', 'seq'), 'tensor')
- grad_up_bias: float32 [8192], P('tensor')
- grad_down_weight: float32 [2048, 8192], P(('dp', 'seq'), 'tensor')
- grad_down_bias: float32 [2048], replicated
The draws below stay inside these ranges and needn't reach their ends.
Inputs may be any that keep to these rules, and one draw needn't show every extreme that they name: Some slot has exactly 1024 valid tokens; the valid tokens of slot s are its first lengths[s] positions. `positions`: strictly increasing along each slot by steps of 1 or 2, the first being 0 or 1; some slot starts at 0 and steps by 2 throughout.
All inputs are finite; a program needn't handle non-finite values.
Results may differ from the reference program's by a relative error of at most 0.014.
The reference program's roundings to bfloat16 on the way count: a program that leaves them out, or rounds other values in their place, can miss the bound.
Values may be sent and summed in bfloat16 or wider, within the bound.
A program may use at most 320 MiB of HBM per device.

```python
import math
import jax
import jax.numpy as jnp
from jax import lax

D = 2048
HEADS = 16
HEAD_DIM = 128
ROT = 32
FF = 8192
MIX_HIDDEN = 16
DEPTH = 4
STREAMS = 4
SLOTS = 8
LEN = 1024


def draw_lengths(key, part):
    drawn = jax.random.randint(jax.random.fold_in(key, 11), (SLOTS,), LEN // 4, LEN + 1)
    chosen = jax.random.randint(jax.random.fold_in(key, 12), (), 0, SLOTS)
    return jnp.where(jnp.arange(SLOTS) == chosen, LEN, drawn).astype(jnp.int32)


def draw_positions(key, part):
    strides = jax.random.randint(jax.random.fold_in(key, 13), (SLOTS, LEN), 1, 3)
    chosen = jax.random.randint(jax.random.fold_in(key, 14), (), 0, SLOTS)
    fixed_steps = jnp.where(jnp.arange(LEN) == 0, 1, 2)[None, :]
    strides = jnp.where((jnp.arange(SLOTS) == chosen)[:, None], fixed_steps, strides)
    return (jnp.cumsum(strides, axis=1) - 1).astype(jnp.int32)


def shard_levels(rng, shape, cuts, least, top_value):
    def one(axis_at, blocks):
        steps = jax.random.uniform(jax.random.fold_in(jax.random.fold_in(rng, 6), axis_at), (blocks,), jnp.float32, least / len(cuts), top_value / len(cuts))
        return jnp.repeat(jnp.exp(steps), shape[axis_at] // blocks).reshape((-1,) + (1,) * (len(shape) - axis_at - 1))

    level = one(*cuts[0])
    for cut in cuts[1:]:
        level = level * one(*cut)
    return level


def scatter_about(own_key, shape, deviation, bound, shards=(), held_as=jnp.bfloat16):
    values = deviation * jax.random.normal(own_key, shape, jnp.float32)
    if shards:
        values = values * shard_levels(own_key, shape, shards, -0.22, 0.18)
    return jnp.clip(values, -bound, bound).astype(held_as)


def setup_inputs(seed: int = 0) -> dict:
    keys = jax.random.split(jax.random.key(seed), 18)
    return {
        "history": scatter_about(keys[0], (DEPTH, SLOTS, LEN, D), 1.0, 6.0, ((1, 4), (2, 2))),
        "positions": draw_positions(jax.random.fold_in(keys[17], 71), 0),
        "lengths": draw_lengths(jax.random.fold_in(keys[17], 71), 0),
        "cotangent": scatter_about(keys[3], (SLOTS, LEN, D), 1.0, 6.0, ((0, 4), (1, 2))),
        "mix_gain": jnp.clip(1.0 + 0.1 * jax.random.normal(keys[4], (D,), jnp.float32), 0.5, 1.5),
        "mix_w1": scatter_about(keys[5], (D, MIX_HIDDEN), D ** -0.5, 0.125, ((0, 8),)),
        "mix_w2": scatter_about(keys[6], (MIX_HIDDEN, STREAMS * DEPTH), MIX_HIDDEN ** -0.5, 1.5, (), jnp.float32),
        "ln_gain": jnp.clip(1.0 + 0.1 * jax.random.normal(keys[7], (4, D), jnp.float32), 0.5, 1.5),
        "ln_bias": scatter_about(keys[8], (4, D), 0.3, 1.8, (), jnp.float32),
        "qkv_weight": scatter_about(keys[9], (3, D, D), D ** -0.5, 0.125, ((1, 8), (2, 4))),
        "qkv_bias": scatter_about(keys[10], (3, D), 0.3, 1.8, ((1, 4),), jnp.float32),
        "out_weight": scatter_about(keys[11], (D, D), (4 * D // LEN) ** -0.5, 2.0, ((0, 8), (1, 4))),
        "out_bias": scatter_about(keys[12], (D,), 0.3, 1.8, (), jnp.float32),
        "up_weight": scatter_about(keys[13], (D, FF), D ** -0.5, 0.125, ((0, 8), (1, 4))),
        "up_bias": scatter_about(keys[14], (FF,), 0.3, 1.8, ((0, 4),), jnp.float32),
        "down_weight": scatter_about(keys[15], (D, FF), FF ** -0.5, 0.0625, ((0, 8), (1, 4))),
        "down_bias": scatter_about(keys[16], (D,), 0.3, 1.8, (), jnp.float32),
    }


EXACT = lax.Precision.HIGHEST
RMS_EPSILON = 1e-06
NORM_EPSILON = 1e-05

@jax.custom_vjp
def low(v):
    return lax.optimization_barrier(v.astype(jnp.bfloat16)).astype(jnp.float32)

@jax.custom_vjp
def low_back(v):
    return v

def low_keep(v):
    return (low(v), None)

def low_pass(kept, grad):
    return (grad,)

def back_keep(v):
    return (v, None)

def back_low(kept, grad):
    return (low(grad),)
low.defvjp(low_keep, low_pass)
low_back.defvjp(back_keep, back_low)

def layer_norm(values, norm_gain, norm_bias):
    centred = values - lax.optimization_barrier(jnp.mean(values, axis=-1, keepdims=True))
    variance = lax.optimization_barrier(jnp.mean(centred * centred, axis=-1, keepdims=True))
    return centred * lax.rsqrt(variance + NORM_EPSILON) * norm_gain + norm_bias

def rms_scale(values, norm_gain):
    return values * lax.rsqrt(lax.optimization_barrier(jnp.mean(values * values, axis=-1, keepdims=True)) + RMS_EPSILON) * norm_gain

def exact_gelu(values):
    return jax.nn.gelu(values, approximate=False)

def rotary_tables(positions):
    exponents = jnp.arange(0, ROT, 2).astype(jnp.float32) / ROT
    inverse = jnp.power(10000.0, -exponents)
    phases = positions.astype(jnp.float32)[:, None] * inverse[None, :]
    phases = jnp.concatenate([phases, phases], axis=-1)[:, None, :]
    return (jnp.cos(phases), jnp.sin(phases))

def rotary(values, cosines, sines):
    rot_width = cosines.shape[-1]
    half_width = rot_width // 2
    turned = values[..., :rot_width]
    rotated = jnp.concatenate([-turned[..., half_width:], turned[..., :half_width]], axis=-1)
    return jnp.concatenate([turned * cosines + rotated * sines, values[..., rot_width:]], axis=-1)

def combine_layers(layers, latest, mix_weights):
    combined = []
    for target in range(mix_weights.shape[1]):
        running = latest
        for source in range(layers.shape[0]):
            running = running + mix_weights[:, target, source][:, None] * layers[source]
        combined.append(running)
    return combined

def head_attend(pieces, allowed):
    queries, keys_in, values_in = pieces
    scores = low_back(jnp.dot(queries, keys_in.T, precision=EXACT) * (1.0 / math.sqrt(HEAD_DIM)))
    scores = jnp.where(allowed, scores, -1e+30)
    row_max = lax.optimization_barrier(jnp.max(scores, axis=-1, keepdims=True))
    weights = jnp.exp(scores - row_max)
    probabilities = weights / lax.optimization_barrier(jnp.sum(weights, axis=-1, keepdims=True))
    return jnp.dot(low(probabilities), values_in, precision=EXACT)

def layer_fn(params, layers, place_ids, length):
    mix_gain, mix_w1, mix_w2, ln_gain, ln_bias, qkv_weight, qkv_bias, out_weight, out_bias, up_weight, up_bias, down_weight, down_bias = params
    latest = layers[DEPTH - 1]
    normed = low(rms_scale(latest, mix_gain))
    mix_pre = low_back(jnp.dot(normed, mix_w1, precision=EXACT))
    mix_act = exact_gelu(mix_pre)
    mix_weights = jnp.dot(mix_act, mix_w2, precision=EXACT).reshape(LEN, STREAMS, DEPTH)
    combined = combine_layers(layers, latest, mix_weights)
    cosines, sines = rotary_tables(place_ids)
    projected = []
    for branch in range(3):
        normed_in = low(layer_norm(combined[branch], ln_gain[branch], ln_bias[branch]))
        projected.append(low_back(jnp.dot(normed_in, qkv_weight[branch], precision=EXACT) + qkv_bias[branch]))
    queries = low(rotary(projected[0].reshape(LEN, HEADS, HEAD_DIM), cosines, sines))
    key_rows = low(rotary(projected[1].reshape(LEN, HEADS, HEAD_DIM), cosines, sines))
    value_rows = low(projected[2]).reshape(LEN, HEADS, HEAD_DIM)
    places = jnp.arange(LEN, dtype=jnp.int32)
    allowed = (places[None, :] <= places[:, None]) & (places[None, :] < length)
    attended = lax.map(jax.checkpoint(lambda pieces: head_attend(pieces, allowed)), (queries.transpose(1, 0, 2), key_rows.transpose(1, 0, 2), value_rows.transpose(1, 0, 2)))
    attn_vals = low(low_back(attended.transpose(1, 0, 2).reshape(LEN, D)))
    attn_out = low_back(jnp.dot(attn_vals, out_weight.T, precision=EXACT) + out_bias)
    hidden = combined[STREAMS - 1] + attn_out
    mlp_in = low(layer_norm(hidden, ln_gain[3], ln_bias[3]))
    up_lin = low_back(jnp.dot(mlp_in, up_weight, precision=EXACT) + up_bias)
    up_act = low(exact_gelu(up_lin))
    mlp_out = low_back(jnp.dot(up_act, down_weight.T, precision=EXACT) + down_bias)
    return hidden + mlp_out

def reference(history, positions, lengths, cotangent, mix_gain, mix_w1, mix_w2, ln_gain, ln_bias, qkv_weight, qkv_bias, out_weight, out_bias, up_weight, up_bias, down_weight, down_bias):
    params = tuple((item.astype(jnp.float32) for item in (mix_gain, mix_w1, mix_w2, ln_gain, ln_bias, qkv_weight, qkv_bias, out_weight, out_bias, up_weight, up_bias, down_weight, down_bias)))
    grads_zero = tuple((jnp.zeros_like(item) for item in params))

    def slot_step(carried, slot_item):
        layers, place_ids, length, cot_slot = slot_item
        layers_wide = layers.astype(jnp.float32)
        result, pullback = jax.vjp(lambda weights, inputs: layer_fn(weights, inputs, place_ids, length), params, layers_wide)
        valid_rows = (jnp.arange(LEN, dtype=jnp.int32) < length)[:, None]
        grad_result = jnp.where(valid_rows, cot_slot.astype(jnp.float32), 0.0)
        grad_params, grad_layers = pullback(grad_result)
        carried = tuple((first + second for first, second in zip(carried, grad_params)))
        return (carried, (result.astype(jnp.bfloat16), grad_layers))
    summed, (outputs, grad_hist) = lax.scan(slot_step, grads_zero, (history.transpose(1, 0, 2, 3), positions, lengths, cotangent))
    return (outputs, grad_hist.transpose(1, 0, 2, 3), summed[0], summed[1], summed[2], summed[3], summed[4], summed[5], summed[6], summed[7], summed[8], summed[9], summed[10], summed[11], summed[12])
```

```python
import functools
import math

import jax
import jax.numpy as jnp
from jax import lax
from jax.experimental import pallas as pl
from jax.experimental.pallas import tpu as pltpu
from jax.sharding import PartitionSpec as P

HEAD_DIM = 128
ROT = 32
STREAMS = 4
EXACT = lax.Precision.HIGHEST
RMS_EPSILON = 1e-06
NORM_EPSILON = 1e-05
BF = jnp.bfloat16
F32 = jnp.float32
MESH = pl.DeviceIdType.MESH
ANY = pl.BlockSpec(memory_space=pl.ANY)
VMEM = pl.BlockSpec(memory_space=pltpu.VMEM)
RING = 4
NN = (((1,), (0,)), ((), ()))
NT = (((1,), (1,)), ((), ()))
TN = (((0,), (0,)), ((), ()))


def dot(left, right, dims=NN, precision=None):
    return lax.dot_general(left, right, dims, precision=precision, preferred_element_type=F32)


def normal_cdf(values):
    return 0.5 * (1.0 + lax.erf(values * math.sqrt(0.5)))


def gelu_slope(values, cdf):
    return cdf + values * (jnp.exp(-0.5 * values * values) * (1.0 / math.sqrt(2.0 * math.pi)))


def mean_last(values):
    return jnp.mean(values, axis=-1, keepdims=True)


def rows_loop(total, step, body):
    def one(index, carry):
        body(pl.ds(pl.multiple_of(index * step, step), step))
        return carry

    lax.fori_loop(0, total // step, one, 0)


def params(limit_mib, collective_id=None):
    if collective_id is None:
        return pltpu.CompilerParams(vmem_limit_bytes=limit_mib << 20)
    return pltpu.CompilerParams(
        vmem_limit_bytes=limit_mib << 20, collective_id=collective_id, has_side_effects=True
    )


def cost(micros):
    return pl.CostEstimate(flops=0, bytes_accessed=int(micros * 3.0e6), transcendentals=0)


def front_kernel(hist, gain, w1, w2, lg, lb, normed_out, resid_out, mix_out, pre_out, scratch):
    depth, rows, _ = hist.shape

    def rms(part):
        wide = hist[depth - 1, part, :].astype(F32)
        scale = lax.rsqrt(mean_last(wide * wide) + RMS_EPSILON)
        scratch[part, :] = (wide * scale * gain[...]).astype(BF)

    rows_loop(rows, 16, rms)
    pre = dot(scratch[...], w1[...])
    pre_out[...] = pre
    mix_out[...] = dot(pre * normal_cdf(pre), w2[...], precision=EXACT)

    def combine(part):
        layers = [hist[j, part, :].astype(F32) for j in range(depth)]
        mix = mix_out[part, :]
        for m in range(STREAMS):
            running = layers[depth - 1]
            for j in range(depth):
                running = running + mix[:, m * depth + j : m * depth + j + 1] * layers[j]
            if m == STREAMS - 1:
                resid_out[part, :] = running
            else:
                centred = running - mean_last(running)
                inverse = lax.rsqrt(mean_last(centred * centred) + NORM_EPSILON)
                normed = centred * inverse * lg[m : m + 1, :] + lb[m : m + 1, :]
                normed_out[m, part, :] = normed.astype(BF)

    rows_loop(rows, 16, combine)


def front(layers, gain, w1, w2, lg, lb):
    depth, rows, feats = layers.shape
    tile = min(128, rows)
    hidden = w1.shape[1]
    full = lambda shape: pl.BlockSpec(shape, lambda i: (0,) * len(shape))
    return pl.pallas_call(
        front_kernel,
        grid=(rows // tile,),
        in_specs=[
            pl.BlockSpec((depth, tile, feats), lambda i: (0, i, 0)),
            full((1, feats)),
            full(w1.shape),
            full(w2.shape),
            full(lg.shape),
            full(lb.shape),
        ],
        out_specs=[
            pl.BlockSpec((3, tile, feats), lambda i: (0, i, 0)),
            pl.BlockSpec((tile, feats), lambda i: (i, 0)),
            pl.BlockSpec((tile, STREAMS * depth), lambda i: (i, 0)),
            pl.BlockSpec((tile, hidden), lambda i: (i, 0)),
        ],
        out_shape=[
            jax.ShapeDtypeStruct((3, rows, feats), BF),
            jax.ShapeDtypeStruct((rows, feats), F32),
            jax.ShapeDtypeStruct((rows, STREAMS * depth), F32),
            jax.ShapeDtypeStruct((rows, hidden), F32),
        ],
        scratch_shapes=[pltpu.VMEM((tile, feats), BF)],
        compiler_params=params(40),
        cost_estimate=cost(20),
        name="front",
    )(layers, gain.reshape(1, feats), w1, w2, lg, lb)


def turn(values, tables, sign):
    cosines, low, high = tables
    return values * cosines + sign * (
        pltpu.roll(values, HEAD_DIM - ROT // 2, 1) * low + pltpu.roll(values, ROT // 2, 1) * high
    )


def rotary_tables(positions):
    exponents = jnp.arange(0, ROT, 2).astype(F32) / ROT
    inverse = jnp.power(10000.0, -exponents)
    phases = positions.astype(F32)[:, None] * inverse[None, :]
    cosines, sines = jnp.cos(phases), jnp.sin(phases)
    rows, half = phases.shape
    ones = jnp.ones((rows, HEAD_DIM - 2 * half), F32)
    none = jnp.zeros((rows, HEAD_DIM - 2 * half), F32)
    zero = jnp.zeros((rows, half), F32)
    return jnp.stack(
        [
            jnp.concatenate([cosines, cosines, ones], axis=1),
            jnp.concatenate([-sines, zero, none], axis=1),
            jnp.concatenate([zero, sines, none], axis=1),
        ]
    )


def proj_kernel(first, lhs, weight, bias, tables, out):
    branch = pl.program_id(0) + first
    value = dot(lhs[0], weight[...]) + bias[0]

    @pl.when(branch < 2)
    def _():
        tabs = (tables[0], tables[1], tables[2])
        for head in range(value.shape[1] // HEAD_DIM):
            cols = slice(head * HEAD_DIM, (head + 1) * HEAD_DIM)
            out[0, :, cols] = turn(value[:, cols], tabs, 1.0).astype(BF)

    @pl.when(branch >= 2)
    def _():
        out[0] = value.astype(BF)


def project(normed, weight, bias, tables, first):
    _, rows, feats = normed.shape
    count, width = bias.shape
    tile = min(256, rows)
    return pl.pallas_call(
        functools.partial(proj_kernel, first),
        grid=(count, rows // tile),
        in_specs=[
            pl.BlockSpec((1, tile, feats), lambda b, r: (b + first, r, 0)),
            pl.BlockSpec((feats, width), lambda b, r: (0, b)),
            pl.BlockSpec((1, 1, width), lambda b, r: (b, 0, 0)),
            pl.BlockSpec((3, tile, HEAD_DIM), lambda b, r: (0, r, 0)),
        ],
        out_specs=pl.BlockSpec((1, tile, width), lambda b, r: (b, r, 0)),
        out_shape=jax.ShapeDtypeStruct((count, rows, width), BF),
        compiler_params=params(40),
        cost_estimate=cost(4 * count),
        name="project",
    )(normed, weight, bias.reshape(count, 1, width), tables)


def attend_kernel(scalars, q, k, v, out):
    keys = k[...].reshape(-1, HEAD_DIM)
    values = v[...].reshape(-1, HEAD_DIM)
    length = scalars[pl.program_id(0)]
    offset = scalars[pl.num_programs(0)]
    scores = dot(q[0], keys, NT) * (1.0 / math.sqrt(HEAD_DIM))
    key_place = lax.broadcasted_iota(jnp.int32, scores.shape, 1)
    query_place = lax.broadcasted_iota(jnp.int32, scores.shape, 0) + offset
    scores = jnp.where((key_place <= query_place) & (key_place < length), scores, -1e30)
    weights = jnp.exp(scores - jnp.max(scores, axis=-1, keepdims=True))
    total = jnp.sum(weights, axis=-1, keepdims=True)
    probs = (weights * (1.0 / total)).astype(BF)
    out[0] = dot(probs, values).astype(BF)


def attend(scalars, q, kv, heads):
    seqs, _, slots, length, width = kv.shape
    block = (1, length, HEAD_DIM)
    return pl.pallas_call(
        attend_kernel,
        grid_spec=pltpu.PrefetchScalarGridSpec(
            num_scalar_prefetch=1,
            grid=(slots, heads),
            in_specs=[
                pl.BlockSpec(block, lambda s, h, _: (s, 0, h)),
                pl.BlockSpec((seqs, 1, 1, length, HEAD_DIM), lambda s, h, _: (0, 0, s, 0, h)),
                pl.BlockSpec((seqs, 1, 1, length, HEAD_DIM), lambda s, h, _: (0, 1, s, 0, h)),
            ],
            out_specs=pl.BlockSpec(block, lambda s, h, _: (s, 0, h)),
        ),
        out_shape=jax.ShapeDtypeStruct((slots, length, width), BF),
        compiler_params=params(40),
        cost_estimate=cost(15),
        name="attend",
    )(scalars, q.reshape(slots, length, width), kv, kv)


def attend_back_kernel(scalars, q, k, v, g, tables, dq_out, dkv_out):
    seqs = k.shape[0]
    scaling = 1.0 / math.sqrt(HEAD_DIM)
    keys = k[...].reshape(-1, HEAD_DIM)
    values = v[...].reshape(-1, HEAD_DIM)
    length = scalars[pl.program_id(0)]
    offset = scalars[pl.num_programs(0)]
    queries, grads = q[0], g[0]
    scores = dot(keys, queries, NT) * scaling
    key_place = lax.broadcasted_iota(jnp.int32, scores.shape, 0)
    query_place = lax.broadcasted_iota(jnp.int32, scores.shape, 1) + offset
    scores = jnp.where((key_place <= query_place) & (key_place < length), scores, -1e30)
    weights = jnp.exp(scores - jnp.max(scores, axis=0, keepdims=True))
    probs = weights * (1.0 / jnp.sum(weights, axis=0, keepdims=True))
    grad_probs = dot(values, grads, NT)
    mixed = jnp.sum(probs * grad_probs, axis=0, keepdims=True)
    grad_scores = (probs * (grad_probs - mixed)).astype(BF)
    grad_values = dot(probs.astype(BF), grads)
    grad_keys = dot(grad_scores, queries) * scaling
    shape = (seqs, -1, HEAD_DIM)
    dkv_out[:, 0, 0] = grad_keys.astype(BF).reshape(shape)
    dkv_out[:, 1, 0] = grad_values.astype(BF).reshape(shape)
    grad_queries = dot(grad_scores, keys, TN) * scaling
    tabs = (tables[0], tables[1], tables[2])
    dq_out[0] = turn(grad_queries, tabs, -1.0).astype(BF)


def attend_back(scalars, q, kv, g, tables, heads):
    seqs, _, slots, length, width = kv.shape
    block = (1, length, HEAD_DIM)
    own = pl.BlockSpec(block, lambda s, h, _: (s, 0, h))
    return pl.pallas_call(
        attend_back_kernel,
        grid_spec=pltpu.PrefetchScalarGridSpec(
            num_scalar_prefetch=1,
            grid=(slots, heads),
            in_specs=[
                own,
                pl.BlockSpec((seqs, 1, 1, length, HEAD_DIM), lambda s, h, _: (0, 0, s, 0, h)),
                pl.BlockSpec((seqs, 1, 1, length, HEAD_DIM), lambda s, h, _: (0, 1, s, 0, h)),
                own,
                pl.BlockSpec((3, length, HEAD_DIM), lambda s, h, _: (0, s, 0)),
            ],
            out_specs=[
                own,
                pl.BlockSpec((seqs, 2, 1, length, HEAD_DIM), lambda s, h, _: (0, 0, s, 0, h)),
            ],
        ),
        out_shape=[
            jax.ShapeDtypeStruct((slots, length, width), BF),
            jax.ShapeDtypeStruct((seqs, 2, slots, length, width), BF),
        ],
        compiler_params=params(48),
        cost_estimate=cost(25),
        name="attend_back",
    )(scalars, q.reshape(slots, length, width), kv, kv, g.reshape(slots, length, width), tables)


class Ring:
    def __init__(self, chunk):
        me = lax.axis_index("tensor")
        self.chunk, self.half = chunk, chunk // 2
        self.me = me
        self.right = lax.rem(me + 1, RING)
        self.left = lax.rem(me + RING - 1, RING)
        self.far = lax.rem(me + 2, RING)

    def at(self, index, shift=0):
        return pl.multiple_of(index * self.chunk + shift, self.half)

    def barrier(self):
        gate = pltpu.get_barrier_semaphore()
        for near in (self.left, self.right):
            pl.semaphore_signal(gate, inc=1, device_id={"tensor": near}, device_id_type=MESH)
        pl.semaphore_wait(gate, 2)


def remote(source, target, sems, index, device):
    return pltpu.make_async_remote_copy(
        src_ref=source,
        dst_ref=target,
        send_sem=sems.at[0, index],
        recv_sem=sems.at[1, index],
        device_id={"tensor": device},
        device_id_type=MESH,
    )


def product(lhs, rhs, start, count, write, step=512):
    total = rhs.shape[0]

    def one(cols):
        write(cols, dot(lhs[pl.ds(start, count), :], rhs[cols, :], NT))

    rows_loop(total, min(step, total), one)


class Scatter:
    def __init__(self, ring, lhs, rhs, far, near, far_in, near_in, sems):
        self.ring, self.lhs, self.rhs = ring, lhs, rhs
        self.far, self.near, self.far_in, self.near_in = far, near, far_in, near_in
        half = ring.half
        up, down = pl.ds(0, half), pl.ds(half, half)
        self.copies = [
            remote(far.at[0], far_in.at[0], sems, 0, ring.right),
            remote(far.at[1], far_in.at[1], sems, 1, ring.left),
            remote(near.at[0, down], near_in.at[0, down], sems, 2, ring.right),
            remote(near.at[1, up], near_in.at[1, up], sems, 3, ring.left),
            remote(near.at[0, up], near_in.at[0, up], sems, 4, ring.right),
            remote(near.at[1, down], near_in.at[1, down], sems, 5, ring.left),
        ]

    def begin(self):
        ring, half = self.ring, self.ring.half

        def far_half(which):
            def write(cols, value):
                self.far[which, :, cols] = value.astype(BF)

            product(self.lhs, self.rhs, ring.at(ring.far, which * half), half, write)
            self.copies[which].start()

        def near_half(which, device, part, copy):
            def write(cols, value):
                self.near[which, pl.ds(part * half, half), cols] = value.astype(BF)

            product(self.lhs, self.rhs, ring.at(device, part * half), half, write)
            self.copies[copy].start()

        far_half(0)
        far_half(1)
        near_half(0, ring.right, 1, 2)
        near_half(1, ring.left, 0, 3)

    def relay(self):
        ring, half = self.ring, self.ring.half

        def add_half(which, device, part, copy):
            self.copies[which].wait_recv()

            def write(cols, value):
                arrived = self.far_in[which, :, cols].astype(F32)
                self.near[which, pl.ds(part * half, half), cols] = (value + arrived).astype(BF)

            product(self.lhs, self.rhs, ring.at(device, part * half), half, write)
            self.copies[copy].start()

        add_half(0, ring.right, 0, 4)
        add_half(1, ring.left, 1, 5)

    def arrive(self):
        for copy in self.copies[2:]:
            copy.wait_recv()

    def finish(self):
        for copy in self.copies:
            copy.wait_send()


class Gather:
    def __init__(self, ring, own, out, sems, base, local_sem):
        half = ring.half

        def rows(index, shift=0, count=ring.chunk):
            return out.at[pl.ds(ring.at(index, shift), count), :]

        mine = rows(ring.me)
        self.local = pltpu.make_async_copy(own, mine, local_sem)
        self.first = [
            remote(own, mine, sems, base, ring.right),
            remote(own, mine, sems, base + 1, ring.left),
        ]
        up, down = rows(ring.left, 0, half), rows(ring.right, half, half)
        self.second = [
            remote(up, up, sems, base + 2, ring.right),
            remote(down, down, sems, base + 3, ring.left),
        ]

    def begin(self):
        for copy in self.first:
            copy.start()
        self.local.start()

    def relay(self):
        for arrived, onward in zip(self.first, self.second):
            arrived.wait_recv()
            onward.start()

    def finish(self):
        for copy in self.second:
            copy.wait_recv()
        for copy in self.first + self.second:
            copy.wait_send()
        self.local.wait()


def scatter_scratch(chunk, feats, count=1):
    half = chunk // 2
    lead = () if count == 1 else (count,)
    return [
        pltpu.VMEM(lead + (2, half, feats), BF),
        pltpu.VMEM(lead + (2, chunk, feats), BF),
        pltpu.VMEM(lead + (2, half, feats), BF),
        pltpu.VMEM(lead + (2, chunk, feats), BF),
    ]


def own_sum(scatter, total):
    ring = scatter.ring

    def write(cols, value):
        total[:, cols] = value

    product(scatter.lhs, scatter.rhs, ring.at(ring.me), ring.chunk, write)


def whole_sum(scatter, total, part):
    near = scatter.near_in
    return total[part, :] + near[0, part, :].astype(F32) + near[1, part, :].astype(F32)


def attn_out_kernel(
    lhs, rhs, resid, bias, lg, lb, hidden_out, mlp_out,
    far, near, far_in, near_in, total, base_rows, own, sems, local_sems,
):
    chunk, feats = total.shape
    ring = Ring(chunk)
    fetch = pltpu.make_async_copy(
        resid.at[pl.ds(ring.at(ring.me), chunk), :], base_rows, local_sems.at[0]
    )
    fetch.start()
    ring.barrier()
    scatter = Scatter(ring, lhs, rhs, far, near, far_in, near_in, sems)
    scatter.begin()
    scatter.relay()
    own_sum(scatter, total)
    fetch.wait()
    scatter.arrive()

    def norm(part):
        value = base_rows[part, :] + (whole_sum(scatter, total, part) + bias[...])
        hidden_out[part, :] = value
        centred = value - mean_last(value)
        inverse = lax.rsqrt(mean_last(centred * centred) + NORM_EPSILON)
        own[part, :] = (centred * inverse * lg[...] + lb[...]).astype(BF)

    rows_loop(chunk, 16, norm)
    gather = Gather(ring, own, mlp_out, sems, 6, local_sems.at[1])
    gather.begin()
    gather.relay()
    scatter.finish()
    gather.finish()


def attn_out(lhs, rhs, resid, bias, lg, lb):
    rows, feats = resid.shape
    chunk = rows // RING
    return pl.pallas_call(
        attn_out_kernel,
        in_specs=[VMEM, VMEM, ANY, VMEM, VMEM, VMEM],
        out_specs=[VMEM, ANY],
        out_shape=[
            jax.ShapeDtypeStruct((chunk, feats), F32),
            jax.ShapeDtypeStruct((rows, feats), BF),
        ],
        scratch_shapes=scatter_scratch(chunk, feats)
        + [
            pltpu.VMEM((chunk, feats), F32),
            pltpu.VMEM((chunk, feats), F32),
            pltpu.VMEM((chunk, feats), BF),
            pltpu.SemaphoreType.DMA((2, 10)),
            pltpu.SemaphoreType.DMA((2,)),
        ],
        compiler_params=params(48, 0),
        cost_estimate=cost(80),
        name="attn_out",
    )(lhs, rhs, resid, bias, lg, lb)


def norm_back(values, grads, gain):
    centred = values - mean_last(values)
    inverse = lax.rsqrt(mean_last(centred * centred) + NORM_EPSILON)
    normed = centred * inverse
    inner = grads * gain
    back = inverse * (inner - mean_last(inner) - normed * mean_last(inner * normed))
    return back, normed


def fold(values):
    rows, feats = values.shape
    return jnp.sum(values.reshape(rows // 8, 8, feats), axis=0)


def mlp_back_kernel(
    lhs, rhs, hidden, cot, lg, grad_out, small_out,
    far, near, far_in, near_in, total, cot_rows, own, sums, sems, local_sems,
):
    chunk, feats = total.shape
    ring = Ring(chunk)
    fetch = pltpu.make_async_copy(
        cot.at[pl.ds(ring.at(ring.me), chunk), :], cot_rows, local_sems.at[0]
    )
    fetch.start()
    ring.barrier()
    scatter = Scatter(ring, lhs, rhs, far, near, far_in, near_in, sems)
    scatter.begin()
    scatter.relay()
    own_sum(scatter, total)
    fetch.wait()
    sums[...] = jnp.zeros_like(sums)
    scatter.arrive()

    def back(part):
        grads = whole_sum(scatter, total, part)
        step, normed = norm_back(hidden[part, :], grads, lg[...])
        low = (cot_rows[part, :].astype(F32) + step).astype(BF)
        own[part, :] = low
        sums[0] += fold(grads * normed)
        sums[1] += fold(grads)
        sums[2] += fold(low.astype(F32))

    rows_loop(chunk, 16, back)
    gather = Gather(ring, own, grad_out, sems, 6, local_sems.at[1])
    gather.begin()
    for i in range(3):
        small_out[i : i + 1, :] = jnp.sum(sums[i], axis=0, keepdims=True)
    gather.relay()
    scatter.finish()
    gather.finish()


def mlp_back(lhs, rhs, hidden, cot, lg):
    rows, feats = cot.shape
    chunk = rows // RING
    return pl.pallas_call(
        mlp_back_kernel,
        in_specs=[VMEM, VMEM, VMEM, ANY, VMEM],
        out_specs=[ANY, VMEM],
        out_shape=[
            jax.ShapeDtypeStruct((rows, feats), BF),
            jax.ShapeDtypeStruct((3, feats), F32),
        ],
        scratch_shapes=scatter_scratch(chunk, feats)
        + [
            pltpu.VMEM((chunk, feats), F32),
            pltpu.VMEM((chunk, feats), BF),
            pltpu.VMEM((chunk, feats), BF),
            pltpu.VMEM((3, 8, feats), F32),
            pltpu.SemaphoreType.DMA((2, 10)),
            pltpu.SemaphoreType.DMA((2,)),
        ],
        compiler_params=params(52, 1),
        cost_estimate=cost(80),
        name="mlp_back",
    )(lhs, rhs, hidden, cot, lg)


def streams_back_kernel(
    lhs, rhs_q, rhs_kv, hist, mix, lg, grads_out, small_out,
    far, near, far_in, near_in, total, layers, mix_rows, own, sums, sems, local_sems,
):
    chunk, feats = total.shape
    depth = layers.shape[0]
    width = lhs.shape[2]
    ring = Ring(chunk)
    mine = pl.ds(ring.at(ring.me), chunk)
    fetch = pltpu.make_async_copy(hist.at[:, mine, :], layers, local_sems.at[0])
    fetch.start()
    fetch_mix = pltpu.make_async_copy(mix.at[mine, :], mix_rows, local_sems.at[1])
    fetch_mix.start()
    ring.barrier()
    weights = [
        rhs_q,
        rhs_kv.at[:, pl.ds(0, width)],
        rhs_kv.at[:, pl.ds(width, width)],
    ]
    scatters = [
        Scatter(
            ring, lhs.at[i], weights[i], far.at[i], near.at[i], far_in.at[i], near_in.at[i],
            sems.at[i],
        )
        for i in range(3)
    ]
    gathers = [
        Gather(ring, own.at[i], grads_out.at[i], sems.at[i], 6, local_sems.at[2 + i])
        for i in range(3)
    ]
    for scatter in scatters:
        scatter.begin()
    sums[...] = jnp.zeros_like(sums)
    fetch.wait()
    fetch_mix.wait()
    for i, scatter in enumerate(scatters):
        scatter.relay()
    for i, scatter in enumerate(scatters):
        own_sum(scatter, total)
        scatter.arrive()

        def back(part):
            grads = whole_sum(scatter, total, part)
            running = layers[depth - 1, part, :].astype(F32)
            weight = mix_rows[part, :]
            mixture = running
            for j in range(depth):
                at = i * depth + j
                mixture = mixture + weight[:, at : at + 1] * layers[j, part, :].astype(F32)
            step, normed = norm_back(mixture, grads, lg[i : i + 1, :])
            own[i, part, :] = step.astype(BF)
            sums[i, 0] += fold(grads * normed)
            sums[i, 1] += fold(grads)

        rows_loop(chunk, 16, back)
        gathers[i].begin()
        if i:
            gathers[i - 1].relay()
    for i in range(3):
        for j in range(2):
            small_out[j, i : i + 1, :] = jnp.sum(sums[i, j], axis=0, keepdims=True)
    gathers[2].relay()
    for scatter, gather in zip(scatters, gathers):
        scatter.finish()
        gather.finish()


def streams_back(lhs, rhs_q, rhs_kv, hist, mix, lg):
    depth, rows, feats = hist.shape
    chunk = rows // RING
    return pl.pallas_call(
        streams_back_kernel,
        in_specs=[VMEM, VMEM, VMEM, ANY, ANY, VMEM],
        out_specs=[ANY, VMEM],
        out_shape=[
            jax.ShapeDtypeStruct((3, rows, feats), BF),
            jax.ShapeDtypeStruct((2, 3, feats), F32),
        ],
        scratch_shapes=scatter_scratch(chunk, feats, 3)
        + [
            pltpu.VMEM((chunk, feats), F32),
            pltpu.VMEM((depth, chunk, feats), BF),
            pltpu.VMEM((chunk, mix.shape[1]), F32),
            pltpu.VMEM((3, chunk, feats), BF),
            pltpu.VMEM((3, 2, 8, feats), F32),
            pltpu.SemaphoreType.DMA((3, 2, 10)),
            pltpu.SemaphoreType.DMA((5,)),
        ],
        compiler_params=params(58, 2),
        cost_estimate=cost(220),
        name="streams_back",
    )(lhs, rhs_q, rhs_kv, hist, mix, lg)


def mlp_kernel(mlp_in, cot, up, down, bias, act_out, grad_out, sum_out):
    lin = dot(mlp_in[...], up[...]) + bias[...]
    grad_act = dot(cot[...], down[...])
    cdf = normal_cdf(lin)
    act_out[...] = (lin * cdf).astype(BF)
    grad = (grad_act * gelu_slope(lin, cdf)).astype(BF)
    grad_out[...] = grad

    @pl.when(pl.program_id(1) == 0)
    def _():
        sum_out[...] = jnp.zeros_like(sum_out)

    sum_out[...] += jnp.sum(grad.astype(F32), axis=0, keepdims=True)


def mlp(mlp_in, cot, up, down, bias):
    rows, feats = mlp_in.shape
    width = up.shape[1]
    tile, cols = min(256, rows), 512
    return pl.pallas_call(
        mlp_kernel,
        grid=(width // cols, rows // tile),
        in_specs=[
            pl.BlockSpec((tile, feats), lambda n, r: (r, 0)),
            pl.BlockSpec((tile, feats), lambda n, r: (r, 0)),
            pl.BlockSpec((feats, cols), lambda n, r: (0, n)),
            pl.BlockSpec((feats, cols), lambda n, r: (0, n)),
            pl.BlockSpec((1, cols), lambda n, r: (0, n)),
        ],
        out_specs=[
            pl.BlockSpec((tile, cols), lambda n, r: (r, n)),
            pl.BlockSpec((tile, cols), lambda n, r: (r, n)),
            pl.BlockSpec((1, cols), lambda n, r: (0, n)),
        ],
        out_shape=[
            jax.ShapeDtypeStruct((rows, width), BF),
            jax.ShapeDtypeStruct((rows, width), BF),
            jax.ShapeDtypeStruct((1, width), F32),
        ],
        compiler_params=params(48),
        cost_estimate=cost(25),
        name="mlp",
    )(mlp_in, cot, up, down, bias)


def turn_back_kernel(dkv, tables, dk_out, sum_out):
    tabs = (tables[0], tables[1], tables[2])
    for head in range(dk_out.shape[1] // HEAD_DIM):
        cols = slice(head * HEAD_DIM, (head + 1) * HEAD_DIM)
        dk_out[:, cols] = turn(dkv[0, :, cols].astype(F32), tabs, -1.0).astype(BF)


def last_kernel(
    hist, streams, attn, mix, pre, gain, w1, w2, grad_out, gain_out, w1_out, w2_out,
    normed, grad_mix, grad_normed, gain_sum,
):
    depth, rows, feats = hist.shape
    step_index = pl.program_id(0)

    @pl.when(step_index == 0)
    def _():
        gain_sum[...] = jnp.zeros_like(gain_sum)
        w1_out[...] = jnp.zeros_like(w1_out)
        w2_out[...] = jnp.zeros_like(w2_out)

    def reduce(part):
        layers = [hist[j, part, :].astype(F32) for j in range(depth)]
        latest = layers[depth - 1]
        scale = lax.rsqrt(mean_last(latest * latest) + RMS_EPSILON)
        normed[part, :] = (latest * scale * gain[...]).astype(BF)
        for m in range(STREAMS):
            grads = (attn[part, :] if m == STREAMS - 1 else streams[m, part, :]).astype(F32)
            for j in range(depth):
                at = m * depth + j
                grad_mix[part, at : at + 1] = jnp.sum(grads * layers[j], axis=-1, keepdims=True)

    rows_loop(rows, 16, reduce)
    pre_value = pre[...]
    cdf = normal_cdf(pre_value)
    grads = grad_mix[...]
    w2_out[...] += dot(pre_value * cdf, grads, TN, EXACT)
    grad_act = dot(grads, w2[...], NT, EXACT)
    grad_pre = (grad_act * gelu_slope(pre_value, cdf)).astype(BF)
    w1_out[...] += dot(grad_pre, normed[...], TN)
    grad_normed[...] = dot(grad_pre, w1[...], NT)

    def write(part):
        layers = [hist[depth - 1, part, :].astype(F32)]
        latest = layers[0]
        scale = lax.rsqrt(mean_last(latest * latest) + RMS_EPSILON)
        value = grad_normed[part, :]
        gain_sum[...] += fold(value * latest * scale)
        value = value * gain[...]
        back = scale * value - latest * (scale * scale * scale * mean_last(latest * value))
        weight = mix[part, :]
        grads = [streams[m, part, :].astype(F32) for m in range(STREAMS - 1)]
        grads.append(attn[part, :].astype(F32))
        for j in range(depth):
            total = weight[:, j : j + 1] * grads[0]
            for m in range(1, STREAMS):
                at = m * depth + j
                total = total + weight[:, at : at + 1] * grads[m]
            if j == depth - 1:
                total = total + (grads[0] + grads[1] + grads[2] + grads[3]) + back
            grad_out[j, part, :] = total

    rows_loop(rows, 16, write)

    @pl.when(step_index == pl.num_programs(0) - 1)
    def _():
        gain_out[...] = jnp.sum(gain_sum[...], axis=0, keepdims=True)


def last(hist, streams, attn, mix, pre, gain, w1, w2):
    depth, rows, feats = hist.shape
    hidden = w1.shape[1]
    tile = min(64, rows)
    full = lambda shape: pl.BlockSpec(shape, lambda i: (0,) * len(shape))
    return pl.pallas_call(
        last_kernel,
        grid=(rows // tile,),
        in_specs=[
            pl.BlockSpec((depth, tile, feats), lambda i: (0, i, 0)),
            pl.BlockSpec((3, tile, feats), lambda i: (0, i, 0)),
            pl.BlockSpec((tile, feats), lambda i: (i, 0)),
            pl.BlockSpec((tile, STREAMS * depth), lambda i: (i, 0)),
            pl.BlockSpec((tile, hidden), lambda i: (i, 0)),
            full((1, feats)),
            full(w1.shape),
            full(w2.shape),
        ],
        out_specs=[
            pl.BlockSpec((depth, tile, feats), lambda i: (0, i, 0)),
            full((1, feats)),
            full((hidden, feats)),
            full(w2.shape),
        ],
        out_shape=[
            jax.ShapeDtypeStruct((depth, rows, feats), F32),
            jax.ShapeDtypeStruct((1, feats), F32),
            jax.ShapeDtypeStruct((hidden, feats), F32),
            jax.ShapeDtypeStruct(w2.shape, F32),
        ],
        scratch_shapes=[
            pltpu.VMEM((tile, feats), BF),
            pltpu.VMEM((tile, STREAMS * depth), F32),
            pltpu.VMEM((tile, feats), F32),
            pltpu.VMEM((8, feats), F32),
        ],
        compiler_params=params(40),
        cost_estimate=cost(30),
        name="last",
    )(hist, streams, attn, mix, pre, gain.reshape(1, feats), w1, w2)


def turn_back(dkv, tables):
    _, rows, width = dkv.shape
    return pl.pallas_call(
        lambda d, t, o: turn_back_kernel(d, t, o, None),
        grid=(1,),
        in_specs=[
            pl.BlockSpec((1, rows, width), lambda i: (0, 0, 0)),
            pl.BlockSpec(tables.shape, lambda i: (0, 0, 0)),
        ],
        out_specs=pl.BlockSpec((rows, width), lambda i: (0, 0)),
        out_shape=jax.ShapeDtypeStruct((rows, width), BF),
        compiler_params=params(40),
        cost_estimate=cost(3),
        name="turn_back",
    )(dkv, tables)


def row_product(left, right):
    return dot(left, right, TN).astype(BF)


def shards(
    history,
    positions,
    lengths,
    cotangent,
    mix_gain,
    mix_w1,
    mix_w2,
    ln_gain,
    ln_bias,
    qkv_weight,
    qkv_bias,
    out_weight,
    out_bias,
    up_weight,
    up_bias,
    down_weight,
    down_bias,
):
    depth, slots, block_len, feats = history.shape
    rows = slots * block_len
    width = qkv_weight.shape[2]
    heads = width // HEAD_DIM
    owners = ("dp", "seq")
    layers = history.reshape(depth, rows, feats)

    w_mix = lax.all_gather(mix_w1, owners, axis=0, tiled=True)
    kv_shard = jnp.concatenate([qkv_weight[1], qkv_weight[2]], axis=1)
    w_kv = lax.all_gather(kv_shard, owners, axis=0, tiled=True)
    w_q = lax.all_gather(qkv_weight[0], owners, axis=0, tiled=True)
    w_out = lax.all_gather(out_weight, owners, axis=0, tiled=True)
    w_up = lax.all_gather(up_weight, owners, axis=0, tiled=True)
    w_down = lax.all_gather(down_weight, owners, axis=0, tiled=True)

    offset = lax.axis_index("seq") * block_len
    query_place = offset + jnp.arange(block_len, dtype=jnp.int32)
    valid = (query_place[None, :] < lengths[:, None]).reshape(rows, 1)
    cot = jnp.where(valid, cotangent.reshape(rows, feats), jnp.zeros((), BF))
    scalars = jnp.concatenate([lengths, offset[None].astype(jnp.int32)])
    tables = rotary_tables(positions.reshape(rows))

    normed, resid, mix, pre = front(layers, mix_gain, w_mix, mix_w2, ln_gain, ln_bias)
    kv = project(normed, w_kv, qkv_bias[1:], tables, 1)
    kv_all = lax.all_gather(kv.reshape(2, slots, block_len, width), "seq", axis=0)
    q = project(normed, w_q, qkv_bias[:1], tables, 0)[0]
    attn_vals = attend(scalars, q, kv_all, heads).reshape(rows, width)
    hidden, mlp_in = attn_out(
        attn_vals, w_out, resid, out_bias[None, :], ln_gain[3:4], ln_bias[3:4]
    )
    up_act, grad_up, grad_up_bias = mlp(mlp_in, cot, w_up, w_down, up_bias[None, :])

    mine = lax.psum_scatter(
        dot(up_act, w_down, NT).astype(BF), "tensor", scatter_dimension=0, tiled=True
    )
    out_rows = (hidden + (mine.astype(F32) + down_bias)).astype(BF)
    layer_out = lax.all_gather(out_rows, "tensor", axis=0, tiled=True)

    grad_attn, small_mlp = mlp_back(grad_up, w_up, hidden, cot, ln_gain[3:4])
    scatter = functools.partial(
        lax.psum_scatter, axis_name=owners, scatter_dimension=0, tiled=True
    )
    shard_down = scatter(row_product(cot, up_act)).astype(F32)
    shard_up = scatter(row_product(mlp_in, grad_up)).astype(F32)
    grad_vals = dot(grad_attn, w_out).astype(BF)
    dq, dkv = attend_back(scalars, q, kv_all, grad_vals, tables, heads)
    dkv_own = lax.psum_scatter(dkv, "seq", scatter_dimension=0).reshape(2, rows, width)
    shard_out = scatter(row_product(grad_attn, attn_vals)).astype(F32)
    grad_lin = jnp.stack([dq.reshape(rows, width), turn_back(dkv_own, tables), dkv_own[1]])
    grads, small_qkv = streams_back(grad_lin, w_q, w_kv, layers, mix, ln_gain)
    shard_qkv = jnp.stack(
        [scatter(row_product(normed[i], grad_lin[i])).astype(F32) for i in range(3)]
    )
    grad_layers, grad_gain, grad_w1, grad_w2 = last(
        layers, grads, grad_attn, mix, pre, mix_gain, w_mix, mix_w2
    )
    grad_history = grad_layers.reshape(depth, slots, block_len, feats)
    shard_w1 = lax.psum_scatter(grad_w1.T, owners, scatter_dimension=0, tiled=True)
    small_mlp, small_qkv = lax.psum((small_mlp, small_qkv), ("dp", "seq", "tensor"))
    grad_gain, grad_w2, grad_qkv_bias, grad_up_bias, grad_down_bias = lax.psum(
        (
            grad_gain[0],
            grad_w2,
            jnp.sum(grad_lin.astype(F32), axis=1),
            grad_up_bias[0],
            jnp.sum(cot.astype(F32), axis=0),
        ),
        owners,
    )
    return (
        layer_out.reshape(slots, block_len, feats),
        grad_history,
        grad_gain,
        shard_w1,
        grad_w2,
        jnp.concatenate([small_qkv[0], small_mlp[0:1]], axis=0),
        jnp.concatenate([small_qkv[1], small_mlp[1:2]], axis=0),
        shard_qkv,
        grad_qkv_bias,
        shard_out,
        small_mlp[2],
        shard_up,
        grad_up_bias,
        shard_down,
        grad_down_bias,
    )


def solution(mesh):
    in_specs = (
        P(None, "dp", "seq", None),
        P("dp", "seq"),
        P("dp"),
        P("dp", "seq", None),
        P(),
        P(("dp", "seq"), None),
        P(),
        P(),
        P(),
        P(None, ("dp", "seq"), "tensor"),
        P(None, "tensor"),
        P(("dp", "seq"), "tensor"),
        P(),
        P(("dp", "seq"), "tensor"),
        P("tensor"),
        P(("dp", "seq"), "tensor"),
        P(),
    )
    out_specs = (
        P("dp", "seq", None),
        P(None, "dp", "seq", None),
        P(),
        P(("dp", "seq"), None),
        P(),
        P(),
        P(),
        P(None, ("dp", "seq"), "tensor"),
        P(None, "tensor"),
        P(("dp", "seq"), "tensor"),
        P(),
        P(("dp", "seq"), "tensor"),
        P("tensor"),
        P(("dp", "seq"), "tensor"),
        P(),
    )
    return jax.shard_map(shards, mesh=mesh, in_specs=in_specs, out_specs=out_specs, check_vma=False)
```

```python
import functools
import math

import jax
import jax.numpy as jnp
from jax import lax
from jax.experimental import pallas as pl
from jax.experimental.pallas import tpu as pltpu
from jax.sharding import PartitionSpec as P

HEAD_DIM = 128
ROT = 32
STREAMS = 4
EXACT = lax.Precision.HIGHEST
RMS_EPSILON = 1e-06
NORM_EPSILON = 1e-05
BF = jnp.bfloat16
F32 = jnp.float32
MESH = pl.DeviceIdType.MESH
ANY = pl.BlockSpec(memory_space=pl.ANY)
VMEM = pl.BlockSpec(memory_space=pltpu.VMEM)
RING = 4
NN = (((1,), (0,)), ((), ()))
NT = (((1,), (1,)), ((), ()))
TN = (((0,), (0,)), ((), ()))


def dot(left, right, dims=NN, precision=None):
    return lax.dot_general(left, right, dims, precision=precision, preferred_element_type=F32)


def normal_cdf(values):
    return 0.5 * (1.0 + lax.erf(values * math.sqrt(0.5)))


def gelu_slope(values, cdf):
    return cdf + values * (jnp.exp(-0.5 * values * values) * (1.0 / math.sqrt(2.0 * math.pi)))


def mean_last(values):
    return jnp.mean(values, axis=-1, keepdims=True)


def rows_loop(total, step, body):
    def one(index, carry):
        body(pl.ds(pl.multiple_of(index * step, step), step))
        return carry

    lax.fori_loop(0, total // step, one, 0)


def params(limit_mib, collective_id=None):
    if collective_id is None:
        return pltpu.CompilerParams(vmem_limit_bytes=limit_mib << 20)
    return pltpu.CompilerParams(
        vmem_limit_bytes=limit_mib << 20, collective_id=collective_id, has_side_effects=True
    )


def cost(micros):
    return pl.CostEstimate(flops=0, bytes_accessed=int(micros * 3.0e6), transcendentals=0)


def front_kernel(hist, gain, w1, w2, lg, lb, normed_out, resid_out, mix_out, pre_out, scratch):
    depth, rows, _ = hist.shape

    def rms(part):
        wide = hist[depth - 1, part, :].astype(F32)
        scale = lax.rsqrt(mean_last(wide * wide) + RMS_EPSILON)
        scratch[part, :] = (wide * scale * gain[...]).astype(BF)

    rows_loop(rows, 16, rms)
    pre = dot(scratch[...], w1[...])
    pre_out[...] = pre
    mix_out[...] = dot(pre * normal_cdf(pre), w2[...], precision=EXACT)

    def combine(part):
        layers = [hist[j, part, :].astype(F32) for j in range(depth)]
        mix = mix_out[part, :]
        for m in range(STREAMS):
            running = layers[depth - 1]
            for j in range(depth):
                running = running + mix[:, m * depth + j : m * depth + j + 1] * layers[j]
            if m == STREAMS - 1:
                resid_out[part, :] = running
            else:
                centred = running - mean_last(running)
                inverse = lax.rsqrt(mean_last(centred * centred) + NORM_EPSILON)
                normed = centred * inverse * lg[m : m + 1, :] + lb[m : m + 1, :]
                normed_out[m, part, :] = normed.astype(BF)

    rows_loop(rows, 16, combine)


def front(layers, gain, w1, w2, lg, lb):
    depth, rows, feats = layers.shape
    tile = min(128, rows)
    hidden = w1.shape[1]
    full = lambda shape: pl.BlockSpec(shape, lambda i: (0,) * len(shape))
    return pl.pallas_call(
        front_kernel,
        grid=(rows // tile,),
        in_specs=[
            pl.BlockSpec((depth, tile, feats), lambda i: (0, i, 0)),
            full((1, feats)),
            full(w1.shape),
            full(w2.shape),
            full(lg.shape),
            full(lb.shape),
        ],
        out_specs=[
            pl.BlockSpec((3, tile, feats), lambda i: (0, i, 0)),
            pl.BlockSpec((tile, feats), lambda i: (i, 0)),
            pl.BlockSpec((tile, STREAMS * depth), lambda i: (i, 0)),
            pl.BlockSpec((tile, hidden), lambda i: (i, 0)),
        ],
        out_shape=[
            jax.ShapeDtypeStruct((3, rows, feats), BF),
            jax.ShapeDtypeStruct((rows, feats), F32),
            jax.ShapeDtypeStruct((rows, STREAMS * depth), F32),
            jax.ShapeDtypeStruct((rows, hidden), F32),
        ],
        scratch_shapes=[pltpu.VMEM((tile, feats), BF)],
        compiler_params=params(40),
        cost_estimate=cost(20),
        name="front",
    )(layers, gain.reshape(1, feats), w1, w2, lg, lb)


def turn(values, tables, sign):
    cosines, low, high = tables
    return values * cosines + sign * (
        pltpu.roll(values, HEAD_DIM - ROT // 2, 1) * low + pltpu.roll(values, ROT // 2, 1) * high
    )


def rotary_tables(positions):
    exponents = jnp.arange(0, ROT, 2).astype(F32) / ROT
    inverse = jnp.power(10000.0, -exponents)
    phases = positions.astype(F32)[:, None] * inverse[None, :]
    cosines, sines = jnp.cos(phases), jnp.sin(phases)
    rows, half = phases.shape
    ones = jnp.ones((rows, HEAD_DIM - 2 * half), F32)
    none = jnp.zeros((rows, HEAD_DIM - 2 * half), F32)
    zero = jnp.zeros((rows, half), F32)
    return jnp.stack(
        [
            jnp.concatenate([cosines, cosines, ones], axis=1),
            jnp.concatenate([-sines, zero, none], axis=1),
            jnp.concatenate([zero, sines, none], axis=1),
        ]
    )


def proj_kernel(first, lhs, weight, bias, tables, out):
    branch = pl.program_id(0) + first
    value = dot(lhs[0], weight[...]) + bias[0]

    @pl.when(branch < 2)
    def _():
        tabs = (tables[0], tables[1], tables[2])
        for head in range(value.shape[1] // HEAD_DIM):
            cols = slice(head * HEAD_DIM, (head + 1) * HEAD_DIM)
            out[0, :, cols] = turn(value[:, cols], tabs, 1.0).astype(BF)

    @pl.when(branch >= 2)
    def _():
        out[0] = value.astype(BF)


def project(normed, weight, bias, tables, first):
    _, rows, feats = normed.shape
    count, width = bias.shape
    tile = min(256, rows)
    return pl.pallas_call(
        functools.partial(proj_kernel, first),
        grid=(count, rows // tile),
        in_specs=[
            pl.BlockSpec((1, tile, feats), lambda b, r: (b + first, r, 0)),
            pl.BlockSpec((feats, width), lambda b, r: (0, b)),
            pl.BlockSpec((1, 1, width), lambda b, r: (b, 0, 0)),
            pl.BlockSpec((3, tile, HEAD_DIM), lambda b, r: (0, r, 0)),
        ],
        out_specs=pl.BlockSpec((1, tile, width), lambda b, r: (b, r, 0)),
        out_shape=jax.ShapeDtypeStruct((count, rows, width), BF),
        compiler_params=params(40),
        cost_estimate=cost(4 * count),
        name="project",
    )(normed, weight, bias.reshape(count, 1, width), tables)


def attend_kernel(scalars, q, k, v, out):
    keys = k[...].reshape(-1, HEAD_DIM)
    values = v[...].reshape(-1, HEAD_DIM)
    length = scalars[pl.program_id(0)]
    offset = scalars[pl.num_programs(0)]
    scores = dot(q[0], keys, NT) * (1.0 / math.sqrt(HEAD_DIM))
    key_place = lax.broadcasted_iota(jnp.int32, scores.shape, 1)
    query_place = lax.broadcasted_iota(jnp.int32, scores.shape, 0) + offset
    scores = jnp.where((key_place <= query_place) & (key_place < length), scores, -1e30)
    weights = jnp.exp(scores - jnp.max(scores, axis=-1, keepdims=True))
    total = jnp.sum(weights, axis=-1, keepdims=True)
    probs = (weights * (1.0 / total)).astype(BF)
    out[0] = dot(probs, values).astype(BF)


def attend(scalars, q, kv, heads):
    seqs, _, slots, length, width = kv.shape
    block = (1, length, HEAD_DIM)
    return pl.pallas_call(
        attend_kernel,
        grid_spec=pltpu.PrefetchScalarGridSpec(
            num_scalar_prefetch=1,
            grid=(slots, heads),
            in_specs=[
                pl.BlockSpec(block, lambda s, h, _: (s, 0, h)),
                pl.BlockSpec((seqs, 1, 1, length, HEAD_DIM), lambda s, h, _: (0, 0, s, 0, h)),
                pl.BlockSpec((seqs, 1, 1, length, HEAD_DIM), lambda s, h, _: (0, 1, s, 0, h)),
            ],
            out_specs=pl.BlockSpec(block, lambda s, h, _: (s, 0, h)),
        ),
        out_shape=jax.ShapeDtypeStruct((slots, length, width), BF),
        compiler_params=params(40),
        cost_estimate=cost(15),
        name="attend",
    )(scalars, q.reshape(slots, length, width), kv, kv)


def attend_back_kernel(scalars, q, k, v, g, tables, dq_out, dkv_out):
    seqs = k.shape[0]
    scaling = 1.0 / math.sqrt(HEAD_DIM)
    keys = k[...].reshape(-1, HEAD_DIM)
    values = v[...].reshape(-1, HEAD_DIM)
    length = scalars[pl.program_id(0)]
    offset = scalars[pl.num_programs(0)]
    queries, grads = q[0], g[0]
    scores = dot(keys, queries, NT) * scaling
    key_place = lax.broadcasted_iota(jnp.int32, scores.shape, 0)
    query_place = lax.broadcasted_iota(jnp.int32, scores.shape, 1) + offset
    scores = jnp.where((key_place <= query_place) & (key_place < length), scores, -1e30)
    weights = jnp.exp(scores - jnp.max(scores, axis=0, keepdims=True))
    probs = weights * (1.0 / jnp.sum(weights, axis=0, keepdims=True))
    grad_probs = dot(values, grads, NT)
    mixed = jnp.sum(probs * grad_probs, axis=0, keepdims=True)
    grad_scores = (probs * (grad_probs - mixed)).astype(BF)
    grad_values = dot(probs.astype(BF), grads)
    grad_keys = dot(grad_scores, queries) * scaling
    shape = (seqs, -1, HEAD_DIM)
    dkv_out[:, 0, 0] = grad_keys.astype(BF).reshape(shape)
    dkv_out[:, 1, 0] = grad_values.astype(BF).reshape(shape)
    grad_queries = dot(grad_scores, keys, TN) * scaling
    tabs = (tables[0], tables[1], tables[2])
    dq_out[0] = turn(grad_queries, tabs, -1.0).astype(BF)


def attend_back(scalars, q, kv, g, tables, heads):
    seqs, _, slots, length, width = kv.shape
    block = (1, length, HEAD_DIM)
    own = pl.BlockSpec(block, lambda s, h, _: (s, 0, h))
    return pl.pallas_call(
        attend_back_kernel,
        grid_spec=pltpu.PrefetchScalarGridSpec(
            num_scalar_prefetch=1,
            grid=(slots, heads),
            in_specs=[
                own,
                pl.BlockSpec((seqs, 1, 1, length, HEAD_DIM), lambda s, h, _: (0, 0, s, 0, h)),
                pl.BlockSpec((seqs, 1, 1, length, HEAD_DIM), lambda s, h, _: (0, 1, s, 0, h)),
                own,
                pl.BlockSpec((3, length, HEAD_DIM), lambda s, h, _: (0, s, 0)),
            ],
            out_specs=[
                own,
                pl.BlockSpec((seqs, 2, 1, length, HEAD_DIM), lambda s, h, _: (0, 0, s, 0, h)),
            ],
        ),
        out_shape=[
            jax.ShapeDtypeStruct((slots, length, width), BF),
            jax.ShapeDtypeStruct((seqs, 2, slots, length, width), BF),
        ],
        compiler_params=params(48),
        cost_estimate=cost(25),
        name="attend_back",
    )(scalars, q.reshape(slots, length, width), kv, kv, g.reshape(slots, length, width), tables)


class Ring:
    def __init__(self, chunk):
        me = lax.axis_index("tensor")
        self.chunk, self.half = chunk, chunk // 2
        self.me = me
        self.right = lax.rem(me + 1, RING)
        self.left = lax.rem(me + RING - 1, RING)
        self.far = lax.rem(me + 2, RING)

    def at(self, index, shift=0):
        return pl.multiple_of(index * self.chunk + shift, self.half)

    def barrier(self):
        gate = pltpu.get_barrier_semaphore()
        for near in (self.left, self.right):
            pl.semaphore_signal(gate, inc=1, device_id={"tensor": near}, device_id_type=MESH)
        pl.semaphore_wait(gate, 2)


def remote(source, target, sems, index, device):
    return pltpu.make_async_remote_copy(
        src_ref=source,
        dst_ref=target,
        send_sem=sems.at[0, index],
        recv_sem=sems.at[1, index],
        device_id={"tensor": device},
        device_id_type=MESH,
    )


def product(lhs, rhs, start, count, write, step=512):
    total = rhs.shape[0]

    def one(cols):
        write(cols, dot(lhs[pl.ds(start, count), :], rhs[cols, :], NT))

    rows_loop(total, min(step, total), one)


class Scatter:
    def __init__(self, ring, lhs, rhs, far, near, far_in, near_in, sems):
        self.ring, self.lhs, self.rhs = ring, lhs, rhs
        self.far, self.near, self.far_in, self.near_in = far, near, far_in, near_in
        half = ring.half
        up, down = pl.ds(0, half), pl.ds(half, half)
        self.copies = [
            remote(far.at[0], far_in.at[0], sems, 0, ring.right),
            remote(far.at[1], far_in.at[1], sems, 1, ring.left),
            remote(near.at[0, down], near_in.at[0, down], sems, 2, ring.right),
            remote(near.at[1, up], near_in.at[1, up], sems, 3, ring.left),
            remote(near.at[0, up], near_in.at[0, up], sems, 4, ring.right),
            remote(near.at[1, down], near_in.at[1, down], sems, 5, ring.left),
        ]

    def begin(self):
        ring, half = self.ring, self.ring.half

        def far_half(which):
            def write(cols, value):
                self.far[which, :, cols] = value.astype(BF)

            product(self.lhs, self.rhs, ring.at(ring.far, which * half), half, write)
            self.copies[which].start()

        def near_half(which, device, part, copy):
            def write(cols, value):
                self.near[which, pl.ds(part * half, half), cols] = value.astype(BF)

            product(self.lhs, self.rhs, ring.at(device, part * half), half, write)
            self.copies[copy].start()

        far_half(0)
        far_half(1)
        near_half(0, ring.right, 1, 2)
        near_half(1, ring.left, 0, 3)

    def relay(self):
        ring, half = self.ring, self.ring.half

        def add_half(which, device, part, copy):
            self.copies[which].wait_recv()

            def write(cols, value):
                arrived = self.far_in[which, :, cols].astype(F32)
                self.near[which, pl.ds(part * half, half), cols] = (value + arrived).astype(BF)

            product(self.lhs, self.rhs, ring.at(device, part * half), half, write)
            self.copies[copy].start()

        add_half(0, ring.right, 0, 4)
        add_half(1, ring.left, 1, 5)

    def arrive(self):
        for copy in self.copies[2:]:
            copy.wait_recv()

    def finish(self):
        for copy in self.copies:
            copy.wait_send()


class Gather:
    def __init__(self, ring, own, out, sems, base, local_sem):
        half = ring.half

        def rows(index, shift=0, count=ring.chunk):
            return out.at[pl.ds(ring.at(index, shift), count), :]

        mine = rows(ring.me)
        self.local = pltpu.make_async_copy(own, mine, local_sem)
        self.first = [
            remote(own, mine, sems, base, ring.right),
            remote(own, mine, sems, base + 1, ring.left),
        ]
        up, down = rows(ring.left, 0, half), rows(ring.right, half, half)
        self.second = [
            remote(up, up, sems, base + 2, ring.right),
            remote(down, down, sems, base + 3, ring.left),
        ]

    def begin(self):
        for copy in self.first:
            copy.start()
        self.local.start()

    def relay(self):
        for arrived, onward in zip(self.first, self.second):
            arrived.wait_recv()
            onward.start()

    def finish(self):
        for copy in self.second:
            copy.wait_recv()
        for copy in self.first + self.second:
            copy.wait_send()
        self.local.wait()


def scatter_scratch(chunk, feats, count=1):
    half = chunk // 2
    lead = () if count == 1 else (count,)
    return [
        pltpu.VMEM(lead + (2, half, feats), BF),
        pltpu.VMEM(lead + (2, chunk, feats), BF),
        pltpu.VMEM(lead + (2, half, feats), BF),
        pltpu.VMEM(lead + (2, chunk, feats), BF),
    ]


def own_sum(scatter, total):
    ring = scatter.ring

    def write(cols, value):
        total[:, cols] = value

    product(scatter.lhs, scatter.rhs, ring.at(ring.me), ring.chunk, write)


def whole_sum(scatter, total, part):
    near = scatter.near_in
    return total[part, :] + near[0, part, :].astype(F32) + near[1, part, :].astype(F32)


def attn_out_kernel(
    lhs, rhs, resid, bias, lg, lb, hidden_out, mlp_out,
    far, near, far_in, near_in, total, base_rows, own, sems, local_sems,
):
    chunk, feats = total.shape
    ring = Ring(chunk)
    fetch = pltpu.make_async_copy(
        resid.at[pl.ds(ring.at(ring.me), chunk), :], base_rows, local_sems.at[0]
    )
    fetch.start()
    ring.barrier()
    scatter = Scatter(ring, lhs, rhs, far, near, far_in, near_in, sems)
    scatter.begin()
    scatter.relay()
    own_sum(scatter, total)
    fetch.wait()
    scatter.arrive()

    def norm(part):
        value = base_rows[part, :] + (whole_sum(scatter, total, part) + bias[...])
        hidden_out[part, :] = value
        centred = value - mean_last(value)
        inverse = lax.rsqrt(mean_last(centred * centred) + NORM_EPSILON)
        own[part, :] = (centred * inverse * lg[...] + lb[...]).astype(BF)

    rows_loop(chunk, 16, norm)
    gather = Gather(ring, own, mlp_out, sems, 6, local_sems.at[1])
    gather.begin()
    gather.relay()
    scatter.finish()
    gather.finish()


def attn_out(lhs, rhs, resid, bias, lg, lb):
    rows, feats = resid.shape
    chunk = rows // RING
    return pl.pallas_call(
        attn_out_kernel,
        in_specs=[VMEM, VMEM, ANY, VMEM, VMEM, VMEM],
        out_specs=[VMEM, ANY],
        out_shape=[
            jax.ShapeDtypeStruct((chunk, feats), F32),
            jax.ShapeDtypeStruct((rows, feats), BF),
        ],
        scratch_shapes=scatter_scratch(chunk, feats)
        + [
            pltpu.VMEM((chunk, feats), F32),
            pltpu.VMEM((chunk, feats), F32),
            pltpu.VMEM((chunk, feats), BF),
            pltpu.SemaphoreType.DMA((2, 10)),
            pltpu.SemaphoreType.DMA((2,)),
        ],
        compiler_params=params(48, 0),
        cost_estimate=cost(80),
        name="attn_out",
    )(lhs, rhs, resid, bias, lg, lb)


def mlp_out_kernel(
    lhs, rhs, hidden, bias, out,
    far, near, far_in, near_in, total, own, sems, local_sems,
):
    chunk, feats = total.shape
    ring = Ring(chunk)
    ring.barrier()
    scatter = Scatter(ring, lhs, rhs, far, near, far_in, near_in, sems)
    scatter.begin()
    scatter.relay()
    own_sum(scatter, total)
    scatter.arrive()

    def add(part):
        own[part, :] = (hidden[part, :] + (whole_sum(scatter, total, part) + bias[...])).astype(BF)

    rows_loop(chunk, 16, add)
    gather = Gather(ring, own, out, sems, 6, local_sems.at[0])
    gather.begin()
    gather.relay()
    scatter.finish()
    gather.finish()


def mlp_out(lhs, rhs, hidden, bias):
    rows = lhs.shape[0]
    chunk, feats = hidden.shape
    return pl.pallas_call(
        mlp_out_kernel,
        in_specs=[VMEM, VMEM, VMEM, VMEM],
        out_specs=ANY,
        out_shape=jax.ShapeDtypeStruct((rows, feats), BF),
        scratch_shapes=scatter_scratch(chunk, feats)
        + [
            pltpu.VMEM((chunk, feats), F32),
            pltpu.VMEM((chunk, feats), BF),
            pltpu.SemaphoreType.DMA((2, 10)),
            pltpu.SemaphoreType.DMA((1,)),
        ],
        compiler_params=params(52, 3),
        cost_estimate=cost(140),
        name="mlp_out",
    )(lhs, rhs, hidden, bias)


def weights_kernel(normed, grad_attn, grad_lin, attn_vals, out):
    branch = pl.program_id(0)

    @pl.when(branch < 3)
    def _():
        out[...] = dot(normed[0], grad_lin[0], TN).astype(BF)

    @pl.when(branch == 3)
    def _():
        out[...] = dot(grad_attn[...], attn_vals[...], TN).astype(BF)


def weight_grads(normed, grad_attn, grad_lin, attn_vals):
    _, rows, feats = normed.shape
    width = attn_vals.shape[1]
    cols = 512
    last_block = feats // cols - 1
    return pl.pallas_call(
        weights_kernel,
        grid=(4, feats // cols),
        in_specs=[
            pl.BlockSpec(
                (1, rows, cols),
                lambda b, n: (jnp.minimum(b, 2), 0, jnp.where(b < 3, n, last_block)),
            ),
            pl.BlockSpec((rows, cols), lambda b, n: (0, jnp.where(b < 3, 0, n))),
            pl.BlockSpec((1, rows, width), lambda b, n: (jnp.minimum(b, 2), 0, 0)),
            pl.BlockSpec((rows, width), lambda b, n: (0, 0)),
        ],
        out_specs=pl.BlockSpec((cols, width), lambda b, n: (n, b)),
        out_shape=jax.ShapeDtypeStruct((feats, 4 * width), BF),
        compiler_params=params(40),
        cost_estimate=cost(15),
        name="weight_grads",
    )(normed, grad_attn, grad_lin, attn_vals)


def norm_back(values, grads, gain):
    centred = values - mean_last(values)
    inverse = lax.rsqrt(mean_last(centred * centred) + NORM_EPSILON)
    normed = centred * inverse
    inner = grads * gain
    back = inverse * (inner - mean_last(inner) - normed * mean_last(inner * normed))
    return back, normed


def fold(values):
    rows, feats = values.shape
    return jnp.sum(values.reshape(rows // 8, 8, feats), axis=0)


def mlp_back_kernel(
    lhs, rhs, hidden, cot, lg, grad_out, small_out,
    far, near, far_in, near_in, total, cot_rows, own, sums, sems, local_sems,
):
    chunk, feats = total.shape
    ring = Ring(chunk)
    fetch = pltpu.make_async_copy(
        cot.at[pl.ds(ring.at(ring.me), chunk), :], cot_rows, local_sems.at[0]
    )
    fetch.start()
    ring.barrier()
    scatter = Scatter(ring, lhs, rhs, far, near, far_in, near_in, sems)
    scatter.begin()
    scatter.relay()
    own_sum(scatter, total)
    fetch.wait()
    sums[...] = jnp.zeros_like(sums)
    scatter.arrive()

    def back(part):
        grads = whole_sum(scatter, total, part)
        step, normed = norm_back(hidden[part, :], grads, lg[...])
        low = (cot_rows[part, :].astype(F32) + step).astype(BF)
        own[part, :] = low
        sums[0] += fold(grads * normed)
        sums[1] += fold(grads)
        sums[2] += fold(low.astype(F32))

    rows_loop(chunk, 16, back)
    gather = Gather(ring, own, grad_out, sems, 6, local_sems.at[1])
    gather.begin()
    for i in range(3):
        small_out[i : i + 1, :] = jnp.sum(sums[i], axis=0, keepdims=True)
    gather.relay()
    scatter.finish()
    gather.finish()


def mlp_back(lhs, rhs, hidden, cot, lg):
    rows, feats = cot.shape
    chunk = rows // RING
    return pl.pallas_call(
        mlp_back_kernel,
        in_specs=[VMEM, VMEM, VMEM, ANY, VMEM],
        out_specs=[ANY, VMEM],
        out_shape=[
            jax.ShapeDtypeStruct((rows, feats), BF),
            jax.ShapeDtypeStruct((3, feats), F32),
        ],
        scratch_shapes=scatter_scratch(chunk, feats)
        + [
            pltpu.VMEM((chunk, feats), F32),
            pltpu.VMEM((chunk, feats), BF),
            pltpu.VMEM((chunk, feats), BF),
            pltpu.VMEM((3, 8, feats), F32),
            pltpu.SemaphoreType.DMA((2, 10)),
            pltpu.SemaphoreType.DMA((2,)),
        ],
        compiler_params=params(52, 1),
        cost_estimate=cost(80),
        name="mlp_back",
    )(lhs, rhs, hidden, cot, lg)


class Spread:
    def __init__(self, ring, slots, sems, base):
        half = slots.shape[1] // 2
        mine = slots.at[ring.me]
        self.first = [
            remote(mine, mine, sems, base, ring.right),
            remote(mine, mine, sems, base + 1, ring.left),
        ]
        up = slots.at[ring.left, pl.ds(0, half), :]
        down = slots.at[ring.right, pl.ds(half, half), :]
        self.second = [
            remote(up, up, sems, base + 2, ring.right),
            remote(down, down, sems, base + 3, ring.left),
        ]

    def begin(self):
        for copy in self.first:
            copy.start()

    def relay(self):
        for arrived, onward in zip(self.first, self.second):
            arrived.wait_recv()
            onward.start()

    def arrive(self):
        for copy in self.second:
            copy.wait_recv()

    def finish(self):
        for copy in self.first + self.second:
            copy.wait_send()


def streams_back_kernel(
    lin, weight, hist, mix, lg, grads_out, small_out,
    slots, weights, total, layers, stage, sums, sems, weight_sems, layer_sem, stage_sems, own_sems,
):
    tile, feats = total.shape
    depth = layers.shape[0]
    rows, width = lin.shape[1], lin.shape[2]
    tiles = rows // tile
    ring = Ring(rows)

    def fetch(stream):
        return [
            pltpu.make_async_copy(
                weight.at[pl.ds(z * feats, feats), pl.ds(stream * width, width)],
                weights.at[stream % 2, z],
                weight_sems.at[stream % 2, z],
            )
            for z in range(RING)
        ]

    local = [
        pltpu.make_async_copy(lin.at[i], slots.at[i, ring.me], own_sems.at[i]) for i in range(3)
    ]
    for copy in local:
        copy.start()
    for stream in range(2):
        for copy in fetch(stream):
            copy.start()
    sums[...] = jnp.zeros_like(sums)
    ring.barrier()
    spreads = [Spread(ring, slots.at[i], sems.at[i], 0) for i in range(3)]

    def write_out(stream, index, slot):
        part = pl.ds(pl.multiple_of(index * tile, tile), tile)
        return pltpu.make_async_copy(
            stage.at[slot], grads_out.at[stream, part, :], stage_sems.at[slot]
        )

    def compute(stream):
        for copy in fetch(stream):
            copy.wait()

        def one(index, carry):
            part = pl.ds(pl.multiple_of(index * tile, tile), tile)
            load = pltpu.make_async_copy(hist.at[:, part, :], layers, layer_sem)
            load.start()
            slot = lax.rem(index, 2)

            def columns(cols):
                value = dot(slots[stream, 0, part, :], weights[stream % 2, 0, cols, :], NT)
                for z in range(1, RING):
                    value += dot(slots[stream, z, part, :], weights[stream % 2, z, cols, :], NT)
                total[:, cols] = value

            rows_loop(feats, 512, columns)
            load.wait()

            @pl.when(index >= 2)
            def _():
                write_out(stream, index - 2, slot).wait()

            def back(sub):
                grads = total[sub, :]
                latest = layers[depth - 1, sub, :].astype(F32)
                at = pl.multiple_of(index * tile + sub.start, 16)
                share = mix[pl.ds(at, 16), :]
                mixture = latest
                for j in range(depth):
                    col = stream * depth + j
                    mixture = mixture + share[:, col : col + 1] * layers[j, sub, :].astype(F32)
                step, normed = norm_back(mixture, grads, lg[stream : stream + 1, :])
                stage[slot, sub, :] = step.astype(BF)
                sums[stream, 0] += fold(grads * normed)
                sums[stream, 1] += fold(grads)

            rows_loop(tile, 16, back)
            write_out(stream, index, slot).start()
            return carry

        lax.fori_loop(0, tiles, one, 0)
        for index in range(max(tiles - 2, 0), tiles):
            write_out(stream, index, index % 2).wait()
        if stream == 0:
            for copy in fetch(2):
                copy.start()

    for copy in local:
        copy.wait()
    spreads[0].begin()
    spreads[1].begin()
    spreads[0].relay()
    spreads[2].begin()
    spreads[1].relay()
    spreads[0].arrive()
    compute(0)
    spreads[2].relay()
    spreads[1].arrive()
    compute(1)
    spreads[2].arrive()
    compute(2)
    for i in range(3):
        for j in range(2):
            small_out[j, i : i + 1, :] = jnp.sum(sums[i, j], axis=0, keepdims=True)
    for spread in spreads:
        spread.finish()


def streams_back(lin, weight, hist, mix, lg):
    depth, rows, feats = hist.shape
    width = lin.shape[2]
    tile = min(256, rows)
    return pl.pallas_call(
        streams_back_kernel,
        in_specs=[VMEM, ANY, ANY, VMEM, VMEM],
        out_specs=[ANY, VMEM],
        out_shape=[
            jax.ShapeDtypeStruct((3, rows, feats), BF),
            jax.ShapeDtypeStruct((2, 3, feats), F32),
        ],
        scratch_shapes=[
            pltpu.VMEM((3, RING, rows, width), BF),
            pltpu.VMEM((2, RING, feats, width), BF),
            pltpu.VMEM((tile, feats), F32),
            pltpu.VMEM((depth, tile, feats), BF),
            pltpu.VMEM((2, tile, feats), BF),
            pltpu.VMEM((3, 2, 8, feats), F32),
            pltpu.SemaphoreType.DMA((3, 2, 4)),
            pltpu.SemaphoreType.DMA((2, RING)),
            pltpu.SemaphoreType.DMA,
            pltpu.SemaphoreType.DMA((2,)),
            pltpu.SemaphoreType.DMA((3,)),
        ],
        compiler_params=params(58, 2),
        cost_estimate=cost(240),
        name="streams_back",
    )(lin, weight, hist, mix, lg)


def small_kernel(seqs, owners, ours, share, out, share_out, near, all_ours, all_shares, near_sems, sems):
    ring = Ring(2)
    near_rows = near.shape[1]
    rank = lax.axis_index("dp") * seqs + lax.axis_index("seq")
    peers = [lax.rem(rank + k, owners) for k in range(1, owners)]
    places = [{"dp": lax.div(p, seqs), "seq": lax.rem(p, seqs)} for p in peers]
    mates = [ring.right, ring.far, ring.left]
    gate = pltpu.get_barrier_semaphore()
    for place in places + [{"tensor": z} for z in mates]:
        pl.semaphore_signal(gate, inc=1, device_id=place, device_id_type=MESH)
    pl.semaphore_wait(gate, len(places) + len(mates))

    def send(source, target, pair, index, place):
        return pltpu.make_async_remote_copy(
            src_ref=source,
            dst_ref=target,
            send_sem=pair.at[0, index],
            recv_sem=pair.at[1, index],
            device_id=place,
            device_id_type=MESH,
        )

    near[ring.me] = ours[0:near_rows, :]
    shares = [
        send(share.at[p], all_shares.at[rank], sems.at[0], k, place)
        for k, (p, place) in enumerate(zip(peers, places))
    ]
    first = [
        send(near.at[ring.me], near.at[ring.me], near_sems, k, {"tensor": z})
        for k, z in enumerate(mates)
    ]
    for copy in first + shares:
        copy.start()
    for copy in first:
        copy.wait()
    all_ours[rank, 0:near_rows, :] = (near[0] + near[1]) + (near[2] + near[3])
    all_ours[rank, near_rows:, :] = ours[near_rows:, :]
    all_shares[rank] = share[rank]
    second = [
        send(all_ours.at[rank], all_ours.at[rank], sems.at[1], k, place)
        for k, place in enumerate(places)
    ]
    for copy in second:
        copy.start()
    for copy in shares + second:
        copy.wait()
    total, part = all_ours[0], all_shares[0]
    for index in range(1, owners):
        total += all_ours[index]
        part += all_shares[index]
    out[...] = total
    share_out[...] = part


def small_sums(ours, share, seqs):
    owners = share.shape[0]
    rows, feats = ours.shape
    return pl.pallas_call(
        functools.partial(small_kernel, seqs, owners),
        in_specs=[VMEM, VMEM],
        out_specs=[VMEM, VMEM],
        out_shape=[
            jax.ShapeDtypeStruct(ours.shape, F32),
            jax.ShapeDtypeStruct(share.shape[1:], F32),
        ],
        scratch_shapes=[
            pltpu.VMEM((RING, 8, feats), F32),
            pltpu.VMEM((owners,) + ours.shape, F32),
            pltpu.VMEM(share.shape, F32),
            pltpu.SemaphoreType.DMA((2, 3)),
            pltpu.SemaphoreType.DMA((2, 2, owners - 1)),
        ],
        compiler_params=params(40, 4),
        cost_estimate=cost(12),
        name="small_sums",
    )(ours, share)


def mlp_kernel(mlp_in, cot, up, down, bias, act_out, grad_out, sum_out):
    lin = dot(mlp_in[...], up[...]) + bias[...]
    grad_act = dot(cot[...], down[...])
    cdf = normal_cdf(lin)
    act_out[...] = (lin * cdf).astype(BF)
    grad = (grad_act * gelu_slope(lin, cdf)).astype(BF)
    grad_out[...] = grad

    @pl.when(pl.program_id(1) == 0)
    def _():
        sum_out[...] = jnp.zeros_like(sum_out)

    sum_out[...] += jnp.sum(grad.astype(F32), axis=0, keepdims=True)


def mlp(mlp_in, cot, up, down, bias):
    rows, feats = mlp_in.shape
    width = up.shape[1]
    tile, cols = min(256, rows), 512
    return pl.pallas_call(
        mlp_kernel,
        grid=(width // cols, rows // tile),
        in_specs=[
            pl.BlockSpec((tile, feats), lambda n, r: (r, 0)),
            pl.BlockSpec((tile, feats), lambda n, r: (r, 0)),
            pl.BlockSpec((feats, cols), lambda n, r: (0, n)),
            pl.BlockSpec((feats, cols), lambda n, r: (0, n)),
            pl.BlockSpec((1, cols), lambda n, r: (0, n)),
        ],
        out_specs=[
            pl.BlockSpec((tile, cols), lambda n, r: (r, n)),
            pl.BlockSpec((tile, cols), lambda n, r: (r, n)),
            pl.BlockSpec((1, cols), lambda n, r: (0, n)),
        ],
        out_shape=[
            jax.ShapeDtypeStruct((rows, width), BF),
            jax.ShapeDtypeStruct((rows, width), BF),
            jax.ShapeDtypeStruct((1, width), F32),
        ],
        compiler_params=params(48),
        cost_estimate=cost(25),
        name="mlp",
    )(mlp_in, cot, up, down, bias)


def turn_back_kernel(dkv, tables, dk_out, sum_out):
    tabs = (tables[0], tables[1], tables[2])
    for head in range(dk_out.shape[1] // HEAD_DIM):
        cols = slice(head * HEAD_DIM, (head + 1) * HEAD_DIM)
        dk_out[:, cols] = turn(dkv[0, :, cols].astype(F32), tabs, -1.0).astype(BF)


def last_kernel(
    hist, streams, attn, mix, pre, gain, w1, w2, grad_out, gain_out, w1_out, w2_out,
    normed, grad_mix, grad_normed, gain_sum,
):
    depth, rows, feats = hist.shape
    step_index = pl.program_id(0)

    @pl.when(step_index == 0)
    def _():
        gain_sum[...] = jnp.zeros_like(gain_sum)
        w1_out[...] = jnp.zeros_like(w1_out)
        w2_out[...] = jnp.zeros_like(w2_out)

    def reduce(part):
        layers = [hist[j, part, :].astype(F32) for j in range(depth)]
        latest = layers[depth - 1]
        scale = lax.rsqrt(mean_last(latest * latest) + RMS_EPSILON)
        normed[part, :] = (latest * scale * gain[...]).astype(BF)
        for m in range(STREAMS):
            grads = (attn[part, :] if m == STREAMS - 1 else streams[m, part, :]).astype(F32)
            for j in range(depth):
                at = m * depth + j
                grad_mix[part, at : at + 1] = jnp.sum(grads * layers[j], axis=-1, keepdims=True)

    rows_loop(rows, 16, reduce)
    pre_value = pre[...]
    cdf = normal_cdf(pre_value)
    grads = grad_mix[...]
    w2_out[...] += dot(pre_value * cdf, grads, TN, EXACT)
    grad_act = dot(grads, w2[...], NT, EXACT)
    grad_pre = (grad_act * gelu_slope(pre_value, cdf)).astype(BF)
    w1_out[...] += dot(grad_pre, normed[...], TN)
    grad_normed[...] = dot(grad_pre, w1[...], NT)

    def write(part):
        layers = [hist[depth - 1, part, :].astype(F32)]
        latest = layers[0]
        scale = lax.rsqrt(mean_last(latest * latest) + RMS_EPSILON)
        value = grad_normed[part, :]
        gain_sum[...] += fold(value * latest * scale)
        value = value * gain[...]
        back = scale * value - latest * (scale * scale * scale * mean_last(latest * value))
        weight = mix[part, :]
        grads = [streams[m, part, :].astype(F32) for m in range(STREAMS - 1)]
        grads.append(attn[part, :].astype(F32))
        for j in range(depth):
            total = weight[:, j : j + 1] * grads[0]
            for m in range(1, STREAMS):
                at = m * depth + j
                total = total + weight[:, at : at + 1] * grads[m]
            if j == depth - 1:
                total = total + (grads[0] + grads[1] + grads[2] + grads[3]) + back
            grad_out[j, part, :] = total

    rows_loop(rows, 16, write)

    @pl.when(step_index == pl.num_programs(0) - 1)
    def _():
        gain_out[...] = jnp.sum(gain_sum[...], axis=0, keepdims=True)


def last(hist, streams, attn, mix, pre, gain, w1, w2):
    depth, rows, feats = hist.shape
    hidden = w1.shape[1]
    tile = min(64, rows)
    full = lambda shape: pl.BlockSpec(shape, lambda i: (0,) * len(shape))
    return pl.pallas_call(
        last_kernel,
        grid=(rows // tile,),
        in_specs=[
            pl.BlockSpec((depth, tile, feats), lambda i: (0, i, 0)),
            pl.BlockSpec((3, tile, feats), lambda i: (0, i, 0)),
            pl.BlockSpec((tile, feats), lambda i: (i, 0)),
            pl.BlockSpec((tile, STREAMS * depth), lambda i: (i, 0)),
            pl.BlockSpec((tile, hidden), lambda i: (i, 0)),
            full((1, feats)),
            full(w1.shape),
            full(w2.shape),
        ],
        out_specs=[
            pl.BlockSpec((depth, tile, feats), lambda i: (0, i, 0)),
            full((1, feats)),
            full((hidden, feats)),
            full(w2.shape),
        ],
        out_shape=[
            jax.ShapeDtypeStruct((depth, rows, feats), F32),
            jax.ShapeDtypeStruct((1, feats), F32),
            jax.ShapeDtypeStruct((hidden, feats), F32),
            jax.ShapeDtypeStruct(w2.shape, F32),
        ],
        scratch_shapes=[
            pltpu.VMEM((tile, feats), BF),
            pltpu.VMEM((tile, STREAMS * depth), F32),
            pltpu.VMEM((tile, feats), F32),
            pltpu.VMEM((8, feats), F32),
        ],
        compiler_params=params(40),
        cost_estimate=cost(30),
        name="last",
    )(hist, streams, attn, mix, pre, gain.reshape(1, feats), w1, w2)


def turn_back(dkv, tables):
    _, rows, width = dkv.shape
    return pl.pallas_call(
        lambda d, t, o: turn_back_kernel(d, t, o, None),
        grid=(1,),
        in_specs=[
            pl.BlockSpec((1, rows, width), lambda i: (0, 0, 0)),
            pl.BlockSpec(tables.shape, lambda i: (0, 0, 0)),
        ],
        out_specs=pl.BlockSpec((rows, width), lambda i: (0, 0)),
        out_shape=jax.ShapeDtypeStruct((rows, width), BF),
        compiler_params=params(40),
        cost_estimate=cost(3),
        name="turn_back",
    )(dkv, tables)


def row_product(left, right):
    return dot(left, right, TN).astype(BF)


def shards(
    history,
    positions,
    lengths,
    cotangent,
    mix_gain,
    mix_w1,
    mix_w2,
    ln_gain,
    ln_bias,
    qkv_weight,
    qkv_bias,
    out_weight,
    out_bias,
    up_weight,
    up_bias,
    down_weight,
    down_bias,
):
    depth, slots, block_len, feats = history.shape
    rows = slots * block_len
    width = qkv_weight.shape[2]
    heads = width // HEAD_DIM
    owners = ("dp", "seq")
    layers = history.reshape(depth, rows, feats)

    w_mix = lax.all_gather(mix_w1, owners, axis=0, tiled=True)
    kv_shard = jnp.concatenate([qkv_weight[1], qkv_weight[2]], axis=1)
    w_kv = lax.all_gather(kv_shard, owners, axis=0, tiled=True)
    w_q = lax.all_gather(qkv_weight[0], owners, axis=0, tiled=True)
    w_out = lax.all_gather(out_weight, owners, axis=0, tiled=True)
    w_up = lax.all_gather(up_weight, owners, axis=0, tiled=True)
    w_down = lax.all_gather(down_weight, owners, axis=0, tiled=True)
    tie = lax.optimization_barrier
    qkv_shard, w_down = tie(
        (jnp.concatenate([qkv_weight[0], qkv_weight[1], qkv_weight[2]], axis=1), w_down)
    )
    w_qkv = lax.all_gather(qkv_shard, ("tensor",) + owners, axis=0, tiled=True)

    offset = lax.axis_index("seq") * block_len
    query_place = offset + jnp.arange(block_len, dtype=jnp.int32)
    valid = (query_place[None, :] < lengths[:, None]).reshape(rows, 1)
    cot = jnp.where(valid, cotangent.reshape(rows, feats), jnp.zeros((), BF))
    scalars = jnp.concatenate([lengths, offset[None].astype(jnp.int32)])
    tables = rotary_tables(positions.reshape(rows))

    normed, resid, mix, pre = front(layers, mix_gain, w_mix, mix_w2, ln_gain, ln_bias)
    kv = project(normed, w_kv, qkv_bias[1:], tables, 1)
    kv_all = lax.all_gather(kv.reshape(2, slots, block_len, width), "seq", axis=0)
    q = project(normed, w_q, qkv_bias[:1], tables, 0)[0]
    attn_vals = attend(scalars, q, kv_all, heads).reshape(rows, width)
    hidden, mlp_in = attn_out(
        attn_vals, w_out, resid, out_bias[None, :], ln_gain[3:4], ln_bias[3:4]
    )
    up_act, grad_up, grad_up_bias = mlp(mlp_in, cot, w_up, w_down, up_bias[None, :])
    scatter = functools.partial(
        lax.psum_scatter, axis_name=owners, scatter_dimension=0, tiled=True
    )
    grad_down, grad_upw, grad_up = tie(
        (row_product(cot, up_act), row_product(mlp_in, grad_up), grad_up)
    )
    grad_attn, small_mlp = mlp_back(grad_up, w_up, hidden, cot, ln_gain[3:4])
    grad_vals = dot(grad_attn, w_out).astype(BF)
    dq, dkv = attend_back(scalars, q, kv_all, grad_vals, tables, heads)
    w_qkv, up_act, dkv = tie((w_qkv, up_act, dkv))
    dkv_own = lax.psum_scatter(dkv, "seq", scatter_dimension=0).reshape(2, rows, width)
    layer_out = mlp_out(up_act, w_down, hidden, down_bias[None, :])
    layer_out, dkv_own, grad_down, grad_upw = tie((layer_out, dkv_own, grad_down, grad_upw))
    shard_down, shard_up = scatter(grad_down), scatter(grad_upw)
    grad_lin = jnp.stack([dq.reshape(rows, width), turn_back(dkv_own, tables), dkv_own[1]])
    grad_owqkv, grad_lin = tie((weight_grads(normed, grad_attn, grad_lin, attn_vals), grad_lin))
    shard_all = scatter(grad_owqkv)
    grads, small_qkv = streams_back(grad_lin, w_qkv, layers, mix, ln_gain)
    shard_down, shard_up, shard_all, grads = tie((shard_down, shard_up, shard_all, grads))
    shard_down, shard_up, shard_all = (
        shard_down.astype(F32), shard_up.astype(F32), shard_all.astype(F32)
    )
    shard_qkv = jnp.stack([shard_all[:, i * width : (i + 1) * width] for i in range(3)])
    shard_out = shard_all[:, 3 * width :]
    grad_layers, grad_gain, grad_w1, grad_w2 = last(
        layers, grads, grad_attn, mix, pre, mix_gain, w_mix, mix_w2
    )
    grad_history = grad_layers.reshape(depth, slots, block_len, feats)
    seqs = lax.axis_size("seq")
    count = lax.axis_size("dp") * seqs
    hidden_count = mix_w1.shape[1]
    share = grad_w1.reshape(hidden_count, count, feats // count).transpose(1, 0, 2)

    def as_row(values):
        flat = values.reshape(1, -1)
        return jnp.pad(flat, ((0, 0), (0, feats - flat.shape[1])))

    grad_qkv_bias = jnp.sum(grad_lin.astype(F32), axis=1)
    ours = jnp.concatenate(
        [small_mlp, jnp.zeros((5, feats), F32), small_qkv.reshape(6, feats)]
        + [
            as_row(values)
            for values in (
                grad_gain, grad_w2, grad_qkv_bias, grad_up_bias, jnp.sum(cot.astype(F32), axis=0)
            )
        ]
        + [jnp.zeros((5, feats), F32)],
        axis=0,
    )
    summed, shard_w1 = small_sums(ours, share.reshape(count, -1, 128), seqs)
    return (
        layer_out.reshape(slots, block_len, feats),
        grad_history,
        summed[14],
        shard_w1.reshape(hidden_count, feats // count).T,
        summed[15, : grad_w2.size].reshape(grad_w2.shape),
        jnp.concatenate([summed[8:11], summed[0:1]], axis=0),
        jnp.concatenate([summed[11:14], summed[1:2]], axis=0),
        shard_qkv,
        summed[16, : grad_qkv_bias.size].reshape(grad_qkv_bias.shape),
        shard_out,
        summed[2],
        shard_up,
        summed[17, : up_bias.size],
        shard_down,
        summed[18],
    )


def solution(mesh):
    in_specs = (
        P(None, "dp", "seq", None),
        P("dp", "seq"),
        P("dp"),
        P("dp", "seq", None),
        P(),
        P(("dp", "seq"), None),
        P(),
        P(),
        P(),
        P(None, ("dp", "seq"), "tensor"),
        P(None, "tensor"),
        P(("dp", "seq"), "tensor"),
        P(),
        P(("dp", "seq"), "tensor"),
        P("tensor"),
        P(("dp", "seq"), "tensor"),
        P(),
    )
    out_specs = (
        P("dp", "seq", None),
        P(None, "dp", "seq", None),
        P(),
        P(("dp", "seq"), None),
        P(),
        P(),
        P(),
        P(None, ("dp", "seq"), "tensor"),
        P(None, "tensor"),
        P(("dp", "seq"), "tensor"),
        P(),
        P(("dp", "seq"), "tensor"),
        P("tensor"),
        P(("dp", "seq"), "tensor"),
        P(),
    )
    return jax.shard_map(shards, mesh=mesh, in_specs=in_specs, out_specs=out_specs, check_vma=False)
```

```python
import functools
import math

import jax
import jax.numpy as jnp
from jax import lax
from jax.experimental import pallas as pl
from jax.experimental.pallas import tpu as pltpu
from jax.sharding import PartitionSpec as P

HEAD_DIM = 128
ROT = 32
STREAMS = 4
EXACT = lax.Precision.HIGHEST
RMS_EPSILON = 1e-06
NORM_EPSILON = 1e-05
BF = jnp.bfloat16
F32 = jnp.float32
MESH = pl.DeviceIdType.MESH
ANY = pl.BlockSpec(memory_space=pl.ANY)
VMEM = pl.BlockSpec(memory_space=pltpu.VMEM)
RING = 4
NN = (((1,), (0,)), ((), ()))
NT = (((1,), (1,)), ((), ()))
TN = (((0,), (0,)), ((), ()))


def dot(left, right, dims=NN, precision=None):
    return lax.dot_general(left, right, dims, precision=precision, preferred_element_type=F32)


def normal_cdf(values):
    return 0.5 * (1.0 + lax.erf(values * math.sqrt(0.5)))


def gelu_slope(values, cdf):
    return cdf + values * (jnp.exp(-0.5 * values * values) * (1.0 / math.sqrt(2.0 * math.pi)))


def mean_last(values):
    return jnp.mean(values, axis=-1, keepdims=True)


def rows_loop(total, step, body):
    def one(index, carry):
        body(pl.ds(pl.multiple_of(index * step, step), step))
        return carry

    lax.fori_loop(0, total // step, one, 0)


def params(limit_mib, collective_id=None):
    if collective_id is None:
        return pltpu.CompilerParams(vmem_limit_bytes=limit_mib << 20)
    return pltpu.CompilerParams(
        vmem_limit_bytes=limit_mib << 20, collective_id=collective_id, has_side_effects=True
    )


def cost(micros):
    return pl.CostEstimate(flops=0, bytes_accessed=int(micros * 3.0e6), transcendentals=0)


def owner_places(seqs, owners):
    rank = lax.axis_index("dp") * seqs + lax.axis_index("seq")
    peers = [lax.rem(rank + k, owners) for k in range(1, owners)]
    return rank, peers, [{"dp": lax.div(p, seqs), "seq": lax.rem(p, seqs)} for p in peers]


def push(source, target, sems, index, place):
    return pltpu.make_async_remote_copy(
        src_ref=source,
        dst_ref=target,
        send_sem=sems.at[0, index],
        recv_sem=sems.at[1, index],
        device_id=place,
        device_id_type=MESH,
    )


def enter(places):
    gate = pltpu.get_barrier_semaphore()
    for place in places:
        pl.semaphore_signal(gate, inc=1, device_id=place, device_id_type=MESH)
    pl.semaphore_wait(gate, len(places))


def front_kernel(
    seqs, owners,
    hist, gain, w1, w2, lg, lb, shard_out, shard_qkv,
    normed_out, resid_out, mix_out, pre_out, w1_out, ring_out, ring_qkv,
    scratch, w1_all, w1_sems, ring_sems, own_sems,
):
    depth, rows, _ = hist.shape
    index = pl.program_id(0)
    ring = Ring(16)
    rank, _, places = owner_places(seqs, owners)
    w1_copies = [push(w1, w1_all.at[rank], w1_sems, k, p) for k, p in enumerate(places)]
    spreads = [
        Spread(ring, slots, ring_sems.at[i], 0, source)
        for i, (slots, source) in enumerate(((ring_out, shard_out), (ring_qkv, shard_qkv)))
    ]
    local = [
        pltpu.make_async_copy(shard_out, ring_out.at[ring.me], own_sems.at[0]),
        pltpu.make_async_copy(shard_qkv, ring_qkv.at[ring.me], own_sems.at[1]),
    ]

    @pl.when(index == 0)
    def _():
        enter(places + [{"tensor": ring.left}, {"tensor": ring.right}])
        for copy in w1_copies:
            copy.start()
        for copy in local:
            copy.start()
        for spread in spreads:
            spread.begin()
        w1_all[rank] = w1[...]
        for copy in w1_copies:
            copy.wait()
        w1_out[...] = w1_all[...].reshape(w1_out.shape)

    @pl.when(index == pl.num_programs(0) - 1)
    def _():
        for spread in spreads:
            spread.relay()

    def rms(part):
        wide = hist[depth - 1, part, :].astype(F32)
        scale = lax.rsqrt(mean_last(wide * wide) + RMS_EPSILON)
        scratch[part, :] = (wide * scale * gain[...]).astype(BF)

    rows_loop(rows, 16, rms)
    pre = dot(scratch[...], w1_out[...])
    pre_out[...] = pre
    mix_out[...] = dot(pre * normal_cdf(pre), w2[...], precision=EXACT)

    def combine(part):
        layers = [hist[j, part, :].astype(F32) for j in range(depth)]
        mix = mix_out[part, :]
        for m in range(STREAMS):
            running = layers[depth - 1]
            for j in range(depth):
                running = running + mix[:, m * depth + j : m * depth + j + 1] * layers[j]
            if m == STREAMS - 1:
                resid_out[part, :] = running
            else:
                centred = running - mean_last(running)
                inverse = lax.rsqrt(mean_last(centred * centred) + NORM_EPSILON)
                normed = centred * inverse * lg[m : m + 1, :] + lb[m : m + 1, :]
                normed_out[m, part, :] = normed.astype(BF)

    rows_loop(rows, 16, combine)

    @pl.when(index == pl.num_programs(0) - 1)
    def _():
        for spread in spreads:
            spread.arrive()
            spread.finish()
        for copy in local:
            copy.wait()


def front(layers, gain, w1, w2, lg, lb, shard_out, shard_qkv, seqs, owners):
    depth, rows, feats = layers.shape
    tile = min(128, rows)
    hidden = w1.shape[1]
    full = lambda shape: pl.BlockSpec(shape, lambda i: (0,) * len(shape))
    return pl.pallas_call(
        functools.partial(front_kernel, seqs, owners),
        grid=(rows // tile,),
        in_specs=[
            pl.BlockSpec((depth, tile, feats), lambda i: (0, i, 0)),
            full((1, feats)),
            full(w1.shape),
            full(w2.shape),
            full(lg.shape),
            full(lb.shape),
            ANY,
            ANY,
        ],
        out_specs=[
            pl.BlockSpec((3, tile, feats), lambda i: (0, i, 0)),
            pl.BlockSpec((tile, feats), lambda i: (i, 0)),
            pl.BlockSpec((tile, STREAMS * depth), lambda i: (i, 0)),
            pl.BlockSpec((tile, hidden), lambda i: (i, 0)),
            full((feats, hidden)),
            ANY,
            ANY,
        ],
        out_shape=[
            jax.ShapeDtypeStruct((3, rows, feats), BF),
            jax.ShapeDtypeStruct((rows, feats), F32),
            jax.ShapeDtypeStruct((rows, STREAMS * depth), F32),
            jax.ShapeDtypeStruct((rows, hidden), F32),
            jax.ShapeDtypeStruct((feats, hidden), BF),
            jax.ShapeDtypeStruct((RING,) + shard_out.shape, BF),
            jax.ShapeDtypeStruct((RING,) + shard_qkv.shape, BF),
        ],
        scratch_shapes=[
            pltpu.VMEM((tile, feats), BF),
            pltpu.VMEM((owners,) + w1.shape, BF),
            pltpu.SemaphoreType.DMA((2, owners - 1)),
            pltpu.SemaphoreType.DMA((2, 2, 4)),
            pltpu.SemaphoreType.DMA((2,)),
        ],
        compiler_params=params(48, 5),
        cost_estimate=cost(70),
        name="front",
    )(layers, gain.reshape(1, feats), w1, w2, lg, lb, shard_out, shard_qkv)


def turn(values, tables, sign):
    cosines, low, high = tables
    return values * cosines + sign * (
        pltpu.roll(values, HEAD_DIM - ROT // 2, 1) * low + pltpu.roll(values, ROT // 2, 1) * high
    )


def rotary_tables(positions):
    exponents = jnp.arange(0, ROT, 2).astype(F32) / ROT
    inverse = jnp.power(10000.0, -exponents)
    phases = positions.astype(F32)[:, None] * inverse[None, :]
    cosines, sines = jnp.cos(phases), jnp.sin(phases)
    rows, half = phases.shape
    ones = jnp.ones((rows, HEAD_DIM - 2 * half), F32)
    none = jnp.zeros((rows, HEAD_DIM - 2 * half), F32)
    zero = jnp.zeros((rows, half), F32)
    return jnp.stack(
        [
            jnp.concatenate([cosines, cosines, ones], axis=1),
            jnp.concatenate([-sines, zero, none], axis=1),
            jnp.concatenate([zero, sines, none], axis=1),
        ]
    )


def proj_kernel(first, lhs, weight, bias, tables, out):
    branch = pl.program_id(0) + first
    value = dot(lhs[0], weight[...]) + bias[0]

    @pl.when(branch < 2)
    def _():
        tabs = (tables[0], tables[1], tables[2])
        for head in range(value.shape[1] // HEAD_DIM):
            cols = slice(head * HEAD_DIM, (head + 1) * HEAD_DIM)
            out[0, :, cols] = turn(value[:, cols], tabs, 1.0).astype(BF)

    @pl.when(branch >= 2)
    def _():
        out[0] = value.astype(BF)


def project(normed, weight, bias, tables, first):
    _, rows, feats = normed.shape
    count, width = bias.shape
    tile = min(256, rows)
    return pl.pallas_call(
        functools.partial(proj_kernel, first),
        grid=(count, rows // tile),
        in_specs=[
            pl.BlockSpec((1, tile, feats), lambda b, r: (b + first, r, 0)),
            pl.BlockSpec((feats, width), lambda b, r: (0, b)),
            pl.BlockSpec((1, 1, width), lambda b, r: (b, 0, 0)),
            pl.BlockSpec((3, tile, HEAD_DIM), lambda b, r: (0, r, 0)),
        ],
        out_specs=pl.BlockSpec((1, tile, width), lambda b, r: (b, r, 0)),
        out_shape=jax.ShapeDtypeStruct((count, rows, width), BF),
        compiler_params=params(40),
        cost_estimate=cost(4 * count),
        name="project",
    )(normed, weight, bias.reshape(count, 1, width), tables)


def share_kernel(lhs, weight, bias, tables, kv, q_out, kv_out, sems, own_sem):
    seqs = kv_out.shape[0]
    me = lax.axis_index("seq")
    places = [{"seq": lax.rem(me + k, seqs)} for k in range(1, seqs)]
    local = pltpu.make_async_copy(kv, kv_out.at[me], own_sem)
    local.start()
    enter(places)
    copies = [push(kv, kv_out.at[me], sems, k, place) for k, place in enumerate(places)]
    for copy in copies:
        copy.start()

    def rows(part):
        value = dot(lhs[0, part, :], weight[...]) + bias[...]
        tabs = (tables[0, part, :], tables[1, part, :], tables[2, part, :])
        for head in range(value.shape[1] // HEAD_DIM):
            cols = slice(head * HEAD_DIM, (head + 1) * HEAD_DIM)
            q_out[part, cols] = turn(value[:, cols], tabs, 1.0).astype(BF)

    rows_loop(lhs.shape[1], 256, rows)
    for copy in copies:
        copy.wait()
    local.wait()


def share(normed, weight, bias, tables, kv, seqs):
    _, rows, feats = normed.shape
    width = weight.shape[1]
    return pl.pallas_call(
        share_kernel,
        grid=(1,),
        in_specs=[
            pl.BlockSpec((1, rows, feats), lambda i: (0, 0, 0)),
            pl.BlockSpec(weight.shape, lambda i: (0, 0)),
            pl.BlockSpec(bias.shape, lambda i: (0, 0)),
            pl.BlockSpec(tables.shape, lambda i: (0, 0, 0)),
            ANY,
        ],
        out_specs=[pl.BlockSpec((rows, width), lambda i: (0, 0)), ANY],
        out_shape=[
            jax.ShapeDtypeStruct((rows, width), BF),
            jax.ShapeDtypeStruct((seqs,) + kv.shape, BF),
        ],
        scratch_shapes=[
            pltpu.SemaphoreType.DMA((2, seqs - 1)),
            pltpu.SemaphoreType.DMA,
        ],
        compiler_params=params(48, 6),
        cost_estimate=cost(50),
        name="share",
    )(normed, weight, bias, tables, kv)


def attend_kernel(scalars, q, k, v, out):
    keys = k[...].reshape(-1, HEAD_DIM)
    values = v[...].reshape(-1, HEAD_DIM)
    length = scalars[pl.program_id(0)]
    offset = scalars[pl.num_programs(0)]
    scores = dot(q[0], keys, NT) * (1.0 / math.sqrt(HEAD_DIM))
    key_place = lax.broadcasted_iota(jnp.int32, scores.shape, 1)
    query_place = lax.broadcasted_iota(jnp.int32, scores.shape, 0) + offset
    scores = jnp.where((key_place <= query_place) & (key_place < length), scores, -1e30)
    weights = jnp.exp(scores - jnp.max(scores, axis=-1, keepdims=True))
    total = jnp.sum(weights, axis=-1, keepdims=True)
    probs = (weights * (1.0 / total)).astype(BF)
    out[0] = dot(probs, values).astype(BF)


def attend(scalars, q, kv, heads):
    seqs, _, slots, length, width = kv.shape
    block = (1, length, HEAD_DIM)
    return pl.pallas_call(
        attend_kernel,
        grid_spec=pltpu.PrefetchScalarGridSpec(
            num_scalar_prefetch=1,
            grid=(slots, heads),
            in_specs=[
                pl.BlockSpec(block, lambda s, h, _: (s, 0, h)),
                pl.BlockSpec((seqs, 1, 1, length, HEAD_DIM), lambda s, h, _: (0, 0, s, 0, h)),
                pl.BlockSpec((seqs, 1, 1, length, HEAD_DIM), lambda s, h, _: (0, 1, s, 0, h)),
            ],
            out_specs=pl.BlockSpec(block, lambda s, h, _: (s, 0, h)),
        ),
        out_shape=jax.ShapeDtypeStruct((slots, length, width), BF),
        compiler_params=params(40),
        cost_estimate=cost(15),
        name="attend",
    )(scalars, q.reshape(slots, length, width), kv, kv)


def attend_back_kernel(scalars, q, k, v, g, tables, dq_out, dkv_out):
    seqs = k.shape[0]
    scaling = 1.0 / math.sqrt(HEAD_DIM)
    keys = k[...].reshape(-1, HEAD_DIM)
    values = v[...].reshape(-1, HEAD_DIM)
    length = scalars[pl.program_id(0)]
    offset = scalars[pl.num_programs(0)]
    queries, grads = q[0], g[0]
    scores = dot(keys, queries, NT) * scaling
    key_place = lax.broadcasted_iota(jnp.int32, scores.shape, 0)
    query_place = lax.broadcasted_iota(jnp.int32, scores.shape, 1) + offset
    scores = jnp.where((key_place <= query_place) & (key_place < length), scores, -1e30)
    weights = jnp.exp(scores - jnp.max(scores, axis=0, keepdims=True))
    probs = weights * (1.0 / jnp.sum(weights, axis=0, keepdims=True))
    grad_probs = dot(values, grads, NT)
    mixed = jnp.sum(probs * grad_probs, axis=0, keepdims=True)
    grad_scores = (probs * (grad_probs - mixed)).astype(BF)
    grad_values = dot(probs.astype(BF), grads)
    grad_keys = dot(grad_scores, queries) * scaling
    shape = (seqs, -1, HEAD_DIM)
    dkv_out[:, 0, 0] = grad_keys.astype(BF).reshape(shape)
    dkv_out[:, 1, 0] = grad_values.astype(BF).reshape(shape)
    grad_queries = dot(grad_scores, keys, TN) * scaling
    tabs = (tables[0], tables[1], tables[2])
    dq_out[0] = turn(grad_queries, tabs, -1.0).astype(BF)


def attend_back(scalars, q, kv, g, tables, heads):
    seqs, _, slots, length, width = kv.shape
    block = (1, length, HEAD_DIM)
    own = pl.BlockSpec(block, lambda s, h, _: (s, 0, h))
    return pl.pallas_call(
        attend_back_kernel,
        grid_spec=pltpu.PrefetchScalarGridSpec(
            num_scalar_prefetch=1,
            grid=(slots, heads),
            in_specs=[
                own,
                pl.BlockSpec((seqs, 1, 1, length, HEAD_DIM), lambda s, h, _: (0, 0, s, 0, h)),
                pl.BlockSpec((seqs, 1, 1, length, HEAD_DIM), lambda s, h, _: (0, 1, s, 0, h)),
                own,
                pl.BlockSpec((3, length, HEAD_DIM), lambda s, h, _: (0, s, 0)),
            ],
            out_specs=[
                own,
                pl.BlockSpec((seqs, 2, 1, length, HEAD_DIM), lambda s, h, _: (0, 0, s, 0, h)),
            ],
        ),
        out_shape=[
            jax.ShapeDtypeStruct((slots, length, width), BF),
            jax.ShapeDtypeStruct((seqs, 2, slots, length, width), BF),
        ],
        compiler_params=params(48),
        cost_estimate=cost(25),
        name="attend_back",
    )(scalars, q.reshape(slots, length, width), kv, kv, g.reshape(slots, length, width), tables)


class Ring:
    def __init__(self, chunk):
        me = lax.axis_index("tensor")
        self.chunk, self.half = chunk, chunk // 2
        self.me = me
        self.right = lax.rem(me + 1, RING)
        self.left = lax.rem(me + RING - 1, RING)
        self.far = lax.rem(me + 2, RING)

    def at(self, index, shift=0):
        return pl.multiple_of(index * self.chunk + shift, self.half)

    def barrier(self):
        gate = pltpu.get_barrier_semaphore()
        for near in (self.left, self.right):
            pl.semaphore_signal(gate, inc=1, device_id={"tensor": near}, device_id_type=MESH)
        pl.semaphore_wait(gate, 2)


def remote(source, target, sems, index, device):
    return pltpu.make_async_remote_copy(
        src_ref=source,
        dst_ref=target,
        send_sem=sems.at[0, index],
        recv_sem=sems.at[1, index],
        device_id={"tensor": device},
        device_id_type=MESH,
    )


def product(lhs, rhs, start, count, write, step=512):
    total = rhs.shape[0]

    def one(cols):
        write(cols, dot(lhs[pl.ds(start, count), :], rhs[cols, :], NT))

    rows_loop(total, min(step, total), one)


class Scatter:
    def __init__(self, ring, lhs, rhs, far, near, far_in, near_in, sems):
        self.ring, self.lhs, self.rhs = ring, lhs, rhs
        self.far, self.near, self.far_in, self.near_in = far, near, far_in, near_in
        half = ring.half
        up, down = pl.ds(0, half), pl.ds(half, half)
        self.copies = [
            remote(far.at[0], far_in.at[0], sems, 0, ring.right),
            remote(far.at[1], far_in.at[1], sems, 1, ring.left),
            remote(near.at[0, down], near_in.at[0, down], sems, 2, ring.right),
            remote(near.at[1, up], near_in.at[1, up], sems, 3, ring.left),
            remote(near.at[0, up], near_in.at[0, up], sems, 4, ring.right),
            remote(near.at[1, down], near_in.at[1, down], sems, 5, ring.left),
        ]

    def begin(self):
        ring, half = self.ring, self.ring.half

        def far_half(which):
            def write(cols, value):
                self.far[which, :, cols] = value.astype(BF)

            product(self.lhs, self.rhs, ring.at(ring.far, which * half), half, write)
            self.copies[which].start()

        def near_half(which, device, part, copy):
            def write(cols, value):
                self.near[which, pl.ds(part * half, half), cols] = value.astype(BF)

            product(self.lhs, self.rhs, ring.at(device, part * half), half, write)
            self.copies[copy].start()

        far_half(0)
        far_half(1)
        near_half(0, ring.right, 1, 2)
        near_half(1, ring.left, 0, 3)

    def relay(self):
        ring, half = self.ring, self.ring.half

        def add_half(which, device, part, copy):
            self.copies[which].wait_recv()

            def write(cols, value):
                arrived = self.far_in[which, :, cols].astype(F32)
                self.near[which, pl.ds(part * half, half), cols] = (value + arrived).astype(BF)

            product(self.lhs, self.rhs, ring.at(device, part * half), half, write)
            self.copies[copy].start()

        add_half(0, ring.right, 0, 4)
        add_half(1, ring.left, 1, 5)

    def arrive(self):
        for copy in self.copies[2:]:
            copy.wait_recv()

    def finish(self):
        for copy in self.copies:
            copy.wait_send()


class Gather:
    def __init__(self, ring, own, out, sems, base, local_sem):
        half = ring.half

        def rows(index, shift=0, count=ring.chunk):
            return out.at[pl.ds(ring.at(index, shift), count), :]

        mine = rows(ring.me)
        self.local = pltpu.make_async_copy(own, mine, local_sem)
        self.first = [
            remote(own, mine, sems, base, ring.right),
            remote(own, mine, sems, base + 1, ring.left),
        ]
        up, down = rows(ring.left, 0, half), rows(ring.right, half, half)
        self.second = [
            remote(up, up, sems, base + 2, ring.right),
            remote(down, down, sems, base + 3, ring.left),
        ]

    def begin(self):
        for copy in self.first:
            copy.start()
        self.local.start()

    def relay(self):
        for arrived, onward in zip(self.first, self.second):
            arrived.wait_recv()
            onward.start()

    def finish(self):
        for copy in self.second:
            copy.wait_recv()
        for copy in self.first + self.second:
            copy.wait_send()
        self.local.wait()


def scatter_scratch(chunk, feats, count=1):
    half = chunk // 2
    lead = () if count == 1 else (count,)
    return [
        pltpu.VMEM(lead + (2, half, feats), BF),
        pltpu.VMEM(lead + (2, chunk, feats), BF),
        pltpu.VMEM(lead + (2, half, feats), BF),
        pltpu.VMEM(lead + (2, chunk, feats), BF),
    ]


def own_sum(scatter, total):
    ring = scatter.ring

    def write(cols, value):
        total[:, cols] = value

    product(scatter.lhs, scatter.rhs, ring.at(ring.me), ring.chunk, write)


def whole_sum(scatter, total, part):
    near = scatter.near_in
    return total[part, :] + near[0, part, :].astype(F32) + near[1, part, :].astype(F32)


def weight_copies(weight, target, sems, index):
    count = weight.shape[-2]

    def one(owner):
        source = weight.at[owner] if index is None else weight.at[owner, :, index]
        return pltpu.make_async_copy(
            source,
            target.at[:, pl.ds(pl.multiple_of(owner * count, count), count), :],
            sems.at[owner],
        )

    def every(act):
        def step(owner, carry):
            act(one(owner))
            return carry

        lax.fori_loop(0, weight.shape[0], step, 0)

    return every


def ring_product(slots, weight, part, total):
    def columns(cols):
        value = dot(slots[0, part, :], weight[0, cols, :], NT)
        for z in range(1, RING):
            value += dot(slots[z, part, :], weight[z, cols, :], NT)
        total[:, cols] = value

    rows_loop(total.shape[1], 512, columns)


def attn_out_kernel(
    vals, weight, resid, bias, lg, lb, hidden_out, mlp_out,
    slots, weights, total, base_rows, stage, sems, weight_sems, base_sem, stage_sems, own_sem,
):
    chunk, feats = total.shape
    ring = Ring(chunk)
    load = weight_copies(weight, weights, weight_sems, None)
    load(lambda copy: copy.start())
    local = pltpu.make_async_copy(vals, slots.at[ring.me], own_sem)
    local.start()
    ring.barrier()
    spread = Spread(ring, slots, sems, 0, vals)
    spread.begin()
    spread.relay()
    load(lambda copy: copy.wait())
    local.wait()
    spread.arrive()

    def write_out(index, slot):
        part = pl.ds(pl.multiple_of(index * chunk, chunk), chunk)
        return pltpu.make_async_copy(stage.at[slot], mlp_out.at[part, :], stage_sems.at[slot])

    def one(index, carry):
        part = pl.ds(pl.multiple_of(index * chunk, chunk), chunk)
        fetch = pltpu.make_async_copy(resid.at[part, :], base_rows, base_sem)
        fetch.start()
        slot = lax.rem(index, 2)
        ring_product(slots, weights, part, total)
        fetch.wait()

        @pl.when(index >= 2)
        def _():
            write_out(index - 2, slot).wait()

        def norm(sub):
            value = base_rows[sub, :] + (total[sub, :] + bias[...])
            total[sub, :] = value
            centred = value - mean_last(value)
            inverse = lax.rsqrt(mean_last(centred * centred) + NORM_EPSILON)
            stage[slot, sub, :] = (centred * inverse * lg[...] + lb[...]).astype(BF)

        rows_loop(chunk, 16, norm)
        write_out(index, slot).start()

        @pl.when(index == ring.me)
        def _():
            hidden_out[...] = total[...]

        return carry

    lax.fori_loop(0, RING, one, 0)
    for index in range(RING - 2, RING):
        write_out(index, index % 2).wait()
    spread.finish()


def attn_out(vals, weight, resid, bias, lg, lb):
    rows, feats = resid.shape
    width = vals.shape[1]
    chunk = rows // RING
    return pl.pallas_call(
        attn_out_kernel,
        in_specs=[VMEM, ANY, ANY, VMEM, VMEM, VMEM],
        out_specs=[VMEM, ANY],
        out_shape=[
            jax.ShapeDtypeStruct((chunk, feats), F32),
            jax.ShapeDtypeStruct((rows, feats), BF),
        ],
        scratch_shapes=[
            pltpu.VMEM((RING, rows, width), BF),
            pltpu.VMEM((RING, feats, width), BF),
            pltpu.VMEM((chunk, feats), F32),
            pltpu.VMEM((chunk, feats), F32),
            pltpu.VMEM((2, chunk, feats), BF),
            pltpu.SemaphoreType.DMA((2, 4)),
            pltpu.SemaphoreType.DMA((weight.shape[0],)),
            pltpu.SemaphoreType.DMA,
            pltpu.SemaphoreType.DMA((2,)),
            pltpu.SemaphoreType.DMA,
        ],
        compiler_params=params(48, 0),
        cost_estimate=cost(95),
        name="attn_out",
    )(vals, weight, resid, bias, lg, lb)


def layer_out_kernel(own, out, sems, own_sem):
    chunk = own.shape[0]
    ring = Ring(chunk)
    ring.barrier()
    gather = Gather(ring, own, out, sems, 0, own_sem)
    gather.begin()
    gather.relay()
    gather.finish()


def spread_rows(own):
    chunk, feats = own.shape
    return pl.pallas_call(
        layer_out_kernel,
        in_specs=[VMEM],
        out_specs=ANY,
        out_shape=jax.ShapeDtypeStruct((RING * chunk, feats), BF),
        scratch_shapes=[pltpu.SemaphoreType.DMA((2, 4)), pltpu.SemaphoreType.DMA],
        compiler_params=params(32, 3),
        cost_estimate=cost(72),
        name="spread_rows",
    )(own)


def weights_kernel(normed, grad_attn, grad_lin, attn_vals, out):
    branch = pl.program_id(0)

    @pl.when(branch < 3)
    def _():
        out[...] = dot(normed[0], grad_lin[0], TN).astype(BF)

    @pl.when(branch == 3)
    def _():
        out[...] = dot(grad_attn[...], attn_vals[...], TN).astype(BF)


def weight_grads(normed, grad_attn, grad_lin, attn_vals):
    _, rows, feats = normed.shape
    width = attn_vals.shape[1]
    cols = 512
    last_block = feats // cols - 1
    return pl.pallas_call(
        weights_kernel,
        grid=(4, feats // cols),
        in_specs=[
            pl.BlockSpec(
                (1, rows, cols),
                lambda b, n: (jnp.minimum(b, 2), 0, jnp.where(b < 3, n, last_block)),
            ),
            pl.BlockSpec((rows, cols), lambda b, n: (0, jnp.where(b < 3, 0, n))),
            pl.BlockSpec((1, rows, width), lambda b, n: (jnp.minimum(b, 2), 0, 0)),
            pl.BlockSpec((rows, width), lambda b, n: (0, 0)),
        ],
        out_specs=pl.BlockSpec((cols, width), lambda b, n: (n, b)),
        out_shape=jax.ShapeDtypeStruct((feats, 4 * width), BF),
        compiler_params=params(40),
        cost_estimate=cost(15),
        name="weight_grads",
    )(normed, grad_attn, grad_lin, attn_vals)


def norm_back(values, grads, gain):
    centred = values - mean_last(values)
    inverse = lax.rsqrt(mean_last(centred * centred) + NORM_EPSILON)
    normed = centred * inverse
    inner = grads * gain
    back = inverse * (inner - mean_last(inner) - normed * mean_last(inner * normed))
    return back, normed


def fold(values):
    rows, feats = values.shape
    return jnp.sum(values.reshape(rows // 8, 8, feats), axis=0)


def weight_product(source, rhs, out, blocks, stage, load_sems, store_sems):
    width = blocks.shape[2]
    count = source.shape[1] // width

    def load(n, slot):
        cols = pl.ds(pl.multiple_of(n * width, width), width)
        return pltpu.make_async_copy(source.at[:, cols], blocks.at[slot], load_sems.at[slot])

    def store(n, slot):
        part = pl.ds(pl.multiple_of(n * width, width), width)
        return pltpu.make_async_copy(stage.at[slot], out.at[part, :], store_sems.at[slot])

    load(0, 0).start()

    def one(n, carry):
        slot = lax.rem(n, 2)

        @pl.when(n + 1 < count)
        def _():
            load(n + 1, 1 - slot).start()

        load(n, slot).wait()

        @pl.when(n >= 2)
        def _():
            store(n - 2, slot).wait()

        def columns(cols):
            stage[slot, :, cols] = dot(blocks[slot], rhs[:, cols], TN).astype(BF)

        rows_loop(rhs.shape[1], 512, columns)
        store(n, slot).start()
        return carry

    lax.fori_loop(0, count, one, 0)
    for n in range(count - 2, count):
        store(n, n % 2).wait()


class Line:
    def __init__(self, chunk):
        me = lax.axis_index("tensor")
        self.me, self.chunk = me, chunk
        self.low = me < 2
        self.outer = (me == 0) | (me == RING - 1)
        self.inner = (me == 1) | (me == RING - 2)
        self.up = jnp.where(self.low, me + 1, me - 1)
        self.down = jnp.where(self.low, lax.max(me - 1, 0), lax.min(me + 1, RING - 1))

    def at(self, number):
        index = jnp.where(self.low, number, RING - 1 - number)
        return pl.ds(pl.multiple_of(index * self.chunk, self.chunk), self.chunk)

    def barrier(self):
        gate = pltpu.get_barrier_semaphore()
        pl.semaphore_signal(gate, inc=1, device_id={"tensor": self.up}, device_id_type=MESH)

        @pl.when(self.inner)
        def _():
            pl.semaphore_signal(
                gate, inc=1, device_id={"tensor": self.down}, device_id_type=MESH
            )
            pl.semaphore_wait(gate, 2)

        @pl.when(self.outer)
        def _():
            pl.semaphore_wait(gate, 1)


class LineSum:
    def __init__(self, line, lhs, rhs, outbound, inbound, sems, base):
        self.line, self.lhs, self.rhs = line, lhs, rhs
        self.outbound, self.inbound = outbound, inbound
        copy = lambda slot, target, device: remote(
            outbound.at[slot], inbound.at[target], sems, base + target, device
        )
        self.inward = [copy(i, i, line.up) for i in range(3)]
        self.across = [copy(i, 3 + i, line.up) for i in range(2)]
        self.outward = remote(outbound.at[2], inbound.at[5], sems, base + 5, line.down)

    def partial(self, number, slot, arrived=None):
        rows = self.line.at(number)

        def write(cols, value):
            if arrived is not None:
                value = value + self.inbound[arrived, :, cols].astype(F32)
            self.outbound[slot, :, cols] = value.astype(BF)

        product(self.lhs, self.rhs, rows.start, self.line.chunk, write)

    def own(self, total):
        index = self.line.me * self.line.chunk

        def write(cols, value):
            total[:, cols] = value

        product(
            self.lhs, self.rhs, pl.multiple_of(index, self.line.chunk), self.line.chunk, write
        )

    def send_inward(self):
        for slot, copy in enumerate(self.inward):
            self.partial(3 - slot, slot)
            copy.start()

    def send_across(self, i):
        self.inward[i].wait_recv()
        self.partial(3 - i, i, i)
        self.across[i].start()

    def send_outward(self):
        self.across[0].wait_recv()
        self.partial(0, 2, 3)
        self.outward.start()

    def arrive(self):
        line = self.line

        @pl.when(line.inner)
        def _():
            self.inward[2].wait_recv()
            self.across[1].wait_recv()

        @pl.when(line.outer)
        def _():
            self.outward.wait_recv()

    def sent(self):
        line = self.line

        @pl.when(line.inner)
        def _():
            for copy in self.across + [self.outward]:
                copy.wait_send()

        @pl.when(line.outer)
        def _():
            for copy in self.inward:
                copy.wait_send()

    def clear(self):
        @pl.when(self.line.outer)
        def _():
            self.inbound[2] = jnp.zeros_like(self.inbound[2])

    def whole(self, total, part):
        last = jnp.where(self.line.outer, 5, 4)
        return (
            total[part, :]
            + self.inbound[2, part, :].astype(F32)
            + self.inbound[last, part, :].astype(F32)
        )


def mlp_back_kernel(
    lhs, rhs, acts, down, hidden, cot, mlp_in, lg, down_bias,
    grad_out, small_out, rows_out, grad_up, grad_down,
    outbound, inbound, total, cot_rows, own, sums, blocks, stage,
    sems, gather_sems, local_sems, load_sems, store_sems,
):
    chunk, feats = total.shape
    line = Line(chunk)
    mine = pl.ds(pl.multiple_of(line.me * chunk, chunk), chunk)
    fetch = pltpu.make_async_copy(cot.at[mine, :], cot_rows, local_sems.at[0])
    fetch.start()
    line.barrier()
    first = LineSum(line, lhs, rhs, outbound, inbound.at[0], sems.at[0], 0)
    second = LineSum(line, acts, down, outbound, inbound.at[1], sems.at[1], 0)
    first.clear()
    second.clear()

    @pl.when(line.outer)
    def _():
        first.send_inward()

    first.own(total)
    sums[...] = jnp.zeros_like(sums)
    weight_product(mlp_in, lhs, grad_up, blocks, stage, load_sems, store_sems)

    @pl.when(line.inner)
    def _():
        first.send_across(0)
        first.send_across(1)
        first.send_outward()

    weight_product(cot, acts, grad_down, blocks, stage, load_sems, store_sems)
    fetch.wait()
    first.arrive()

    def back(part):
        grads = first.whole(total, part)
        step, normed = norm_back(hidden[part, :], grads, lg[...])
        low = (cot_rows[part, :].astype(F32) + step).astype(BF)
        own[part, :] = low
        sums[0] += fold(grads * normed)
        sums[1] += fold(grads)
        sums[2] += fold(low.astype(F32))

    rows_loop(chunk, 16, back)
    local = pltpu.make_async_copy(own, grad_out.at[mine, :], local_sems.at[1])
    local.start()
    first.sent()

    def chunk_copy(number, index, device, source=None):
        rows = grad_out.at[line.at(number), :]
        return remote(rows if source is None else source, rows, gather_sems, index, device)

    @pl.when(line.outer)
    def _():
        onward = chunk_copy(0, 0, line.up, own)
        onward.start()
        second.send_inward()
        second.own(total)
        for number in range(1, RING):
            chunk_copy(number, 2 + number, line.up).wait_recv()
        onward.wait_send()

    @pl.when(line.inner)
    def _():
        inward = [chunk_copy(1, 1, line.up, own), chunk_copy(1, 3, line.down, own)]
        for copy in inward:
            copy.start()
        second.own(total)
        chunk_copy(0, 0, line.up).wait_recv()
        relay = chunk_copy(0, 2, line.up)
        relay.start()
        chunk_copy(2, 1, line.up).wait_recv()
        near = chunk_copy(2, 4, line.down)
        near.start()
        second.send_across(0)
        chunk_copy(3, 2, line.up).wait_recv()
        far = chunk_copy(3, 5, line.down)
        far.start()
        second.send_across(1)
        second.send_outward()
        for copy in inward + [relay, near, far]:
            copy.wait_send()

    for i in range(3):
        small_out[i : i + 1, :] = jnp.sum(sums[i], axis=0, keepdims=True)
    second.arrive()

    def add(part):
        value = hidden[part, :] + (second.whole(total, part) + down_bias[...])
        rows_out[part, :] = value.astype(BF)

    rows_loop(chunk, 16, add)
    second.sent()
    local.wait()


def mlp_back(lhs, rhs, acts, down, hidden, cot, mlp_in, lg, down_bias):
    rows, feats = cot.shape
    width = lhs.shape[1]
    chunk = rows // RING
    block = 256
    return pl.pallas_call(
        mlp_back_kernel,
        in_specs=[VMEM, VMEM, VMEM, VMEM, VMEM, ANY, ANY, VMEM, VMEM],
        out_specs=[ANY, VMEM, VMEM, ANY, ANY],
        out_shape=[
            jax.ShapeDtypeStruct((rows, feats), BF),
            jax.ShapeDtypeStruct((3, feats), F32),
            jax.ShapeDtypeStruct((chunk, feats), BF),
            jax.ShapeDtypeStruct((feats, width), BF),
            jax.ShapeDtypeStruct((feats, width), BF),
        ],
        scratch_shapes=[
            pltpu.VMEM((3, chunk, feats), BF),
            pltpu.VMEM((2, 6, chunk, feats), BF),
            pltpu.VMEM((chunk, feats), F32),
            pltpu.VMEM((chunk, feats), BF),
            pltpu.VMEM((chunk, feats), BF),
            pltpu.VMEM((3, 8, feats), F32),
            pltpu.VMEM((2, rows, block), BF),
            pltpu.VMEM((2, block, width), BF),
            pltpu.SemaphoreType.DMA((2, 2, 6)),
            pltpu.SemaphoreType.DMA((2, 6)),
            pltpu.SemaphoreType.DMA((2,)),
            pltpu.SemaphoreType.DMA((2,)),
            pltpu.SemaphoreType.DMA((2,)),
        ],
        compiler_params=params(60, 1),
        cost_estimate=cost(175),
        name="mlp_back",
    )(lhs, rhs, acts, down, hidden, cot, mlp_in, lg, down_bias)


class Spread:
    def __init__(self, ring, slots, sems, base, source):
        half = slots.shape[1] // 2
        mine = slots.at[ring.me]
        self.first = [
            remote(source, mine, sems, base, ring.right),
            remote(source, mine, sems, base + 1, ring.left),
        ]
        up = slots.at[ring.left, pl.ds(0, half), :]
        down = slots.at[ring.right, pl.ds(half, half), :]
        self.second = [
            remote(up, up, sems, base + 2, ring.right),
            remote(down, down, sems, base + 3, ring.left),
        ]

    def begin(self):
        for copy in self.first:
            copy.start()

    def relay(self):
        for arrived, onward in zip(self.first, self.second):
            arrived.wait_recv()
            onward.start()

    def arrive(self):
        for copy in self.second:
            copy.wait_recv()

    def finish(self):
        for copy in self.first + self.second:
            copy.wait_send()


def streams_back_kernel(
    lin, weight, hist, mix, lg, grads_out, small_out,
    slots, weights, total, layers, stage, sums, sems, weight_sems, layer_sem, stage_sems, own_sems,
):
    tile, feats = total.shape
    depth = layers.shape[0]
    rows, width = lin.shape[1], lin.shape[2]
    tiles = rows // tile
    ring = Ring(rows)

    def fetch(stream):
        return weight_copies(
            weight, weights.at[stream % 2], weight_sems.at[stream % 2], stream
        )

    local = [
        pltpu.make_async_copy(lin.at[i], slots.at[i, ring.me], own_sems.at[i]) for i in range(3)
    ]
    for copy in local:
        copy.start()
    for stream in range(2):
        fetch(stream)(lambda copy: copy.start())
    sums[...] = jnp.zeros_like(sums)
    ring.barrier()
    spreads = [Spread(ring, slots.at[i], sems.at[i], 0, lin.at[i]) for i in range(3)]

    def write_out(stream, index, slot):
        part = pl.ds(pl.multiple_of(index * tile, tile), tile)
        return pltpu.make_async_copy(
            stage.at[slot], grads_out.at[stream, part, :], stage_sems.at[slot]
        )

    def compute(stream):
        fetch(stream)(lambda copy: copy.wait())

        def one(index, carry):
            part = pl.ds(pl.multiple_of(index * tile, tile), tile)
            load = pltpu.make_async_copy(hist.at[:, part, :], layers, layer_sem)
            load.start()
            slot = lax.rem(index, 2)

            ring_product(slots.at[stream], weights.at[stream % 2], part, total)
            load.wait()

            @pl.when(index >= 2)
            def _():
                write_out(stream, index - 2, slot).wait()

            def back(sub):
                grads = total[sub, :]
                latest = layers[depth - 1, sub, :].astype(F32)
                at = pl.multiple_of(index * tile + sub.start, 16)
                share = mix[pl.ds(at, 16), :]
                mixture = latest
                for j in range(depth):
                    col = stream * depth + j
                    mixture = mixture + share[:, col : col + 1] * layers[j, sub, :].astype(F32)
                step, normed = norm_back(mixture, grads, lg[stream : stream + 1, :])
                stage[slot, sub, :] = step.astype(BF)
                sums[stream, 0] += fold(grads * normed)
                sums[stream, 1] += fold(grads)

            rows_loop(tile, 16, back)
            write_out(stream, index, slot).start()
            return carry

        lax.fori_loop(0, tiles, one, 0)
        for index in range(max(tiles - 2, 0), tiles):
            write_out(stream, index, index % 2).wait()
        if stream == 0:
            fetch(2)(lambda copy: copy.start())

    for copy in local:
        copy.wait()
    spreads[0].begin()
    spreads[1].begin()
    spreads[0].relay()
    spreads[2].begin()
    spreads[1].relay()
    spreads[0].arrive()
    compute(0)
    spreads[2].relay()
    spreads[1].arrive()
    compute(1)
    spreads[2].arrive()
    compute(2)
    for i in range(3):
        for j in range(2):
            small_out[j, i : i + 1, :] = jnp.sum(sums[i, j], axis=0, keepdims=True)
    for spread in spreads:
        spread.finish()


def streams_back(lin, weight, hist, mix, lg):
    depth, rows, feats = hist.shape
    width = lin.shape[2]
    tile = min(256, rows)
    return pl.pallas_call(
        streams_back_kernel,
        in_specs=[VMEM, ANY, ANY, VMEM, VMEM],
        out_specs=[ANY, VMEM],
        out_shape=[
            jax.ShapeDtypeStruct((3, rows, feats), BF),
            jax.ShapeDtypeStruct((2, 3, feats), F32),
        ],
        scratch_shapes=[
            pltpu.VMEM((3, RING, rows, width), BF),
            pltpu.VMEM((2, RING, feats, width), BF),
            pltpu.VMEM((tile, feats), F32),
            pltpu.VMEM((depth, tile, feats), BF),
            pltpu.VMEM((2, tile, feats), BF),
            pltpu.VMEM((3, 2, 8, feats), F32),
            pltpu.SemaphoreType.DMA((3, 2, 4)),
            pltpu.SemaphoreType.DMA((2, weight.shape[0])),
            pltpu.SemaphoreType.DMA,
            pltpu.SemaphoreType.DMA((2,)),
            pltpu.SemaphoreType.DMA((3,)),
        ],
        compiler_params=params(58, 2),
        cost_estimate=cost(240),
        name="streams_back",
    )(lin, weight, hist, mix, lg)


def small_kernel(seqs, owners, ours, share, out, share_out, near, all_ours, all_shares, near_sems, sems):
    ring = Ring(2)
    near_rows = near.shape[1]
    rank, peers, places = owner_places(seqs, owners)
    mates = [ring.right, ring.far, ring.left]
    enter(places + [{"tensor": z} for z in mates])

    near[ring.me] = ours[0:near_rows, :]
    shares = [
        push(share.at[p], all_shares.at[rank], sems.at[0], k, place)
        for k, (p, place) in enumerate(zip(peers, places))
    ]
    first = [
        push(near.at[ring.me], near.at[ring.me], near_sems, k, {"tensor": z})
        for k, z in enumerate(mates)
    ]
    for copy in first + shares:
        copy.start()
    for copy in first:
        copy.wait()
    all_ours[rank, 0:near_rows, :] = (near[0] + near[1]) + (near[2] + near[3])
    all_ours[rank, near_rows:, :] = ours[near_rows:, :]
    all_shares[rank] = share[rank]
    second = [
        push(all_ours.at[rank], all_ours.at[rank], sems.at[1], k, place)
        for k, place in enumerate(places)
    ]
    for copy in second:
        copy.start()
    for copy in shares + second:
        copy.wait()
    total, part = all_ours[0], all_shares[0]
    for index in range(1, owners):
        total += all_ours[index]
        part += all_shares[index]
    out[...] = total
    share_out[...] = part


def small_sums(ours, share, seqs):
    owners = share.shape[0]
    rows, feats = ours.shape
    return pl.pallas_call(
        functools.partial(small_kernel, seqs, owners),
        in_specs=[VMEM, VMEM],
        out_specs=[VMEM, VMEM],
        out_shape=[
            jax.ShapeDtypeStruct(ours.shape, F32),
            jax.ShapeDtypeStruct(share.shape[1:], F32),
        ],
        scratch_shapes=[
            pltpu.VMEM((RING, 8, feats), F32),
            pltpu.VMEM((owners,) + ours.shape, F32),
            pltpu.VMEM(share.shape, F32),
            pltpu.SemaphoreType.DMA((2, 3)),
            pltpu.SemaphoreType.DMA((2, 2, owners - 1)),
        ],
        compiler_params=params(40, 4),
        cost_estimate=cost(12),
        name="small_sums",
    )(ours, share)


def mlp_kernel(mlp_in, cot, up, down, bias, act_out, grad_out, sum_out):
    lin = dot(mlp_in[...], up[...]) + bias[...]
    grad_act = dot(cot[...], down[...])
    cdf = normal_cdf(lin)
    act_out[...] = (lin * cdf).astype(BF)
    grad = (grad_act * gelu_slope(lin, cdf)).astype(BF)
    grad_out[...] = grad

    @pl.when(pl.program_id(1) == 0)
    def _():
        sum_out[...] = jnp.zeros_like(sum_out)

    sum_out[...] += jnp.sum(grad.astype(F32), axis=0, keepdims=True)


def mlp(mlp_in, cot, up, down, bias):
    rows, feats = mlp_in.shape
    width = up.shape[1]
    tile, cols = min(256, rows), 512
    return pl.pallas_call(
        mlp_kernel,
        grid=(width // cols, rows // tile),
        in_specs=[
            pl.BlockSpec((tile, feats), lambda n, r: (r, 0)),
            pl.BlockSpec((tile, feats), lambda n, r: (r, 0)),
            pl.BlockSpec((feats, cols), lambda n, r: (0, n)),
            pl.BlockSpec((feats, cols), lambda n, r: (0, n)),
            pl.BlockSpec((1, cols), lambda n, r: (0, n)),
        ],
        out_specs=[
            pl.BlockSpec((tile, cols), lambda n, r: (r, n)),
            pl.BlockSpec((tile, cols), lambda n, r: (r, n)),
            pl.BlockSpec((1, cols), lambda n, r: (0, n)),
        ],
        out_shape=[
            jax.ShapeDtypeStruct((rows, width), BF),
            jax.ShapeDtypeStruct((rows, width), BF),
            jax.ShapeDtypeStruct((1, width), F32),
        ],
        compiler_params=params(48),
        cost_estimate=cost(25),
        name="mlp",
    )(mlp_in, cot, up, down, bias)


def turn_back_kernel(dkv, tables, dk_out, sum_out):
    tabs = (tables[0], tables[1], tables[2])
    for head in range(dk_out.shape[1] // HEAD_DIM):
        cols = slice(head * HEAD_DIM, (head + 1) * HEAD_DIM)
        dk_out[:, cols] = turn(dkv[0, :, cols].astype(F32), tabs, -1.0).astype(BF)


def last_kernel(
    hist, streams, attn, mix, pre, gain, w1, w2, grad_out, gain_out, w1_out, w2_out,
    normed, grad_mix, grad_normed, gain_sum,
):
    depth, rows, feats = hist.shape
    step_index = pl.program_id(0)

    @pl.when(step_index == 0)
    def _():
        gain_sum[...] = jnp.zeros_like(gain_sum)
        w1_out[...] = jnp.zeros_like(w1_out)
        w2_out[...] = jnp.zeros_like(w2_out)

    def reduce(part):
        layers = [hist[j, part, :].astype(F32) for j in range(depth)]
        latest = layers[depth - 1]
        scale = lax.rsqrt(mean_last(latest * latest) + RMS_EPSILON)
        normed[part, :] = (latest * scale * gain[...]).astype(BF)
        for m in range(STREAMS):
            grads = (attn[part, :] if m == STREAMS - 1 else streams[m, part, :]).astype(F32)
            for j in range(depth):
                at = m * depth + j
                grad_mix[part, at : at + 1] = jnp.sum(grads * layers[j], axis=-1, keepdims=True)

    rows_loop(rows, 16, reduce)
    pre_value = pre[...]
    cdf = normal_cdf(pre_value)
    grads = grad_mix[...]
    w2_out[...] += dot(pre_value * cdf, grads, TN, EXACT)
    grad_act = dot(grads, w2[...], NT, EXACT)
    grad_pre = (grad_act * gelu_slope(pre_value, cdf)).astype(BF)
    w1_out[...] += dot(grad_pre, normed[...], TN)
    grad_normed[...] = dot(grad_pre, w1[...], NT)

    def write(part):
        layers = [hist[depth - 1, part, :].astype(F32)]
        latest = layers[0]
        scale = lax.rsqrt(mean_last(latest * latest) + RMS_EPSILON)
        value = grad_normed[part, :]
        gain_sum[...] += fold(value * latest * scale)
        value = value * gain[...]
        back = scale * value - latest * (scale * scale * scale * mean_last(latest * value))
        weight = mix[part, :]
        grads = [streams[m, part, :].astype(F32) for m in range(STREAMS - 1)]
        grads.append(attn[part, :].astype(F32))
        for j in range(depth):
            total = weight[:, j : j + 1] * grads[0]
            for m in range(1, STREAMS):
                at = m * depth + j
                total = total + weight[:, at : at + 1] * grads[m]
            if j == depth - 1:
                total = total + (grads[0] + grads[1] + grads[2] + grads[3]) + back
            grad_out[j, part, :] = total

    rows_loop(rows, 16, write)

    @pl.when(step_index == pl.num_programs(0) - 1)
    def _():
        gain_out[...] = jnp.sum(gain_sum[...], axis=0, keepdims=True)


def last(hist, streams, attn, mix, pre, gain, w1, w2):
    depth, rows, feats = hist.shape
    hidden = w1.shape[1]
    tile = min(64, rows)
    full = lambda shape: pl.BlockSpec(shape, lambda i: (0,) * len(shape))
    return pl.pallas_call(
        last_kernel,
        grid=(rows // tile,),
        in_specs=[
            pl.BlockSpec((depth, tile, feats), lambda i: (0, i, 0)),
            pl.BlockSpec((3, tile, feats), lambda i: (0, i, 0)),
            pl.BlockSpec((tile, feats), lambda i: (i, 0)),
            pl.BlockSpec((tile, STREAMS * depth), lambda i: (i, 0)),
            pl.BlockSpec((tile, hidden), lambda i: (i, 0)),
            full((1, feats)),
            full(w1.shape),
            full(w2.shape),
        ],
        out_specs=[
            pl.BlockSpec((depth, tile, feats), lambda i: (0, i, 0)),
            full((1, feats)),
            full((hidden, feats)),
            full(w2.shape),
        ],
        out_shape=[
            jax.ShapeDtypeStruct((depth, rows, feats), F32),
            jax.ShapeDtypeStruct((1, feats), F32),
            jax.ShapeDtypeStruct((hidden, feats), F32),
            jax.ShapeDtypeStruct(w2.shape, F32),
        ],
        scratch_shapes=[
            pltpu.VMEM((tile, feats), BF),
            pltpu.VMEM((tile, STREAMS * depth), F32),
            pltpu.VMEM((tile, feats), F32),
            pltpu.VMEM((8, feats), F32),
        ],
        compiler_params=params(40),
        cost_estimate=cost(30),
        name="last",
    )(hist, streams, attn, mix, pre, gain.reshape(1, feats), w1, w2)


def turn_back(dkv, tables):
    _, rows, width = dkv.shape
    return pl.pallas_call(
        lambda d, t, o: turn_back_kernel(d, t, o, None),
        grid=(1,),
        in_specs=[
            pl.BlockSpec((1, rows, width), lambda i: (0, 0, 0)),
            pl.BlockSpec(tables.shape, lambda i: (0, 0, 0)),
        ],
        out_specs=pl.BlockSpec((rows, width), lambda i: (0, 0)),
        out_shape=jax.ShapeDtypeStruct((rows, width), BF),
        compiler_params=params(40),
        cost_estimate=cost(3),
        name="turn_back",
    )(dkv, tables)


def row_product(left, right):
    return dot(left, right, TN).astype(BF)


def shards(
    history,
    positions,
    lengths,
    cotangent,
    mix_gain,
    mix_w1,
    mix_w2,
    ln_gain,
    ln_bias,
    qkv_weight,
    qkv_bias,
    out_weight,
    out_bias,
    up_weight,
    up_bias,
    down_weight,
    down_bias,
):
    depth, slots, block_len, feats = history.shape
    rows = slots * block_len
    width = qkv_weight.shape[2]
    heads = width // HEAD_DIM
    owners = ("dp", "seq")
    layers = history.reshape(depth, rows, feats)

    seqs = lax.axis_size("seq")
    count = lax.axis_size("dp") * seqs
    tie = lax.optimization_barrier
    gather = functools.partial(lax.all_gather, axis_name=owners, axis=0)
    w_kv = gather(jnp.concatenate([qkv_weight[1], qkv_weight[2]], axis=1), tiled=True)
    w_q = gather(qkv_weight[0], tiled=True)

    offset = lax.axis_index("seq") * block_len
    query_place = offset + jnp.arange(block_len, dtype=jnp.int32)
    valid = (query_place[None, :] < lengths[:, None]).reshape(rows, 1)
    cot = jnp.where(valid, cotangent.reshape(rows, feats), jnp.zeros((), BF))
    scalars = jnp.concatenate([lengths, offset[None].astype(jnp.int32)])
    tables = rotary_tables(positions.reshape(rows))

    normed, resid, mix, pre, w_mix, ring_out, ring_qkv = front(
        layers, mix_gain, mix_w1, mix_w2, ln_gain, ln_bias, out_weight,
        qkv_weight.reshape(-1, width), seqs, count
    )
    w_out_all = gather(ring_out)
    kv = project(normed, w_kv, qkv_bias[1:], tables, 1)
    kv, up_weight, down_weight = tie((kv, up_weight, down_weight))
    w_up, w_down = gather(up_weight, tiled=True), gather(down_weight, tiled=True)
    q, kv_all = share(normed, w_q, qkv_bias[:1], tables, kv, seqs)
    kv_all = kv_all.reshape(seqs, 2, slots, block_len, width)
    attn_vals = attend(scalars, q, kv_all, heads).reshape(rows, width)
    attn_vals, ring_qkv = tie((attn_vals, ring_qkv))
    w_qkv = gather(ring_qkv.reshape((RING,) + qkv_weight.shape))
    hidden, mlp_in = attn_out(
        attn_vals, w_out_all, resid, out_bias[None, :], ln_gain[3:4], ln_bias[3:4]
    )
    w_out = lax.dynamic_index_in_dim(
        w_out_all, lax.axis_index("tensor"), 1, keepdims=False
    ).reshape(feats, width)
    up_act, grad_up, grad_up_bias = mlp(mlp_in, cot, w_up, w_down, up_bias[None, :])
    scatter = functools.partial(
        lax.psum_scatter, axis_name=owners, scatter_dimension=0, tiled=True
    )
    grad_attn, small_mlp, out_rows, grad_upw, grad_down = mlp_back(
        grad_up, w_up, up_act, w_down, hidden, cot, mlp_in, ln_gain[3:4], down_bias[None, :]
    )
    grad_vals = dot(grad_attn, w_out).astype(BF)
    dq, dkv = attend_back(scalars, q, kv_all, grad_vals, tables, heads)
    w_qkv, out_rows, dkv = tie((w_qkv, out_rows, dkv))
    dkv_own = lax.psum_scatter(dkv, "seq", scatter_dimension=0).reshape(2, rows, width)
    layer_out = spread_rows(out_rows)
    layer_out, dkv_own, grad_down, grad_upw = tie((layer_out, dkv_own, grad_down, grad_upw))
    shard_down, shard_up = scatter(grad_down), scatter(grad_upw)
    grad_lin = jnp.stack([dq.reshape(rows, width), turn_back(dkv_own, tables), dkv_own[1]])
    grad_owqkv, grad_lin = tie((weight_grads(normed, grad_attn, grad_lin, attn_vals), grad_lin))
    shard_all = scatter(grad_owqkv)
    grads, small_qkv = streams_back(grad_lin, w_qkv, layers, mix, ln_gain)
    shard_down, shard_up, shard_all, grads = tie((shard_down, shard_up, shard_all, grads))
    shard_down, shard_up, shard_all = (
        shard_down.astype(F32), shard_up.astype(F32), shard_all.astype(F32)
    )
    shard_qkv = jnp.stack([shard_all[:, i * width : (i + 1) * width] for i in range(3)])
    shard_out = shard_all[:, 3 * width :]
    grad_layers, grad_gain, grad_w1, grad_w2 = last(
        layers, grads, grad_attn, mix, pre, mix_gain, w_mix, mix_w2
    )
    grad_history = grad_layers.reshape(depth, slots, block_len, feats)
    hidden_count = mix_w1.shape[1]
    w1_share = grad_w1.reshape(hidden_count, count, feats // count).transpose(1, 0, 2)

    def as_row(values):
        flat = values.reshape(1, -1)
        return jnp.pad(flat, ((0, 0), (0, feats - flat.shape[1])))

    grad_qkv_bias = jnp.sum(grad_lin.astype(F32), axis=1)
    ours = jnp.concatenate(
        [small_mlp, jnp.zeros((5, feats), F32), small_qkv.reshape(6, feats)]
        + [
            as_row(values)
            for values in (
                grad_gain, grad_w2, grad_qkv_bias, grad_up_bias, jnp.sum(cot.astype(F32), axis=0)
            )
        ]
        + [jnp.zeros((5, feats), F32)],
        axis=0,
    )
    summed, shard_w1 = small_sums(ours, w1_share.reshape(count, -1, 128), seqs)
    return (
        layer_out.reshape(slots, block_len, feats),
        grad_history,
        summed[14],
        shard_w1.reshape(hidden_count, feats // count).T,
        summed[15, : grad_w2.size].reshape(grad_w2.shape),
        jnp.concatenate([summed[8:11], summed[0:1]], axis=0),
        jnp.concatenate([summed[11:14], summed[1:2]], axis=0),
        shard_qkv,
        summed[16, : grad_qkv_bias.size].reshape(grad_qkv_bias.shape),
        shard_out,
        summed[2],
        shard_up,
        summed[17, : up_bias.size],
        shard_down,
        summed[18],
    )


def solution(mesh):
    in_specs = (
        P(None, "dp", "seq", None),
        P("dp", "seq"),
        P("dp"),
        P("dp", "seq", None),
        P(),
        P(("dp", "seq"), None),
        P(),
        P(),
        P(),
        P(None, ("dp", "seq"), "tensor"),
        P(None, "tensor"),
        P(("dp", "seq"), "tensor"),
        P(),
        P(("dp", "seq"), "tensor"),
        P("tensor"),
        P(("dp", "seq"), "tensor"),
        P(),
    )
    out_specs = (
        P("dp", "seq", None),
        P(None, "dp", "seq", None),
        P(),
        P(("dp", "seq"), None),
        P(),
        P(),
        P(),
        P(None, ("dp", "seq"), "tensor"),
        P(None, "tensor"),
        P(("dp", "seq"), "tensor"),
        P(),
        P(("dp", "seq"), "tensor"),
        P("tensor"),
        P(("dp", "seq"), "tensor"),
        P(),
    )
    return jax.shard_map(shards, mesh=mesh, in_specs=in_specs, out_specs=out_specs, check_vma=False)
```

```python
import functools
import math

import jax
import jax.numpy as jnp
from jax import lax
from jax.experimental import pallas as pl
from jax.experimental.pallas import tpu as pltpu
from jax.sharding import PartitionSpec as P

HEAD_DIM = 128
ROT = 32
STREAMS = 4
EXACT = lax.Precision.HIGHEST
RMS_EPSILON = 1e-06
NORM_EPSILON = 1e-05
BF = jnp.bfloat16
F32 = jnp.float32
MESH = pl.DeviceIdType.MESH
ANY = pl.BlockSpec(memory_space=pl.ANY)
VMEM = pl.BlockSpec(memory_space=pltpu.VMEM)
RING = 4
NN = (((1,), (0,)), ((), ()))
NT = (((1,), (1,)), ((), ()))
TN = (((0,), (0,)), ((), ()))


def dot(left, right, dims=NN, precision=None):
    return lax.dot_general(left, right, dims, precision=precision, preferred_element_type=F32)


def normal_cdf(values):
    return 0.5 * (1.0 + lax.erf(values * math.sqrt(0.5)))


def gelu_slope(values, cdf):
    return cdf + values * (jnp.exp(-0.5 * values * values) * (1.0 / math.sqrt(2.0 * math.pi)))


def mean_last(values):
    return jnp.mean(values, axis=-1, keepdims=True)


def rows_loop(total, step, body):
    def one(index, carry):
        body(pl.ds(pl.multiple_of(index * step, step), step))
        return carry

    lax.fori_loop(0, total // step, one, 0)


def params(limit_mib, collective_id=None):
    if collective_id is None:
        return pltpu.CompilerParams(vmem_limit_bytes=limit_mib << 20)
    return pltpu.CompilerParams(
        vmem_limit_bytes=limit_mib << 20, collective_id=collective_id, has_side_effects=True
    )


def cost(micros):
    return pl.CostEstimate(flops=0, bytes_accessed=int(micros * 3.0e6), transcendentals=0)


def owner_places(seqs, owners):
    rank = lax.axis_index("dp") * seqs + lax.axis_index("seq")
    peers = [lax.rem(rank + k, owners) for k in range(1, owners)]
    return rank, peers, [{"dp": lax.div(p, seqs), "seq": lax.rem(p, seqs)} for p in peers]


def push(source, target, sems, index, place):
    return pltpu.make_async_remote_copy(
        src_ref=source,
        dst_ref=target,
        send_sem=sems.at[0, index],
        recv_sem=sems.at[1, index],
        device_id=place,
        device_id_type=MESH,
    )


def enter(places):
    gate = pltpu.get_barrier_semaphore()
    for place in places:
        pl.semaphore_signal(gate, inc=1, device_id=place, device_id_type=MESH)
    pl.semaphore_wait(gate, len(places))


def front_kernel(
    seqs, owners,
    hist, gain, w1, w2, lg, lb, normed_out, resid_out, mix_out, pre_out, w1_out,
    scratch, w1_all, w1_sems,
):
    depth, rows, _ = hist.shape
    index = pl.program_id(0)
    rank, _, places = owner_places(seqs, owners)
    w1_copies = [push(w1, w1_all.at[rank], w1_sems, k, p) for k, p in enumerate(places)]

    @pl.when(index == 0)
    def _():
        enter(places)
        for copy in w1_copies:
            copy.start()
        w1_all[rank] = w1[...]
        for copy in w1_copies:
            copy.wait()
        w1_out[...] = w1_all[...].reshape(w1_out.shape)

    def rms(part):
        wide = hist[depth - 1, part, :].astype(F32)
        scale = lax.rsqrt(mean_last(wide * wide) + RMS_EPSILON)
        scratch[part, :] = (wide * scale * gain[...]).astype(BF)

    rows_loop(rows, 16, rms)
    pre = dot(scratch[...], w1_out[...])
    pre_out[...] = pre
    mix_out[...] = dot(pre * normal_cdf(pre), w2[...], precision=EXACT)

    def combine(part):
        layers = [hist[j, part, :].astype(F32) for j in range(depth)]
        mix = mix_out[part, :]
        for m in range(STREAMS):
            running = layers[depth - 1]
            for j in range(depth):
                running = running + mix[:, m * depth + j : m * depth + j + 1] * layers[j]
            if m == STREAMS - 1:
                resid_out[part, :] = running
            else:
                centred = running - mean_last(running)
                inverse = lax.rsqrt(mean_last(centred * centred) + NORM_EPSILON)
                normed = centred * inverse * lg[m : m + 1, :] + lb[m : m + 1, :]
                normed_out[m, part, :] = normed.astype(BF)

    rows_loop(rows, 16, combine)


def front(layers, gain, w1, w2, lg, lb, seqs, owners):
    depth, rows, feats = layers.shape
    tile = min(128, rows)
    hidden = w1.shape[1]
    full = lambda shape: pl.BlockSpec(shape, lambda i: (0,) * len(shape))
    return pl.pallas_call(
        functools.partial(front_kernel, seqs, owners),
        grid=(rows // tile,),
        in_specs=[
            pl.BlockSpec((depth, tile, feats), lambda i: (0, i, 0)),
            full((1, feats)),
            full(w1.shape),
            full(w2.shape),
            full(lg.shape),
            full(lb.shape),
        ],
        out_specs=[
            pl.BlockSpec((3, tile, feats), lambda i: (0, i, 0)),
            pl.BlockSpec((tile, feats), lambda i: (i, 0)),
            pl.BlockSpec((tile, STREAMS * depth), lambda i: (i, 0)),
            pl.BlockSpec((tile, hidden), lambda i: (i, 0)),
            full((feats, hidden)),
        ],
        out_shape=[
            jax.ShapeDtypeStruct((3, rows, feats), BF),
            jax.ShapeDtypeStruct((rows, feats), F32),
            jax.ShapeDtypeStruct((rows, STREAMS * depth), F32),
            jax.ShapeDtypeStruct((rows, hidden), F32),
            jax.ShapeDtypeStruct((feats, hidden), BF),
        ],
        scratch_shapes=[
            pltpu.VMEM((tile, feats), BF),
            pltpu.VMEM((owners,) + w1.shape, BF),
            pltpu.SemaphoreType.DMA((2, owners - 1)),
        ],
        compiler_params=params(48, 5),
        cost_estimate=cost(45),
        name="front",
    )(layers, gain.reshape(1, feats), w1, w2, lg, lb)


def turn(values, tables, sign):
    cosines, low, high = tables
    return values * cosines + sign * (
        pltpu.roll(values, HEAD_DIM - ROT // 2, 1) * low + pltpu.roll(values, ROT // 2, 1) * high
    )


def rotary_tables(positions):
    exponents = jnp.arange(0, ROT, 2).astype(F32) / ROT
    inverse = jnp.power(10000.0, -exponents)
    phases = positions.astype(F32)[:, None] * inverse[None, :]
    cosines, sines = jnp.cos(phases), jnp.sin(phases)
    rows, half = phases.shape
    ones = jnp.ones((rows, HEAD_DIM - 2 * half), F32)
    none = jnp.zeros((rows, HEAD_DIM - 2 * half), F32)
    zero = jnp.zeros((rows, half), F32)
    return jnp.stack(
        [
            jnp.concatenate([cosines, cosines, ones], axis=1),
            jnp.concatenate([-sines, zero, none], axis=1),
            jnp.concatenate([zero, sines, none], axis=1),
        ]
    )


def proj_kernel(first, lhs, weight, bias, tables, out):
    branch = pl.program_id(0) + first
    value = dot(lhs[0], weight[...]) + bias[0]

    @pl.when(branch < 2)
    def _():
        tabs = (tables[0], tables[1], tables[2])
        for head in range(value.shape[1] // HEAD_DIM):
            cols = slice(head * HEAD_DIM, (head + 1) * HEAD_DIM)
            out[0, :, cols] = turn(value[:, cols], tabs, 1.0).astype(BF)

    @pl.when(branch >= 2)
    def _():
        out[0] = value.astype(BF)


def project(normed, weight, bias, tables, first):
    _, rows, feats = normed.shape
    count, width = bias.shape
    tile = min(256, rows)
    return pl.pallas_call(
        functools.partial(proj_kernel, first),
        grid=(count, rows // tile),
        in_specs=[
            pl.BlockSpec((1, tile, feats), lambda b, r: (b + first, r, 0)),
            pl.BlockSpec((feats, width), lambda b, r: (0, b)),
            pl.BlockSpec((1, 1, width), lambda b, r: (b, 0, 0)),
            pl.BlockSpec((3, tile, HEAD_DIM), lambda b, r: (0, r, 0)),
        ],
        out_specs=pl.BlockSpec((1, tile, width), lambda b, r: (b, r, 0)),
        out_shape=jax.ShapeDtypeStruct((count, rows, width), BF),
        compiler_params=params(40),
        cost_estimate=cost(4 * count),
        name="project",
    )(normed, weight, bias.reshape(count, 1, width), tables)


def share_kernel(
    kv, shard_out, shard_qkv, kv_out, ring_out, ring_qkv, sems, ring_sems, own_sems
):
    seqs = kv_out.shape[0]
    me = lax.axis_index("seq")
    ring = Ring(16)
    places = [{"seq": lax.rem(me + k, seqs)} for k in range(1, seqs)]
    local = [
        pltpu.make_async_copy(kv, kv_out.at[me], own_sems.at[0]),
        pltpu.make_async_copy(shard_out, ring_out.at[ring.me], own_sems.at[1]),
        pltpu.make_async_copy(shard_qkv, ring_qkv.at[ring.me], own_sems.at[2]),
    ]
    for copy in local:
        copy.start()
    enter(places + [{"tensor": ring.left}, {"tensor": ring.right}])
    copies = [push(kv, kv_out.at[me], sems, k, place) for k, place in enumerate(places)]
    spreads = [
        Spread(ring, slots, ring_sems.at[i], 0, source)
        for i, (slots, source) in enumerate(((ring_out, shard_out), (ring_qkv, shard_qkv)))
    ]
    for copy in copies:
        copy.start()
    for spread in spreads:
        spread.begin()

    for spread in spreads:
        spread.relay()
    for copy in copies:
        copy.wait()
    for spread in spreads:
        spread.arrive()
        spread.finish()
    for copy in local:
        copy.wait()


def share(kv, shard_out, shard_qkv, seqs):
    return pl.pallas_call(
        share_kernel,
        in_specs=[ANY, ANY, ANY],
        out_specs=[ANY, ANY, ANY],
        out_shape=[
            jax.ShapeDtypeStruct((seqs,) + kv.shape, BF),
            jax.ShapeDtypeStruct((RING,) + shard_out.shape, BF),
            jax.ShapeDtypeStruct((RING,) + shard_qkv.shape, BF),
        ],
        scratch_shapes=[
            pltpu.SemaphoreType.DMA((2, seqs - 1)),
            pltpu.SemaphoreType.DMA((2, 2, 4)),
            pltpu.SemaphoreType.DMA((3,)),
        ],
        compiler_params=params(48, 6),
        cost_estimate=cost(72),
        name="share",
    )(kv, shard_out, shard_qkv)


def attend_kernel(scalars, q, k, v, out):
    keys = k[...].reshape(-1, HEAD_DIM)
    values = v[...].reshape(-1, HEAD_DIM)
    length = scalars[pl.program_id(0)]
    offset = scalars[pl.num_programs(0)]
    scores = dot(q[0], keys, NT) * (1.0 / math.sqrt(HEAD_DIM))
    key_place = lax.broadcasted_iota(jnp.int32, scores.shape, 1)
    query_place = lax.broadcasted_iota(jnp.int32, scores.shape, 0) + offset
    scores = jnp.where((key_place <= query_place) & (key_place < length), scores, -1e30)
    weights = jnp.exp(scores - jnp.max(scores, axis=-1, keepdims=True))
    total = jnp.sum(weights, axis=-1, keepdims=True)
    probs = (weights * (1.0 / total)).astype(BF)
    out[0] = dot(probs, values).astype(BF)


def attend(scalars, q, kv, heads):
    seqs, _, slots, length, width = kv.shape
    block = (1, length, HEAD_DIM)
    return pl.pallas_call(
        attend_kernel,
        grid_spec=pltpu.PrefetchScalarGridSpec(
            num_scalar_prefetch=1,
            grid=(slots, heads),
            in_specs=[
                pl.BlockSpec(block, lambda s, h, _: (s, 0, h)),
                pl.BlockSpec((seqs, 1, 1, length, HEAD_DIM), lambda s, h, _: (0, 0, s, 0, h)),
                pl.BlockSpec((seqs, 1, 1, length, HEAD_DIM), lambda s, h, _: (0, 1, s, 0, h)),
            ],
            out_specs=pl.BlockSpec(block, lambda s, h, _: (s, 0, h)),
        ),
        out_shape=jax.ShapeDtypeStruct((slots, length, width), BF),
        compiler_params=params(40),
        cost_estimate=cost(15),
        name="attend",
    )(scalars, q.reshape(slots, length, width), kv, kv)


def attend_back_kernel(scalars, q, k, v, g, tables, dq_out, dkv_out):
    seqs = k.shape[0]
    scaling = 1.0 / math.sqrt(HEAD_DIM)
    keys = k[...].reshape(-1, HEAD_DIM)
    values = v[...].reshape(-1, HEAD_DIM)
    length = scalars[pl.program_id(0)]
    offset = scalars[pl.num_programs(0)]
    queries, grads = q[0], g[0]
    scores = dot(keys, queries, NT) * scaling
    key_place = lax.broadcasted_iota(jnp.int32, scores.shape, 0)
    query_place = lax.broadcasted_iota(jnp.int32, scores.shape, 1) + offset
    scores = jnp.where((key_place <= query_place) & (key_place < length), scores, -1e30)
    weights = jnp.exp(scores - jnp.max(scores, axis=0, keepdims=True))
    probs = weights * (1.0 / jnp.sum(weights, axis=0, keepdims=True))
    grad_probs = dot(values, grads, NT)
    mixed = jnp.sum(probs * grad_probs, axis=0, keepdims=True)
    grad_scores = (probs * (grad_probs - mixed)).astype(BF)
    grad_values = dot(probs.astype(BF), grads)
    grad_keys = dot(grad_scores, queries) * scaling
    shape = (seqs, -1, HEAD_DIM)
    dkv_out[:, 0, 0] = grad_keys.astype(BF).reshape(shape)
    dkv_out[:, 1, 0] = grad_values.astype(BF).reshape(shape)
    grad_queries = dot(grad_scores, keys, TN) * scaling
    tabs = (tables[0], tables[1], tables[2])
    dq_out[0] = turn(grad_queries, tabs, -1.0).astype(BF)


def attend_back(scalars, q, kv, g, tables, heads):
    seqs, _, slots, length, width = kv.shape
    block = (1, length, HEAD_DIM)
    own = pl.BlockSpec(block, lambda s, h, _: (s, 0, h))
    return pl.pallas_call(
        attend_back_kernel,
        grid_spec=pltpu.PrefetchScalarGridSpec(
            num_scalar_prefetch=1,
            grid=(slots, heads),
            in_specs=[
                own,
                pl.BlockSpec((seqs, 1, 1, length, HEAD_DIM), lambda s, h, _: (0, 0, s, 0, h)),
                pl.BlockSpec((seqs, 1, 1, length, HEAD_DIM), lambda s, h, _: (0, 1, s, 0, h)),
                own,
                pl.BlockSpec((3, length, HEAD_DIM), lambda s, h, _: (0, s, 0)),
            ],
            out_specs=[
                own,
                pl.BlockSpec((seqs, 2, 1, length, HEAD_DIM), lambda s, h, _: (0, 0, s, 0, h)),
            ],
        ),
        out_shape=[
            jax.ShapeDtypeStruct((slots, length, width), BF),
            jax.ShapeDtypeStruct((seqs, 2, slots, length, width), BF),
        ],
        compiler_params=params(48),
        cost_estimate=cost(25),
        name="attend_back",
    )(scalars, q.reshape(slots, length, width), kv, kv, g.reshape(slots, length, width), tables)


class Ring:
    def __init__(self, chunk):
        me = lax.axis_index("tensor")
        self.chunk, self.half = chunk, chunk // 2
        self.me = me
        self.right = lax.rem(me + 1, RING)
        self.left = lax.rem(me + RING - 1, RING)
        self.far = lax.rem(me + 2, RING)

    def at(self, index, shift=0):
        return pl.multiple_of(index * self.chunk + shift, self.half)

    def barrier(self):
        gate = pltpu.get_barrier_semaphore()
        for near in (self.left, self.right):
            pl.semaphore_signal(gate, inc=1, device_id={"tensor": near}, device_id_type=MESH)
        pl.semaphore_wait(gate, 2)


def remote(source, target, sems, index, device):
    return pltpu.make_async_remote_copy(
        src_ref=source,
        dst_ref=target,
        send_sem=sems.at[0, index],
        recv_sem=sems.at[1, index],
        device_id={"tensor": device},
        device_id_type=MESH,
    )


def product(lhs, rhs, start, count, write, step=512):
    total = rhs.shape[0]

    def one(cols):
        write(cols, dot(lhs[pl.ds(start, count), :], rhs[cols, :], NT))

    rows_loop(total, min(step, total), one)


class Scatter:
    def __init__(self, ring, lhs, rhs, far, near, far_in, near_in, sems):
        self.ring, self.lhs, self.rhs = ring, lhs, rhs
        self.far, self.near, self.far_in, self.near_in = far, near, far_in, near_in
        half = ring.half
        up, down = pl.ds(0, half), pl.ds(half, half)
        self.copies = [
            remote(far.at[0], far_in.at[0], sems, 0, ring.right),
            remote(far.at[1], far_in.at[1], sems, 1, ring.left),
            remote(near.at[0, down], near_in.at[0, down], sems, 2, ring.right),
            remote(near.at[1, up], near_in.at[1, up], sems, 3, ring.left),
            remote(near.at[0, up], near_in.at[0, up], sems, 4, ring.right),
            remote(near.at[1, down], near_in.at[1, down], sems, 5, ring.left),
        ]

    def begin(self):
        ring, half = self.ring, self.ring.half

        def far_half(which):
            def write(cols, value):
                self.far[which, :, cols] = value.astype(BF)

            product(self.lhs, self.rhs, ring.at(ring.far, which * half), half, write)
            self.copies[which].start()

        def near_half(which, device, part, copy):
            def write(cols, value):
                self.near[which, pl.ds(part * half, half), cols] = value.astype(BF)

            product(self.lhs, self.rhs, ring.at(device, part * half), half, write)
            self.copies[copy].start()

        far_half(0)
        far_half(1)
        near_half(0, ring.right, 1, 2)
        near_half(1, ring.left, 0, 3)

    def relay(self):
        ring, half = self.ring, self.ring.half

        def add_half(which, device, part, copy):
            self.copies[which].wait_recv()

            def write(cols, value):
                arrived = self.far_in[which, :, cols].astype(F32)
                self.near[which, pl.ds(part * half, half), cols] = (value + arrived).astype(BF)

            product(self.lhs, self.rhs, ring.at(device, part * half), half, write)
            self.copies[copy].start()

        add_half(0, ring.right, 0, 4)
        add_half(1, ring.left, 1, 5)

    def arrive(self):
        for copy in self.copies[2:]:
            copy.wait_recv()

    def finish(self):
        for copy in self.copies:
            copy.wait_send()


class Gather:
    def __init__(self, ring, own, out, sems, base, local_sem):
        half = ring.half

        def rows(index, shift=0, count=ring.chunk):
            return out.at[pl.ds(ring.at(index, shift), count), :]

        mine = rows(ring.me)
        self.local = pltpu.make_async_copy(own, mine, local_sem)
        self.first = [
            remote(own, mine, sems, base, ring.right),
            remote(own, mine, sems, base + 1, ring.left),
        ]
        up, down = rows(ring.left, 0, half), rows(ring.right, half, half)
        self.second = [
            remote(up, up, sems, base + 2, ring.right),
            remote(down, down, sems, base + 3, ring.left),
        ]

    def begin(self):
        for copy in self.first:
            copy.start()
        self.local.start()

    def relay(self):
        for arrived, onward in zip(self.first, self.second):
            arrived.wait_recv()
            onward.start()

    def finish(self):
        for copy in self.second:
            copy.wait_recv()
        for copy in self.first + self.second:
            copy.wait_send()
        self.local.wait()


def scatter_scratch(chunk, feats, count=1):
    half = chunk // 2
    lead = () if count == 1 else (count,)
    return [
        pltpu.VMEM(lead + (2, half, feats), BF),
        pltpu.VMEM(lead + (2, chunk, feats), BF),
        pltpu.VMEM(lead + (2, half, feats), BF),
        pltpu.VMEM(lead + (2, chunk, feats), BF),
    ]


def own_sum(scatter, total):
    ring = scatter.ring

    def write(cols, value):
        total[:, cols] = value

    product(scatter.lhs, scatter.rhs, ring.at(ring.me), ring.chunk, write)


def whole_sum(scatter, total, part):
    near = scatter.near_in
    return total[part, :] + near[0, part, :].astype(F32) + near[1, part, :].astype(F32)


def weight_copies(weight, target, sems, index):
    count = weight.shape[-2]

    def one(owner):
        source = weight.at[owner] if index is None else weight.at[owner, :, index]
        return pltpu.make_async_copy(
            source,
            target.at[:, pl.ds(pl.multiple_of(owner * count, count), count), :],
            sems.at[owner],
        )

    def every(act):
        def step(owner, carry):
            act(one(owner))
            return carry

        lax.fori_loop(0, weight.shape[0], step, 0)

    return every


def ring_product(slots, weight, part, total):
    def columns(cols):
        value = dot(slots[0, part, :], weight[0, cols, :], NT)
        for z in range(1, RING):
            value += dot(slots[z, part, :], weight[z, cols, :], NT)
        total[:, cols] = value

    rows_loop(total.shape[1], 512, columns)


def spread_kernel(vals, out, sems, own_sem):
    ring = Ring(16)
    local = pltpu.make_async_copy(vals, out.at[ring.me], own_sem)
    local.start()
    ring.barrier()
    spread = Spread(ring, out, sems, 0, vals)
    spread.begin()
    spread.relay()
    spread.arrive()
    spread.finish()
    local.wait()


def spread_vals(vals):
    return pl.pallas_call(
        spread_kernel,
        in_specs=[ANY],
        out_specs=ANY,
        out_shape=jax.ShapeDtypeStruct((RING,) + vals.shape, BF),
        scratch_shapes=[pltpu.SemaphoreType.DMA((2, 4)), pltpu.SemaphoreType.DMA],
        compiler_params=params(32, 0),
        cost_estimate=cost(70),
        name="spread_vals",
    )(vals)


def attn_out_kernel(
    slots, weight, resid, bias, lg, lb, hidden_out, mlp_out,
    weights, total, base_rows, stage, weight_sems, base_sem, stage_sems,
):
    chunk, feats = total.shape
    me = lax.axis_index("tensor")
    load = weight_copies(weight, weights, weight_sems, None)
    load(lambda copy: copy.start())
    load(lambda copy: copy.wait())

    def write_out(index, slot):
        part = pl.ds(pl.multiple_of(index * chunk, chunk), chunk)
        return pltpu.make_async_copy(stage.at[slot], mlp_out.at[part, :], stage_sems.at[slot])

    def one(index, carry):
        part = pl.ds(pl.multiple_of(index * chunk, chunk), chunk)
        fetch = pltpu.make_async_copy(resid.at[part, :], base_rows, base_sem)
        fetch.start()
        slot = lax.rem(index, 2)
        ring_product(slots, weights, part, total)
        fetch.wait()

        @pl.when(index >= 2)
        def _():
            write_out(index - 2, slot).wait()

        def norm(sub):
            value = base_rows[sub, :] + (total[sub, :] + bias[...])
            total[sub, :] = value
            centred = value - mean_last(value)
            inverse = lax.rsqrt(mean_last(centred * centred) + NORM_EPSILON)
            stage[slot, sub, :] = (centred * inverse * lg[...] + lb[...]).astype(BF)

        rows_loop(chunk, 16, norm)
        write_out(index, slot).start()

        @pl.when(index == me)
        def _():
            hidden_out[...] = total[...]

        return carry

    lax.fori_loop(0, RING, one, 0)
    for index in range(RING - 2, RING):
        write_out(index, index % 2).wait()


def attn_out(slots, weight, resid, bias, lg, lb):
    rows, feats = resid.shape
    width = slots.shape[2]
    chunk = rows // RING
    return pl.pallas_call(
        attn_out_kernel,
        in_specs=[VMEM, ANY, ANY, VMEM, VMEM, VMEM],
        out_specs=[VMEM, ANY],
        out_shape=[
            jax.ShapeDtypeStruct((chunk, feats), F32),
            jax.ShapeDtypeStruct((rows, feats), BF),
        ],
        scratch_shapes=[
            pltpu.VMEM((RING, feats, width), BF),
            pltpu.VMEM((chunk, feats), F32),
            pltpu.VMEM((chunk, feats), F32),
            pltpu.VMEM((2, chunk, feats), BF),
            pltpu.SemaphoreType.DMA((weight.shape[0],)),
            pltpu.SemaphoreType.DMA,
            pltpu.SemaphoreType.DMA((2,)),
        ],
        compiler_params=params(48),
        cost_estimate=cost(30),
        name="attn_out",
    )(slots, weight, resid, bias, lg, lb)


def norm_back(values, grads, gain):
    centred = values - mean_last(values)
    inverse = lax.rsqrt(mean_last(centred * centred) + NORM_EPSILON)
    normed = centred * inverse
    inner = grads * gain
    back = inverse * (inner - mean_last(inner) - normed * mean_last(inner * normed))
    return back, normed


def fold(values):
    rows, feats = values.shape
    return jnp.sum(values.reshape(rows // 8, 8, feats), axis=0)


def weight_product(source, rhs, out, blocks, stage, load_sems, store_sems):
    width = blocks.shape[2]
    count = source.shape[1] // width

    def load(n, slot):
        cols = pl.ds(pl.multiple_of(n * width, width), width)
        return pltpu.make_async_copy(source.at[:, cols], blocks.at[slot], load_sems.at[slot])

    def store(n, slot):
        part = pl.ds(pl.multiple_of(n * width, width), width)
        return pltpu.make_async_copy(stage.at[slot], out.at[part, :], store_sems.at[slot])

    load(0, 0).start()

    def one(n, carry):
        slot = lax.rem(n, 2)

        @pl.when(n + 1 < count)
        def _():
            load(n + 1, 1 - slot).start()

        load(n, slot).wait()

        @pl.when(n >= 2)
        def _():
            store(n - 2, slot).wait()

        def columns(cols):
            stage[slot, :, cols] = dot(blocks[slot], rhs[:, cols], TN).astype(BF)

        rows_loop(rhs.shape[1], 512, columns)
        store(n, slot).start()
        return carry

    lax.fori_loop(0, count, one, 0)
    for n in range(count - 2, count):
        store(n, n % 2).wait()


def spread_dq_kernel(
    lin, normed, grad_attn, vals, out, products,
    blocks, tiles_out, sems, own_sem, load_sems, store_sems,
):
    ring = Ring(16)
    width = lin.shape[1]
    local = pltpu.make_async_copy(lin, out.at[ring.me], own_sem)
    local.start()
    ring.barrier()
    spread = Spread(ring, out, sems, 0, lin)
    spread.begin()
    for i, (source, rhs) in enumerate(((normed.at[0], lin), (grad_attn, vals))):
        target = products.at[:, pl.ds(i * width, width)]
        weight_product(source, rhs, target, blocks, tiles_out, load_sems, store_sems)
    spread.relay()
    spread.arrive()
    spread.finish()
    local.wait()


def spread_dq(lin, normed, grad_attn, vals):
    rows, width = lin.shape
    feats = grad_attn.shape[1]
    return pl.pallas_call(
        spread_dq_kernel,
        in_specs=[VMEM, ANY, ANY, VMEM],
        out_specs=[ANY, ANY],
        out_shape=[
            jax.ShapeDtypeStruct((RING, rows, width), BF),
            jax.ShapeDtypeStruct((feats, 2 * width), BF),
        ],
        scratch_shapes=[
            pltpu.VMEM((2, rows, 256), BF),
            pltpu.VMEM((2, 256, width), BF),
            pltpu.SemaphoreType.DMA((2, 4)),
            pltpu.SemaphoreType.DMA,
            pltpu.SemaphoreType.DMA((2,)),
            pltpu.SemaphoreType.DMA((2,)),
        ],
        compiler_params=params(40, 3),
        cost_estimate=cost(70),
        name="spread_dq",
    )(lin, normed, grad_attn, vals)


class Line:
    def __init__(self, chunk):
        me = lax.axis_index("tensor")
        self.me, self.chunk = me, chunk
        self.low = me < 2
        self.outer = (me == 0) | (me == RING - 1)
        self.inner = (me == 1) | (me == RING - 2)
        self.up = jnp.where(self.low, me + 1, me - 1)
        self.down = jnp.where(self.low, lax.max(me - 1, 0), lax.min(me + 1, RING - 1))

    def at(self, number):
        index = jnp.where(self.low, number, RING - 1 - number)
        return pl.ds(pl.multiple_of(index * self.chunk, self.chunk), self.chunk)

    def barrier(self):
        gate = pltpu.get_barrier_semaphore()
        pl.semaphore_signal(gate, inc=1, device_id={"tensor": self.up}, device_id_type=MESH)

        @pl.when(self.inner)
        def _():
            pl.semaphore_signal(
                gate, inc=1, device_id={"tensor": self.down}, device_id_type=MESH
            )
            pl.semaphore_wait(gate, 2)

        @pl.when(self.outer)
        def _():
            pl.semaphore_wait(gate, 1)


class LineSum:
    def __init__(self, line, lhs, rhs, outbound, inbound, sems, base):
        self.line, self.lhs, self.rhs = line, lhs, rhs
        self.outbound, self.inbound = outbound, inbound
        copy = lambda slot, target, device: remote(
            outbound.at[slot], inbound.at[target], sems, base + target, device
        )
        self.inward = [copy(i, i, line.up) for i in range(3)]
        self.across = [copy(i, 3 + i, line.up) for i in range(2)]
        self.outward = remote(outbound.at[2], inbound.at[5], sems, base + 5, line.down)

    def partial(self, number, slot, arrived=None):
        rows = self.line.at(number)

        def write(cols, value):
            if arrived is not None:
                value = value + self.inbound[arrived, :, cols].astype(F32)
            self.outbound[slot, :, cols] = value.astype(BF)

        product(self.lhs, self.rhs, rows.start, self.line.chunk, write)

    def own(self, total):
        index = self.line.me * self.line.chunk

        def write(cols, value):
            total[:, cols] = value

        product(
            self.lhs, self.rhs, pl.multiple_of(index, self.line.chunk), self.line.chunk, write
        )

    def send_inward(self):
        for slot, copy in enumerate(self.inward):
            self.partial(3 - slot, slot)
            copy.start()

    def send_across(self, i):
        self.inward[i].wait_recv()
        self.partial(3 - i, i, i)
        self.across[i].start()

    def send_outward(self):
        self.across[0].wait_recv()
        self.partial(0, 2, 3)
        self.outward.start()

    def arrive(self):
        line = self.line

        @pl.when(line.inner)
        def _():
            self.inward[2].wait_recv()
            self.across[1].wait_recv()

        @pl.when(line.outer)
        def _():
            self.outward.wait_recv()

    def sent(self):
        line = self.line

        @pl.when(line.inner)
        def _():
            for copy in self.across + [self.outward]:
                copy.wait_send()

        @pl.when(line.outer)
        def _():
            for copy in self.inward:
                copy.wait_send()

    def clear(self):
        @pl.when(self.line.outer)
        def _():
            self.inbound[2] = jnp.zeros_like(self.inbound[2])

    def whole(self, total, part):
        last = jnp.where(self.line.outer, 5, 4)
        return (
            total[part, :]
            + self.inbound[2, part, :].astype(F32)
            + self.inbound[last, part, :].astype(F32)
        )


def mlp_back_kernel(
    lhs, rhs, acts, down, hidden, cot, mlp_in, lg, down_bias,
    grad_out, small_out, rows_out, grad_up, grad_down,
    outbound, inbound, total, cot_rows, own, sums, blocks, stage,
    sems, gather_sems, local_sems, load_sems, store_sems,
):
    chunk, feats = total.shape
    line = Line(chunk)
    mine = pl.ds(pl.multiple_of(line.me * chunk, chunk), chunk)
    fetch = pltpu.make_async_copy(cot.at[mine, :], cot_rows, local_sems.at[0])
    fetch.start()
    line.barrier()
    first = LineSum(line, lhs, rhs, outbound, inbound.at[0], sems.at[0], 0)
    second = LineSum(line, acts, down, outbound, inbound.at[1], sems.at[1], 0)
    first.clear()
    second.clear()

    @pl.when(line.outer)
    def _():
        first.send_inward()

    first.own(total)
    sums[...] = jnp.zeros_like(sums)
    weight_product(mlp_in, lhs, grad_up, blocks, stage, load_sems, store_sems)

    @pl.when(line.inner)
    def _():
        first.send_across(0)
        first.send_across(1)
        first.send_outward()

    weight_product(cot, acts, grad_down, blocks, stage, load_sems, store_sems)
    fetch.wait()
    first.arrive()

    def back(part):
        grads = first.whole(total, part)
        step, normed = norm_back(hidden[part, :], grads, lg[...])
        low = (cot_rows[part, :].astype(F32) + step).astype(BF)
        own[part, :] = low
        sums[0] += fold(grads * normed)
        sums[1] += fold(grads)
        sums[2] += fold(low.astype(F32))

    rows_loop(chunk, 16, back)
    local = pltpu.make_async_copy(own, grad_out.at[mine, :], local_sems.at[1])
    local.start()
    first.sent()

    def chunk_copy(number, index, device, source=None):
        rows = grad_out.at[line.at(number), :]
        return remote(rows if source is None else source, rows, gather_sems, index, device)

    @pl.when(line.outer)
    def _():
        onward = chunk_copy(0, 0, line.up, own)
        onward.start()
        second.send_inward()
        second.own(total)
        for number in range(1, RING):
            chunk_copy(number, 2 + number, line.up).wait_recv()
        onward.wait_send()

    @pl.when(line.inner)
    def _():
        inward = [chunk_copy(1, 1, line.up, own), chunk_copy(1, 3, line.down, own)]
        for copy in inward:
            copy.start()
        second.own(total)
        chunk_copy(0, 0, line.up).wait_recv()
        relay = chunk_copy(0, 2, line.up)
        relay.start()
        chunk_copy(2, 1, line.up).wait_recv()
        near = chunk_copy(2, 4, line.down)
        near.start()
        second.send_across(0)
        chunk_copy(3, 2, line.up).wait_recv()
        far = chunk_copy(3, 5, line.down)
        far.start()
        second.send_across(1)
        second.send_outward()
        for copy in inward + [relay, near, far]:
            copy.wait_send()

    for i in range(3):
        small_out[i : i + 1, :] = jnp.sum(sums[i], axis=0, keepdims=True)
    second.arrive()

    def add(part):
        value = hidden[part, :] + (second.whole(total, part) + down_bias[...])
        rows_out[part, :] = value.astype(BF)

    rows_loop(chunk, 16, add)
    second.sent()
    local.wait()


def mlp_back(lhs, rhs, acts, down, hidden, cot, mlp_in, lg, down_bias):
    rows, feats = cot.shape
    width = lhs.shape[1]
    chunk = rows // RING
    block = 256
    return pl.pallas_call(
        mlp_back_kernel,
        in_specs=[VMEM, VMEM, VMEM, VMEM, VMEM, ANY, ANY, VMEM, VMEM],
        out_specs=[ANY, VMEM, VMEM, ANY, ANY],
        out_shape=[
            jax.ShapeDtypeStruct((rows, feats), BF),
            jax.ShapeDtypeStruct((3, feats), F32),
            jax.ShapeDtypeStruct((chunk, feats), BF),
            jax.ShapeDtypeStruct((feats, width), BF),
            jax.ShapeDtypeStruct((feats, width), BF),
        ],
        scratch_shapes=[
            pltpu.VMEM((3, chunk, feats), BF),
            pltpu.VMEM((2, 6, chunk, feats), BF),
            pltpu.VMEM((chunk, feats), F32),
            pltpu.VMEM((chunk, feats), BF),
            pltpu.VMEM((chunk, feats), BF),
            pltpu.VMEM((3, 8, feats), F32),
            pltpu.VMEM((2, rows, block), BF),
            pltpu.VMEM((2, block, width), BF),
            pltpu.SemaphoreType.DMA((2, 2, 6)),
            pltpu.SemaphoreType.DMA((2, 6)),
            pltpu.SemaphoreType.DMA((2,)),
            pltpu.SemaphoreType.DMA((2,)),
            pltpu.SemaphoreType.DMA((2,)),
        ],
        compiler_params=params(60, 1),
        cost_estimate=cost(175),
        name="mlp_back",
    )(lhs, rhs, acts, down, hidden, cot, mlp_in, lg, down_bias)


class Spread:
    def __init__(self, ring, slots, sems, base, source):
        half = slots.shape[1] // 2
        mine = slots.at[ring.me]
        self.first = [
            remote(source, mine, sems, base, ring.right),
            remote(source, mine, sems, base + 1, ring.left),
        ]
        up = slots.at[ring.left, pl.ds(0, half), :]
        down = slots.at[ring.right, pl.ds(half, half), :]
        self.second = [
            remote(up, up, sems, base + 2, ring.right),
            remote(down, down, sems, base + 3, ring.left),
        ]

    def begin(self):
        for copy in self.first:
            copy.start()

    def relay(self):
        for arrived, onward in zip(self.first, self.second):
            arrived.wait_recv()
            onward.start()

    def arrive(self):
        for copy in self.second:
            copy.wait_recv()

    def finish(self):
        for copy in self.first + self.second:
            copy.wait_send()


def streams_back_kernel(
    first, lin, weight, hist, mix, lg, normed_in, own_rows,
    grads_out, small_out, products, rows_out,
    slots, weights, total, layers, stage, sums, blocks, tiles_out,
    sems, weight_sems, layer_sem, stage_sems, own_sems, load_sems, store_sems,
):
    tile, feats = total.shape
    depth = layers.shape[0]
    rows, width = lin.shape[1], lin.shape[2]
    tiles = rows // tile
    ring = Ring(rows)

    def fetch(stream):
        return weight_copies(
            weight, weights.at[stream % 2], weight_sems.at[stream % 2], stream
        )

    local = [
        pltpu.make_async_copy(lin.at[i], slots.at[i, ring.me], own_sems.at[i])
        for i in range(2)
    ]
    local.append(
        pltpu.make_async_copy(own_rows, rows_out.at[ring.me], own_sems.at[2])
    )
    for copy in local:
        copy.start()
    for stream in range(2):
        fetch(stream)(lambda copy: copy.start())
    sums[...] = jnp.zeros_like(sums)
    ring.barrier()
    spreads = [Spread(ring, slots.at[i], sems.at[i], 0, lin.at[i]) for i in range(2)]
    spreads.append(Spread(ring, rows_out, sems.at[2], 0, own_rows))

    def write_out(stream, index, slot):
        part = pl.ds(pl.multiple_of(index * tile, tile), tile)
        return pltpu.make_async_copy(
            stage.at[slot], grads_out.at[stream, part, :], stage_sems.at[slot]
        )

    def compute(stream):
        fetch(stream)(lambda copy: copy.wait())

        def one(index, carry):
            part = pl.ds(pl.multiple_of(index * tile, tile), tile)
            load = pltpu.make_async_copy(hist.at[:, part, :], layers, layer_sem)
            load.start()
            slot = lax.rem(index, 2)

            gathered = first if stream == 0 else slots.at[stream - 1]
            ring_product(gathered, weights.at[stream % 2], part, total)
            load.wait()

            @pl.when(index >= 2)
            def _():
                write_out(stream, index - 2, slot).wait()

            def back(sub):
                grads = total[sub, :]
                latest = layers[depth - 1, sub, :].astype(F32)
                at = pl.multiple_of(index * tile + sub.start, 16)
                share = mix[pl.ds(at, 16), :]
                mixture = latest
                for j in range(depth):
                    col = stream * depth + j
                    mixture = mixture + share[:, col : col + 1] * layers[j, sub, :].astype(F32)
                step, normed = norm_back(mixture, grads, lg[stream : stream + 1, :])
                stage[slot, sub, :] = step.astype(BF)
                sums[stream, 0] += fold(grads * normed)
                sums[stream, 1] += fold(grads)

            rows_loop(tile, 16, back)
            write_out(stream, index, slot).start()
            return carry

        lax.fori_loop(0, tiles, one, 0)
        for index in range(max(tiles - 2, 0), tiles):
            write_out(stream, index, index % 2).wait()
        if stream == 0:
            fetch(2)(lambda copy: copy.start())

    for copy in local:
        copy.wait()
    spreads[0].begin()
    compute(0)
    spreads[0].relay()
    for i in range(2):
        source, target = normed_in.at[i + 1], products.at[:, pl.ds(i * width, width)]
        weight_product(source, lin.at[i], target, blocks, tiles_out, load_sems, store_sems)
    spreads[0].arrive()
    spreads[1].begin()
    compute(1)
    spreads[1].relay()
    spreads[1].arrive()
    spreads[2].begin()
    compute(2)
    spreads[2].relay()
    spreads[2].arrive()
    for i in range(3):
        for j in range(2):
            small_out[j, i : i + 1, :] = jnp.sum(sums[i, j], axis=0, keepdims=True)
    for spread in spreads:
        spread.finish()


def streams_back(first, lin, weight, hist, mix, lg, normed, own_rows):
    depth, rows, feats = hist.shape
    width = lin.shape[2]
    tile = min(256, rows)
    return pl.pallas_call(
        streams_back_kernel,
        in_specs=[VMEM, VMEM, ANY, ANY, VMEM, VMEM, ANY, ANY],
        out_specs=[ANY, VMEM, ANY, ANY],
        out_shape=[
            jax.ShapeDtypeStruct((3, rows, feats), BF),
            jax.ShapeDtypeStruct((2, 3, feats), F32),
            jax.ShapeDtypeStruct((feats, 2 * width), BF),
            jax.ShapeDtypeStruct((RING,) + own_rows.shape, BF),
        ],
        scratch_shapes=[
            pltpu.VMEM((2, RING, rows, width), BF),
            pltpu.VMEM((2, RING, feats, width), BF),
            pltpu.VMEM((tile, feats), F32),
            pltpu.VMEM((depth, tile, feats), BF),
            pltpu.VMEM((2, tile, feats), BF),
            pltpu.VMEM((3, 2, 8, feats), F32),
            pltpu.VMEM((2, rows, 256), BF),
            pltpu.VMEM((2, 256, width), BF),
            pltpu.SemaphoreType.DMA((3, 2, 4)),
            pltpu.SemaphoreType.DMA((2, weight.shape[0])),
            pltpu.SemaphoreType.DMA,
            pltpu.SemaphoreType.DMA((2,)),
            pltpu.SemaphoreType.DMA((3,)),
            pltpu.SemaphoreType.DMA((2,)),
            pltpu.SemaphoreType.DMA((2,)),
        ],
        compiler_params=params(60, 2),
        cost_estimate=cost(240),
        name="streams_back",
    )(first, lin, weight, hist, mix, lg, normed, own_rows)


def small_kernel(seqs, owners, ours, share, out, share_out, near, all_ours, all_shares, near_sems, sems):
    ring = Ring(2)
    near_rows = near.shape[1]
    rank, peers, places = owner_places(seqs, owners)
    mates = [ring.right, ring.far, ring.left]
    enter(places + [{"tensor": z} for z in mates])

    near[ring.me] = ours[0:near_rows, :]
    shares = [
        push(share.at[p], all_shares.at[rank], sems.at[0], k, place)
        for k, (p, place) in enumerate(zip(peers, places))
    ]
    first = [
        push(near.at[ring.me], near.at[ring.me], near_sems, k, {"tensor": z})
        for k, z in enumerate(mates)
    ]
    for copy in first + shares:
        copy.start()
    for copy in first:
        copy.wait()
    all_ours[rank, 0:near_rows, :] = (near[0] + near[1]) + (near[2] + near[3])
    all_ours[rank, near_rows:, :] = ours[near_rows:, :]
    all_shares[rank] = share[rank]
    second = [
        push(all_ours.at[rank], all_ours.at[rank], sems.at[1], k, place)
        for k, place in enumerate(places)
    ]
    for copy in second:
        copy.start()
    for copy in shares + second:
        copy.wait()
    total, part = all_ours[0], all_shares[0]
    for index in range(1, owners):
        total += all_ours[index]
        part += all_shares[index]
    out[...] = total
    share_out[...] = part


def small_sums(ours, share, seqs):
    owners = share.shape[0]
    rows, feats = ours.shape
    return pl.pallas_call(
        functools.partial(small_kernel, seqs, owners),
        in_specs=[VMEM, VMEM],
        out_specs=[VMEM, VMEM],
        out_shape=[
            jax.ShapeDtypeStruct(ours.shape, F32),
            jax.ShapeDtypeStruct(share.shape[1:], F32),
        ],
        scratch_shapes=[
            pltpu.VMEM((RING, 8, feats), F32),
            pltpu.VMEM((owners,) + ours.shape, F32),
            pltpu.VMEM(share.shape, F32),
            pltpu.SemaphoreType.DMA((2, 3)),
            pltpu.SemaphoreType.DMA((2, 2, owners - 1)),
        ],
        compiler_params=params(40, 4),
        cost_estimate=cost(12),
        name="small_sums",
    )(ours, share)


def mlp_kernel(mlp_in, cot, up, down, bias, act_out, grad_out, sum_out):
    lin = dot(mlp_in[...], up[...]) + bias[...]
    grad_act = dot(cot[...], down[...])
    cdf = normal_cdf(lin)
    act_out[...] = (lin * cdf).astype(BF)
    grad = (grad_act * gelu_slope(lin, cdf)).astype(BF)
    grad_out[...] = grad

    @pl.when(pl.program_id(1) == 0)
    def _():
        sum_out[...] = jnp.zeros_like(sum_out)

    sum_out[...] += jnp.sum(grad.astype(F32), axis=0, keepdims=True)


def mlp(mlp_in, cot, up, down, bias):
    rows, feats = mlp_in.shape
    width = up.shape[1]
    tile, cols = min(256, rows), 512
    return pl.pallas_call(
        mlp_kernel,
        grid=(width // cols, rows // tile),
        in_specs=[
            pl.BlockSpec((tile, feats), lambda n, r: (r, 0)),
            pl.BlockSpec((tile, feats), lambda n, r: (r, 0)),
            pl.BlockSpec((feats, cols), lambda n, r: (0, n)),
            pl.BlockSpec((feats, cols), lambda n, r: (0, n)),
            pl.BlockSpec((1, cols), lambda n, r: (0, n)),
        ],
        out_specs=[
            pl.BlockSpec((tile, cols), lambda n, r: (r, n)),
            pl.BlockSpec((tile, cols), lambda n, r: (r, n)),
            pl.BlockSpec((1, cols), lambda n, r: (0, n)),
        ],
        out_shape=[
            jax.ShapeDtypeStruct((rows, width), BF),
            jax.ShapeDtypeStruct((rows, width), BF),
            jax.ShapeDtypeStruct((1, width), F32),
        ],
        compiler_params=params(48),
        cost_estimate=cost(25),
        name="mlp",
    )(mlp_in, cot, up, down, bias)


def turn_back_kernel(dkv, tables, dk_out, sum_out):
    tabs = (tables[0], tables[1], tables[2])
    for head in range(dk_out.shape[1] // HEAD_DIM):
        cols = slice(head * HEAD_DIM, (head + 1) * HEAD_DIM)
        dk_out[:, cols] = turn(dkv[0, :, cols].astype(F32), tabs, -1.0).astype(BF)


def last_kernel(
    hist, streams, attn, mix, pre, gain, w1, w2, grad_out, gain_out, w1_out, w2_out,
    normed, grad_mix, grad_normed, gain_sum,
):
    depth, rows, feats = hist.shape
    step_index = pl.program_id(0)

    @pl.when(step_index == 0)
    def _():
        gain_sum[...] = jnp.zeros_like(gain_sum)
        w1_out[...] = jnp.zeros_like(w1_out)
        w2_out[...] = jnp.zeros_like(w2_out)

    def reduce(part):
        layers = [hist[j, part, :].astype(F32) for j in range(depth)]
        latest = layers[depth - 1]
        scale = lax.rsqrt(mean_last(latest * latest) + RMS_EPSILON)
        normed[part, :] = (latest * scale * gain[...]).astype(BF)
        for m in range(STREAMS):
            grads = (attn[part, :] if m == STREAMS - 1 else streams[m, part, :]).astype(F32)
            for j in range(depth):
                at = m * depth + j
                grad_mix[part, at : at + 1] = jnp.sum(grads * layers[j], axis=-1, keepdims=True)

    rows_loop(rows, 16, reduce)
    pre_value = pre[...]
    cdf = normal_cdf(pre_value)
    grads = grad_mix[...]
    w2_out[...] += dot(pre_value * cdf, grads, TN, EXACT)
    grad_act = dot(grads, w2[...], NT, EXACT)
    grad_pre = (grad_act * gelu_slope(pre_value, cdf)).astype(BF)
    w1_out[...] += dot(grad_pre, normed[...], TN)
    grad_normed[...] = dot(grad_pre, w1[...], NT)

    def write(part):
        layers = [hist[depth - 1, part, :].astype(F32)]
        latest = layers[0]
        scale = lax.rsqrt(mean_last(latest * latest) + RMS_EPSILON)
        value = grad_normed[part, :]
        gain_sum[...] += fold(value * latest * scale)
        value = value * gain[...]
        back = scale * value - latest * (scale * scale * scale * mean_last(latest * value))
        weight = mix[part, :]
        grads = [streams[m, part, :].astype(F32) for m in range(STREAMS - 1)]
        grads.append(attn[part, :].astype(F32))
        for j in range(depth):
            total = weight[:, j : j + 1] * grads[0]
            for m in range(1, STREAMS):
                at = m * depth + j
                total = total + weight[:, at : at + 1] * grads[m]
            if j == depth - 1:
                total = total + (grads[0] + grads[1] + grads[2] + grads[3]) + back
            grad_out[j, part, :] = total

    rows_loop(rows, 16, write)

    @pl.when(step_index == pl.num_programs(0) - 1)
    def _():
        gain_out[...] = jnp.sum(gain_sum[...], axis=0, keepdims=True)


def last(hist, streams, attn, mix, pre, gain, w1, w2):
    depth, rows, feats = hist.shape
    hidden = w1.shape[1]
    tile = min(64, rows)
    full = lambda shape: pl.BlockSpec(shape, lambda i: (0,) * len(shape))
    return pl.pallas_call(
        last_kernel,
        grid=(rows // tile,),
        in_specs=[
            pl.BlockSpec((depth, tile, feats), lambda i: (0, i, 0)),
            pl.BlockSpec((3, tile, feats), lambda i: (0, i, 0)),
            pl.BlockSpec((tile, feats), lambda i: (i, 0)),
            pl.BlockSpec((tile, STREAMS * depth), lambda i: (i, 0)),
            pl.BlockSpec((tile, hidden), lambda i: (i, 0)),
            full((1, feats)),
            full(w1.shape),
            full(w2.shape),
        ],
        out_specs=[
            pl.BlockSpec((depth, tile, feats), lambda i: (0, i, 0)),
            full((1, feats)),
            full((hidden, feats)),
            full(w2.shape),
        ],
        out_shape=[
            jax.ShapeDtypeStruct((depth, rows, feats), F32),
            jax.ShapeDtypeStruct((1, feats), F32),
            jax.ShapeDtypeStruct((hidden, feats), F32),
            jax.ShapeDtypeStruct(w2.shape, F32),
        ],
        scratch_shapes=[
            pltpu.VMEM((tile, feats), BF),
            pltpu.VMEM((tile, STREAMS * depth), F32),
            pltpu.VMEM((tile, feats), F32),
            pltpu.VMEM((8, feats), F32),
        ],
        compiler_params=params(40),
        cost_estimate=cost(30),
        name="last",
    )(hist, streams, attn, mix, pre, gain.reshape(1, feats), w1, w2)


def turn_back(dkv, tables):
    _, rows, width = dkv.shape
    return pl.pallas_call(
        lambda d, t, o: turn_back_kernel(d, t, o, None),
        grid=(1,),
        in_specs=[
            pl.BlockSpec((1, rows, width), lambda i: (0, 0, 0)),
            pl.BlockSpec(tables.shape, lambda i: (0, 0, 0)),
        ],
        out_specs=pl.BlockSpec((rows, width), lambda i: (0, 0)),
        out_shape=jax.ShapeDtypeStruct((rows, width), BF),
        compiler_params=params(40),
        cost_estimate=cost(3),
        name="turn_back",
    )(dkv, tables)


def row_product(left, right):
    return dot(left, right, TN).astype(BF)


def shards(
    history,
    positions,
    lengths,
    cotangent,
    mix_gain,
    mix_w1,
    mix_w2,
    ln_gain,
    ln_bias,
    qkv_weight,
    qkv_bias,
    out_weight,
    out_bias,
    up_weight,
    up_bias,
    down_weight,
    down_bias,
):
    depth, slots, block_len, feats = history.shape
    rows = slots * block_len
    width = qkv_weight.shape[2]
    heads = width // HEAD_DIM
    owners = ("dp", "seq")
    layers = history.reshape(depth, rows, feats)

    seqs = lax.axis_size("seq")
    count = lax.axis_size("dp") * seqs
    tie = lax.optimization_barrier
    gather = functools.partial(lax.all_gather, axis_name=owners, axis=0)
    w_kv = gather(jnp.concatenate([qkv_weight[1], qkv_weight[2]], axis=1), tiled=True)
    w_q = gather(qkv_weight[0], tiled=True)

    offset = lax.axis_index("seq") * block_len
    query_place = offset + jnp.arange(block_len, dtype=jnp.int32)
    valid = (query_place[None, :] < lengths[:, None]).reshape(rows, 1)
    cot = jnp.where(valid, cotangent.reshape(rows, feats), jnp.zeros((), BF))
    scalars = jnp.concatenate([lengths, offset[None].astype(jnp.int32)])
    tables = rotary_tables(positions.reshape(rows))

    normed, resid, mix, pre, w_mix = front(
        layers, mix_gain, mix_w1, mix_w2, ln_gain, ln_bias, seqs, count
    )
    w_up = gather(up_weight, tiled=True)
    kv = project(normed, w_kv, qkv_bias[1:], tables, 1)
    kv_all, ring_out, ring_qkv = share(kv, out_weight, qkv_weight.reshape(-1, width), seqs)
    kv_all, w_up = tie((kv_all, w_up))
    kv_all, w_q = tie((kv_all, w_q))
    q = project(normed, w_q, qkv_bias[:1], tables, 0)[0]
    w_out_all = gather(ring_out)
    kv_all = kv_all.reshape(seqs, 2, slots, block_len, width)
    attn_vals = attend(scalars, q, kv_all, heads).reshape(rows, width)
    attn_vals, down_weight = tie((attn_vals, down_weight))
    w_down = gather(down_weight, tiled=True)
    vals_all = spread_vals(attn_vals)
    vals_all, ring_qkv = tie((vals_all, ring_qkv))
    w_qkv = gather(ring_qkv.reshape((RING,) + qkv_weight.shape))
    hidden, mlp_in = attn_out(
        vals_all, w_out_all, resid, out_bias[None, :], ln_gain[3:4], ln_bias[3:4]
    )
    w_out = lax.dynamic_index_in_dim(
        w_out_all, lax.axis_index("tensor"), 1, keepdims=False
    ).reshape(feats, width)
    up_act, grad_up, grad_up_bias = mlp(mlp_in, cot, w_up, w_down, up_bias[None, :])
    scatter = functools.partial(
        lax.psum_scatter, axis_name=owners, scatter_dimension=0, tiled=True
    )
    grad_attn, small_mlp, out_rows, grad_upw, grad_down = mlp_back(
        grad_up, w_up, up_act, w_down, hidden, cot, mlp_in, ln_gain[3:4], down_bias[None, :]
    )
    grad_vals = dot(grad_attn, w_out).astype(BF)
    dq, dkv = attend_back(scalars, q, kv_all, grad_vals, tables, heads)
    w_qkv, dq, dkv = tie((w_qkv, dq, dkv))
    dkv_own = lax.psum_scatter(dkv, "seq", scatter_dimension=0).reshape(2, rows, width)
    dq = dq.reshape(rows, width)
    dq_all, grad_qo = spread_dq(dq, normed, grad_attn, attn_vals)
    dq_all, dkv_own, grad_down, grad_upw, grad_qo = tie(
        (dq_all, dkv_own, grad_down, grad_upw, grad_qo)
    )
    shard_down, shard_up, shard_qo = scatter(grad_down), scatter(grad_upw), scatter(grad_qo)
    lin_kv = jnp.stack([turn_back(dkv_own, tables), dkv_own[1]])
    grads, small_qkv, grad_kv, layer_out = streams_back(
        dq_all, lin_kv, w_qkv, layers, mix, ln_gain, normed, out_rows
    )
    shard_down, shard_up, shard_qo, grads, grad_kv = tie(
        (shard_down, shard_up, shard_qo, grads, grad_kv)
    )
    shard_kv = scatter(grad_kv)
    shard_down, shard_up = shard_down.astype(F32), shard_up.astype(F32)
    shard_qkv = jnp.stack([shard_qo[:, :width], shard_kv[:, :width], shard_kv[:, width:]])
    shard_qkv, shard_out = shard_qkv.astype(F32), shard_qo[:, width:].astype(F32)
    grad_layers, grad_gain, grad_w1, grad_w2 = last(
        layers, grads, grad_attn, mix, pre, mix_gain, w_mix, mix_w2
    )
    grad_history = grad_layers.reshape(depth, slots, block_len, feats)
    hidden_count = mix_w1.shape[1]
    w1_share = grad_w1.reshape(hidden_count, count, feats // count).transpose(1, 0, 2)

    def as_row(values):
        flat = values.reshape(1, -1)
        return jnp.pad(flat, ((0, 0), (0, feats - flat.shape[1])))

    grad_qkv_bias = jnp.concatenate(
        [jnp.sum(dq.astype(F32), axis=0)[None], jnp.sum(lin_kv.astype(F32), axis=1)]
    )
    ours = jnp.concatenate(
        [small_mlp, jnp.zeros((5, feats), F32), small_qkv.reshape(6, feats)]
        + [
            as_row(values)
            for values in (
                grad_gain, grad_w2, grad_qkv_bias, grad_up_bias, jnp.sum(cot.astype(F32), axis=0)
            )
        ]
        + [jnp.zeros((5, feats), F32)],
        axis=0,
    )
    summed, shard_w1 = small_sums(ours, w1_share.reshape(count, -1, 128), seqs)
    return (
        layer_out.reshape(slots, block_len, feats),
        grad_history,
        summed[14],
        shard_w1.reshape(hidden_count, feats // count).T,
        summed[15, : grad_w2.size].reshape(grad_w2.shape),
        jnp.concatenate([summed[8:11], summed[0:1]], axis=0),
        jnp.concatenate([summed[11:14], summed[1:2]], axis=0),
        shard_qkv,
        summed[16, : grad_qkv_bias.size].reshape(grad_qkv_bias.shape),
        shard_out,
        summed[2],
        shard_up,
        summed[17, : up_bias.size],
        shard_down,
        summed[18],
    )


def solution(mesh):
    in_specs = (
        P(None, "dp", "seq", None),
        P("dp", "seq"),
        P("dp"),
        P("dp", "seq", None),
        P(),
        P(("dp", "seq"), None),
        P(),
        P(),
        P(),
        P(None, ("dp", "seq"), "tensor"),
        P(None, "tensor"),
        P(("dp", "seq"), "tensor"),
        P(),
        P(("dp", "seq"), "tensor"),
        P("tensor"),
        P(("dp", "seq"), "tensor"),
        P(),
    )
    out_specs = (
        P("dp", "seq", None),
        P(None, "dp", "seq", None),
        P(),
        P(("dp", "seq"), None),
        P(),
        P(),
        P(),
        P(None, ("dp", "seq"), "tensor"),
        P(None, "tensor"),
        P(("dp", "seq"), "tensor"),
        P(),
        P(("dp", "seq"), "tensor"),
        P("tensor"),
        P(("dp", "seq"), "tensor"),
        P(),
    )
    return jax.shard_map(shards, mesh=mesh, in_specs=in_specs, out_specs=out_specs, check_vma=False)
```

```python
import functools
import math

import jax
import jax.numpy as jnp
from jax import lax
from jax.experimental import pallas as pl
from jax.experimental.pallas import tpu as pltpu
from jax.sharding import PartitionSpec as P

HEAD_DIM = 128
ROT = 32
STREAMS = 4
EXACT = lax.Precision.HIGHEST
RMS_EPSILON = 1e-06
NORM_EPSILON = 1e-05
BF = jnp.bfloat16
F32 = jnp.float32
MESH = pl.DeviceIdType.MESH
ANY = pl.BlockSpec(memory_space=pl.ANY)
VMEM = pl.BlockSpec(memory_space=pltpu.VMEM)
RING = 4
NN = (((1,), (0,)), ((), ()))
NT = (((1,), (1,)), ((), ()))
TN = (((0,), (0,)), ((), ()))


def dot(left, right, dims=NN, precision=None):
    return lax.dot_general(left, right, dims, precision=precision, preferred_element_type=F32)


def normal_cdf(values):
    return 0.5 * (1.0 + lax.erf(values * math.sqrt(0.5)))


def gelu_slope(values, cdf):
    return cdf + values * (jnp.exp(-0.5 * values * values) * (1.0 / math.sqrt(2.0 * math.pi)))


def mean_last(values):
    return jnp.mean(values, axis=-1, keepdims=True)


def rows_loop(total, step, body):
    def one(index, carry):
        body(pl.ds(pl.multiple_of(index * step, step), step))
        return carry

    lax.fori_loop(0, total // step, one, 0)


def params(limit_mib, collective_id=None):
    if collective_id is None:
        return pltpu.CompilerParams(vmem_limit_bytes=limit_mib << 20)
    return pltpu.CompilerParams(
        vmem_limit_bytes=limit_mib << 20, collective_id=collective_id, has_side_effects=True
    )


def cost(micros):
    return pl.CostEstimate(flops=0, bytes_accessed=int(micros * 3.0e6), transcendentals=0)


def owner_places(seqs, owners):
    rank = lax.axis_index("dp") * seqs + lax.axis_index("seq")
    peers = [lax.rem(rank + k, owners) for k in range(1, owners)]
    return rank, peers, [{"dp": lax.div(p, seqs), "seq": lax.rem(p, seqs)} for p in peers]


def push(source, target, sems, index, place):
    return pltpu.make_async_remote_copy(
        src_ref=source,
        dst_ref=target,
        send_sem=sems.at[0, index],
        recv_sem=sems.at[1, index],
        device_id=place,
        device_id_type=MESH,
    )


def enter(places):
    gate = pltpu.get_barrier_semaphore()
    for place in places:
        pl.semaphore_signal(gate, inc=1, device_id=place, device_id_type=MESH)
    pl.semaphore_wait(gate, len(places))


def front_kernel(
    seqs, owners,
    hist, gain, w1, w2, lg, lb, normed_out, resid_out, mix_out, pre_out, w1_out,
    scratch, w1_all, w1_sems,
):
    depth, rows, _ = hist.shape
    index = pl.program_id(0)
    rank, _, places = owner_places(seqs, owners)
    w1_copies = [push(w1, w1_all.at[rank], w1_sems, k, p) for k, p in enumerate(places)]

    @pl.when(index == 0)
    def _():
        enter(places)
        for copy in w1_copies:
            copy.start()
        w1_all[rank] = w1[...]
        for copy in w1_copies:
            copy.wait()
        w1_out[...] = w1_all[...].reshape(w1_out.shape)

    def rms(part):
        wide = hist[depth - 1, part, :].astype(F32)
        scale = lax.rsqrt(mean_last(wide * wide) + RMS_EPSILON)
        scratch[part, :] = (wide * scale * gain[...]).astype(BF)

    rows_loop(rows, 64, rms)
    pre = dot(scratch[...], w1_out[...])
    pre_out[...] = pre
    mix_out[...] = dot(pre * normal_cdf(pre), w2[...], precision=EXACT)

    def combine(part):
        layers = [hist[j, part, :].astype(F32) for j in range(depth)]
        mix = mix_out[part, :]
        for m in range(STREAMS):
            running = layers[depth - 1]
            for j in range(depth):
                running = running + mix[:, m * depth + j : m * depth + j + 1] * layers[j]
            if m == STREAMS - 1:
                resid_out[part, :] = running
            else:
                centred = running - mean_last(running)
                inverse = lax.rsqrt(mean_last(centred * centred) + NORM_EPSILON)
                normed = centred * inverse * lg[m : m + 1, :] + lb[m : m + 1, :]
                normed_out[m, part, :] = normed.astype(BF)

    rows_loop(rows, 64, combine)


def front(layers, gain, w1, w2, lg, lb, seqs, owners):
    depth, rows, feats = layers.shape
    tile = min(128, rows)
    hidden = w1.shape[1]
    full = lambda shape: pl.BlockSpec(shape, lambda i: (0,) * len(shape))
    return pl.pallas_call(
        functools.partial(front_kernel, seqs, owners),
        grid=(rows // tile,),
        in_specs=[
            pl.BlockSpec((depth, tile, feats), lambda i: (0, i, 0)),
            full((1, feats)),
            full(w1.shape),
            full(w2.shape),
            full(lg.shape),
            full(lb.shape),
        ],
        out_specs=[
            pl.BlockSpec((3, tile, feats), lambda i: (0, i, 0)),
            pl.BlockSpec((tile, feats), lambda i: (i, 0)),
            pl.BlockSpec((tile, STREAMS * depth), lambda i: (i, 0)),
            pl.BlockSpec((tile, hidden), lambda i: (i, 0)),
            full((feats, hidden)),
        ],
        out_shape=[
            jax.ShapeDtypeStruct((3, rows, feats), BF),
            jax.ShapeDtypeStruct((rows, feats), F32),
            jax.ShapeDtypeStruct((rows, STREAMS * depth), F32),
            jax.ShapeDtypeStruct((rows, hidden), F32),
            jax.ShapeDtypeStruct((feats, hidden), BF),
        ],
        scratch_shapes=[
            pltpu.VMEM((tile, feats), BF),
            pltpu.VMEM((owners,) + w1.shape, BF),
            pltpu.SemaphoreType.DMA((2, owners - 1)),
        ],
        compiler_params=params(48, 5),
        cost_estimate=cost(45),
        name="front",
    )(layers, gain.reshape(1, feats), w1, w2, lg, lb)


def turn(values, tables, sign):
    cosines, low, high = tables
    return values * cosines + sign * (
        pltpu.roll(values, HEAD_DIM - ROT // 2, 1) * low + pltpu.roll(values, ROT // 2, 1) * high
    )


def rotary_tables(positions):
    exponents = jnp.arange(0, ROT, 2).astype(F32) / ROT
    inverse = jnp.power(10000.0, -exponents)
    phases = positions.astype(F32)[:, None] * inverse[None, :]
    cosines, sines = jnp.cos(phases), jnp.sin(phases)
    rows, half = phases.shape
    ones = jnp.ones((rows, HEAD_DIM - 2 * half), F32)
    none = jnp.zeros((rows, HEAD_DIM - 2 * half), F32)
    zero = jnp.zeros((rows, half), F32)
    return jnp.stack(
        [
            jnp.concatenate([cosines, cosines, ones], axis=1),
            jnp.concatenate([-sines, zero, none], axis=1),
            jnp.concatenate([zero, sines, none], axis=1),
        ]
    )


def proj_kernel(first, lhs, weight, bias, tables, out):
    branch = pl.program_id(0) + first
    value = dot(lhs[0], weight[...]) + bias[0]

    @pl.when(branch < 2)
    def _():
        tabs = (tables[0], tables[1], tables[2])
        for head in range(value.shape[1] // HEAD_DIM):
            cols = slice(head * HEAD_DIM, (head + 1) * HEAD_DIM)
            out[0, :, cols] = turn(value[:, cols], tabs, 1.0).astype(BF)

    @pl.when(branch >= 2)
    def _():
        out[0] = value.astype(BF)


def project(normed, weight, bias, tables, first):
    _, rows, feats = normed.shape
    count, width = bias.shape
    tile = min(256, rows)
    return pl.pallas_call(
        functools.partial(proj_kernel, first),
        grid=(count, rows // tile),
        in_specs=[
            pl.BlockSpec((1, tile, feats), lambda b, r: (b + first, r, 0)),
            pl.BlockSpec((feats, width), lambda b, r: (0, b)),
            pl.BlockSpec((1, 1, width), lambda b, r: (b, 0, 0)),
            pl.BlockSpec((3, tile, HEAD_DIM), lambda b, r: (0, r, 0)),
        ],
        out_specs=pl.BlockSpec((1, tile, width), lambda b, r: (b, r, 0)),
        out_shape=jax.ShapeDtypeStruct((count, rows, width), BF),
        compiler_params=params(40),
        cost_estimate=cost(4 * count),
        name="project",
    )(normed, weight, bias.reshape(count, 1, width), tables)


def share_kernel(
    kv, shard_out, shard_qkv, kv_out, ring_out, ring_qkv, sems, ring_sems, own_sems
):
    seqs = kv_out.shape[0]
    me = lax.axis_index("seq")
    ring = Ring(16)
    places = [{"seq": lax.rem(me + k, seqs)} for k in range(1, seqs)]
    local = [
        pltpu.make_async_copy(kv, kv_out.at[me], own_sems.at[0]),
        pltpu.make_async_copy(shard_out, ring_out.at[ring.me], own_sems.at[1]),
        pltpu.make_async_copy(shard_qkv, ring_qkv.at[ring.me], own_sems.at[2]),
    ]
    for copy in local:
        copy.start()
    enter(places + [{"tensor": ring.left}, {"tensor": ring.right}])
    copies = [push(kv, kv_out.at[me], sems, k, place) for k, place in enumerate(places)]
    spreads = [
        Spread(ring, slots, ring_sems.at[i], 0, source)
        for i, (slots, source) in enumerate(((ring_out, shard_out), (ring_qkv, shard_qkv)))
    ]
    for copy in copies:
        copy.start()
    for spread in spreads:
        spread.begin()

    for spread in spreads:
        spread.relay()
    for copy in copies:
        copy.wait()
    for spread in spreads:
        spread.arrive()
        spread.finish()
    for copy in local:
        copy.wait()


def share(kv, shard_out, shard_qkv, seqs):
    return pl.pallas_call(
        share_kernel,
        in_specs=[ANY, ANY, ANY],
        out_specs=[ANY, ANY, ANY],
        out_shape=[
            jax.ShapeDtypeStruct((seqs,) + kv.shape, BF),
            jax.ShapeDtypeStruct((RING,) + shard_out.shape, BF),
            jax.ShapeDtypeStruct((RING,) + shard_qkv.shape, BF),
        ],
        scratch_shapes=[
            pltpu.SemaphoreType.DMA((2, seqs - 1)),
            pltpu.SemaphoreType.DMA((2, 2, 4)),
            pltpu.SemaphoreType.DMA((3,)),
        ],
        compiler_params=params(48, 6),
        cost_estimate=cost(72),
        name="share",
    )(kv, shard_out, shard_qkv)


def attend_kernel(scalars, q, k, v, out):
    keys = k[...].reshape(-1, HEAD_DIM)
    values = v[...].reshape(-1, HEAD_DIM)
    length = scalars[pl.program_id(0)]
    offset = scalars[pl.num_programs(0)]
    scores = dot(q[0], keys, NT) * (1.0 / math.sqrt(HEAD_DIM))
    key_place = lax.broadcasted_iota(jnp.int32, scores.shape, 1)
    query_place = lax.broadcasted_iota(jnp.int32, scores.shape, 0) + offset
    scores = jnp.where((key_place <= query_place) & (key_place < length), scores, -1e30)
    weights = jnp.exp(scores - jnp.max(scores, axis=-1, keepdims=True))
    total = jnp.sum(weights, axis=-1, keepdims=True)
    probs = (weights * (1.0 / total)).astype(BF)
    out[0] = dot(probs, values).astype(BF)


def attend(scalars, q, kv, heads):
    seqs, _, slots, length, width = kv.shape
    block = (1, length, HEAD_DIM)
    return pl.pallas_call(
        attend_kernel,
        grid_spec=pltpu.PrefetchScalarGridSpec(
            num_scalar_prefetch=1,
            grid=(slots, heads),
            in_specs=[
                pl.BlockSpec(block, lambda s, h, _: (s, 0, h)),
                pl.BlockSpec((seqs, 1, 1, length, HEAD_DIM), lambda s, h, _: (0, 0, s, 0, h)),
                pl.BlockSpec((seqs, 1, 1, length, HEAD_DIM), lambda s, h, _: (0, 1, s, 0, h)),
            ],
            out_specs=pl.BlockSpec(block, lambda s, h, _: (s, 0, h)),
        ),
        out_shape=jax.ShapeDtypeStruct((slots, length, width), BF),
        compiler_params=params(40),
        cost_estimate=cost(15),
        name="attend",
    )(scalars, q.reshape(slots, length, width), kv, kv)


def attend_back_kernel(scalars, q, k, v, g, tables, dq_out, dkv_out):
    seqs = k.shape[0]
    scaling = 1.0 / math.sqrt(HEAD_DIM)
    keys = k[...].reshape(-1, HEAD_DIM)
    values = v[...].reshape(-1, HEAD_DIM)
    length = scalars[pl.program_id(0)]
    offset = scalars[pl.num_programs(0)]
    queries, grads = q[0], g[0]
    scores = dot(keys, queries, NT) * scaling
    key_place = lax.broadcasted_iota(jnp.int32, scores.shape, 0)
    query_place = lax.broadcasted_iota(jnp.int32, scores.shape, 1) + offset
    scores = jnp.where((key_place <= query_place) & (key_place < length), scores, -1e30)
    weights = jnp.exp(scores - jnp.max(scores, axis=0, keepdims=True))
    probs = weights * (1.0 / jnp.sum(weights, axis=0, keepdims=True))
    grad_probs = dot(values, grads, NT)
    mixed = jnp.sum(probs * grad_probs, axis=0, keepdims=True)
    grad_scores = (probs * (grad_probs - mixed)).astype(BF)
    grad_values = dot(probs.astype(BF), grads)
    grad_keys = dot(grad_scores, queries) * scaling
    shape = (seqs, -1, HEAD_DIM)
    dkv_out[:, 0, 0] = grad_keys.astype(BF).reshape(shape)
    dkv_out[:, 1, 0] = grad_values.astype(BF).reshape(shape)
    grad_queries = dot(grad_scores, keys, TN) * scaling
    tabs = (tables[0], tables[1], tables[2])
    dq_out[0] = turn(grad_queries, tabs, -1.0).astype(BF)


def attend_back(scalars, q, kv, g, tables, heads):
    seqs, _, slots, length, width = kv.shape
    block = (1, length, HEAD_DIM)
    own = pl.BlockSpec(block, lambda s, h, _: (s, 0, h))
    return pl.pallas_call(
        attend_back_kernel,
        grid_spec=pltpu.PrefetchScalarGridSpec(
            num_scalar_prefetch=1,
            grid=(slots, heads),
            in_specs=[
                own,
                pl.BlockSpec((seqs, 1, 1, length, HEAD_DIM), lambda s, h, _: (0, 0, s, 0, h)),
                pl.BlockSpec((seqs, 1, 1, length, HEAD_DIM), lambda s, h, _: (0, 1, s, 0, h)),
                own,
                pl.BlockSpec((3, length, HEAD_DIM), lambda s, h, _: (0, s, 0)),
            ],
            out_specs=[
                own,
                pl.BlockSpec((seqs, 2, 1, length, HEAD_DIM), lambda s, h, _: (0, 0, s, 0, h)),
            ],
        ),
        out_shape=[
            jax.ShapeDtypeStruct((slots, length, width), BF),
            jax.ShapeDtypeStruct((seqs, 2, slots, length, width), BF),
        ],
        compiler_params=params(48),
        cost_estimate=cost(25),
        name="attend_back",
    )(scalars, q.reshape(slots, length, width), kv, kv, g.reshape(slots, length, width), tables)


class Ring:
    def __init__(self, chunk):
        me = lax.axis_index("tensor")
        self.chunk, self.half = chunk, chunk // 2
        self.me = me
        self.right = lax.rem(me + 1, RING)
        self.left = lax.rem(me + RING - 1, RING)
        self.far = lax.rem(me + 2, RING)

    def at(self, index, shift=0):
        return pl.multiple_of(index * self.chunk + shift, self.half)

    def barrier(self):
        gate = pltpu.get_barrier_semaphore()
        for near in (self.left, self.right):
            pl.semaphore_signal(gate, inc=1, device_id={"tensor": near}, device_id_type=MESH)
        pl.semaphore_wait(gate, 2)


def remote(source, target, sems, index, device):
    return pltpu.make_async_remote_copy(
        src_ref=source,
        dst_ref=target,
        send_sem=sems.at[0, index],
        recv_sem=sems.at[1, index],
        device_id={"tensor": device},
        device_id_type=MESH,
    )


def product(lhs, rhs, start, count, write, step=512):
    total = rhs.shape[0]

    def one(cols):
        write(cols, dot(lhs[pl.ds(start, count), :], rhs[cols, :], NT))

    rows_loop(total, min(step, total), one)


class Scatter:
    def __init__(self, ring, lhs, rhs, far, near, far_in, near_in, sems):
        self.ring, self.lhs, self.rhs = ring, lhs, rhs
        self.far, self.near, self.far_in, self.near_in = far, near, far_in, near_in
        half = ring.half
        up, down = pl.ds(0, half), pl.ds(half, half)
        self.copies = [
            remote(far.at[0], far_in.at[0], sems, 0, ring.right),
            remote(far.at[1], far_in.at[1], sems, 1, ring.left),
            remote(near.at[0, down], near_in.at[0, down], sems, 2, ring.right),
            remote(near.at[1, up], near_in.at[1, up], sems, 3, ring.left),
            remote(near.at[0, up], near_in.at[0, up], sems, 4, ring.right),
            remote(near.at[1, down], near_in.at[1, down], sems, 5, ring.left),
        ]

    def begin(self):
        ring, half = self.ring, self.ring.half

        def far_half(which):
            def write(cols, value):
                self.far[which, :, cols] = value.astype(BF)

            product(self.lhs, self.rhs, ring.at(ring.far, which * half), half, write)
            self.copies[which].start()

        def near_half(which, device, part, copy):
            def write(cols, value):
                self.near[which, pl.ds(part * half, half), cols] = value.astype(BF)

            product(self.lhs, self.rhs, ring.at(device, part * half), half, write)
            self.copies[copy].start()

        far_half(0)
        far_half(1)
        near_half(0, ring.right, 1, 2)
        near_half(1, ring.left, 0, 3)

    def relay(self):
        ring, half = self.ring, self.ring.half

        def add_half(which, device, part, copy):
            self.copies[which].wait_recv()

            def write(cols, value):
                arrived = self.far_in[which, :, cols].astype(F32)
                self.near[which, pl.ds(part * half, half), cols] = (value + arrived).astype(BF)

            product(self.lhs, self.rhs, ring.at(device, part * half), half, write)
            self.copies[copy].start()

        add_half(0, ring.right, 0, 4)
        add_half(1, ring.left, 1, 5)

    def arrive(self):
        for copy in self.copies[2:]:
            copy.wait_recv()

    def finish(self):
        for copy in self.copies:
            copy.wait_send()


class Gather:
    def __init__(self, ring, own, out, sems, base, local_sem):
        half = ring.half

        def rows(index, shift=0, count=ring.chunk):
            return out.at[pl.ds(ring.at(index, shift), count), :]

        mine = rows(ring.me)
        self.local = pltpu.make_async_copy(own, mine, local_sem)
        self.first = [
            remote(own, mine, sems, base, ring.right),
            remote(own, mine, sems, base + 1, ring.left),
        ]
        up, down = rows(ring.left, 0, half), rows(ring.right, half, half)
        self.second = [
            remote(up, up, sems, base + 2, ring.right),
            remote(down, down, sems, base + 3, ring.left),
        ]

    def begin(self):
        for copy in self.first:
            copy.start()
        self.local.start()

    def relay(self):
        for arrived, onward in zip(self.first, self.second):
            arrived.wait_recv()
            onward.start()

    def finish(self):
        for copy in self.second:
            copy.wait_recv()
        for copy in self.first + self.second:
            copy.wait_send()
        self.local.wait()


def scatter_scratch(chunk, feats, count=1):
    half = chunk // 2
    lead = () if count == 1 else (count,)
    return [
        pltpu.VMEM(lead + (2, half, feats), BF),
        pltpu.VMEM(lead + (2, chunk, feats), BF),
        pltpu.VMEM(lead + (2, half, feats), BF),
        pltpu.VMEM(lead + (2, chunk, feats), BF),
    ]


def own_sum(scatter, total):
    ring = scatter.ring

    def write(cols, value):
        total[:, cols] = value

    product(scatter.lhs, scatter.rhs, ring.at(ring.me), ring.chunk, write)


def whole_sum(scatter, total, part):
    near = scatter.near_in
    return total[part, :] + near[0, part, :].astype(F32) + near[1, part, :].astype(F32)


def weight_copies(weight, target, sems, index):
    count = weight.shape[-2]

    def one(owner):
        source = weight.at[owner] if index is None else weight.at[owner, :, index]
        return pltpu.make_async_copy(
            source,
            target.at[:, pl.ds(pl.multiple_of(owner * count, count), count), :],
            sems.at[owner],
        )

    def every(act):
        def step(owner, carry):
            act(one(owner))
            return carry

        lax.fori_loop(0, weight.shape[0], step, 0)

    return every


def ring_product(slots, weight, part, total):
    def columns(cols):
        value = dot(slots[0, part, :], weight[0, cols, :], NT)
        for z in range(1, RING):
            value += dot(slots[z, part, :], weight[z, cols, :], NT)
        total[:, cols] = value

    rows_loop(total.shape[1], 512, columns)


def spread_kernel(vals, out, sems, own_sem):
    ring = Ring(16)
    local = pltpu.make_async_copy(vals, out.at[ring.me], own_sem)
    local.start()
    ring.barrier()
    spread = Spread(ring, out, sems, 0, vals)
    spread.begin()
    spread.relay()
    spread.arrive()
    spread.finish()
    local.wait()


def spread_vals(vals):
    return pl.pallas_call(
        spread_kernel,
        in_specs=[ANY],
        out_specs=ANY,
        out_shape=jax.ShapeDtypeStruct((RING,) + vals.shape, BF),
        scratch_shapes=[pltpu.SemaphoreType.DMA((2, 4)), pltpu.SemaphoreType.DMA],
        compiler_params=params(32, 0),
        cost_estimate=cost(70),
        name="spread_vals",
    )(vals)


def attn_out_kernel(
    slots, weight, resid, bias, lg, lb, hidden_out, mlp_out,
    weights, total, base_rows, stage, weight_sems, base_sem, stage_sems,
):
    chunk, feats = total.shape
    me = lax.axis_index("tensor")
    load = weight_copies(weight, weights, weight_sems, None)
    load(lambda copy: copy.start())
    load(lambda copy: copy.wait())

    def write_out(index, slot):
        part = pl.ds(pl.multiple_of(index * chunk, chunk), chunk)
        return pltpu.make_async_copy(stage.at[slot], mlp_out.at[part, :], stage_sems.at[slot])

    def one(index, carry):
        part = pl.ds(pl.multiple_of(index * chunk, chunk), chunk)
        fetch = pltpu.make_async_copy(resid.at[part, :], base_rows, base_sem)
        fetch.start()
        slot = lax.rem(index, 2)
        ring_product(slots, weights, part, total)
        fetch.wait()

        @pl.when(index >= 2)
        def _():
            write_out(index - 2, slot).wait()

        def norm(sub):
            value = base_rows[sub, :] + (total[sub, :] + bias[...])
            total[sub, :] = value
            centred = value - mean_last(value)
            inverse = lax.rsqrt(mean_last(centred * centred) + NORM_EPSILON)
            stage[slot, sub, :] = (centred * inverse * lg[...] + lb[...]).astype(BF)

        rows_loop(chunk, 64, norm)
        write_out(index, slot).start()

        @pl.when(index == me)
        def _():
            hidden_out[...] = total[...]

        return carry

    lax.fori_loop(0, RING, one, 0)
    for index in range(RING - 2, RING):
        write_out(index, index % 2).wait()


def attn_out(slots, weight, resid, bias, lg, lb):
    rows, feats = resid.shape
    width = slots.shape[2]
    chunk = rows // RING
    return pl.pallas_call(
        attn_out_kernel,
        in_specs=[VMEM, ANY, ANY, VMEM, VMEM, VMEM],
        out_specs=[VMEM, ANY],
        out_shape=[
            jax.ShapeDtypeStruct((chunk, feats), F32),
            jax.ShapeDtypeStruct((rows, feats), BF),
        ],
        scratch_shapes=[
            pltpu.VMEM((RING, feats, width), BF),
            pltpu.VMEM((chunk, feats), F32),
            pltpu.VMEM((chunk, feats), F32),
            pltpu.VMEM((2, chunk, feats), BF),
            pltpu.SemaphoreType.DMA((weight.shape[0],)),
            pltpu.SemaphoreType.DMA,
            pltpu.SemaphoreType.DMA((2,)),
        ],
        compiler_params=params(48),
        cost_estimate=cost(30),
        name="attn_out",
    )(slots, weight, resid, bias, lg, lb)


def norm_back(values, grads, gain):
    centred = values - mean_last(values)
    inverse = lax.rsqrt(mean_last(centred * centred) + NORM_EPSILON)
    normed = centred * inverse
    inner = grads * gain
    back = inverse * (inner - mean_last(inner) - normed * mean_last(inner * normed))
    return back, normed


def fold(values):
    rows, feats = values.shape
    return jnp.sum(values.reshape(rows // 8, 8, feats), axis=0)


def weight_product(source, rhs, out, blocks, stage, load_sems, store_sems):
    width = blocks.shape[2]
    count = source.shape[1] // width

    def load(n, slot):
        cols = pl.ds(pl.multiple_of(n * width, width), width)
        return pltpu.make_async_copy(source.at[:, cols], blocks.at[slot], load_sems.at[slot])

    def store(n, slot):
        part = pl.ds(pl.multiple_of(n * width, width), width)
        return pltpu.make_async_copy(stage.at[slot], out.at[part, :], store_sems.at[slot])

    load(0, 0).start()

    def one(n, carry):
        slot = lax.rem(n, 2)

        @pl.when(n + 1 < count)
        def _():
            load(n + 1, 1 - slot).start()

        load(n, slot).wait()

        @pl.when(n >= 2)
        def _():
            store(n - 2, slot).wait()

        def columns(cols):
            stage[slot, :, cols] = dot(blocks[slot], rhs[:, cols], TN).astype(BF)

        rows_loop(rhs.shape[1], 512, columns)
        store(n, slot).start()
        return carry

    lax.fori_loop(0, count, one, 0)
    for n in range(count - 2, count):
        store(n, n % 2).wait()


def spread_dq_kernel(
    lin, normed, grad_attn, vals, out, products,
    blocks, tiles_out, sems, own_sem, load_sems, store_sems,
):
    ring = Ring(16)
    width = lin.shape[1]
    local = pltpu.make_async_copy(lin, out.at[ring.me], own_sem)
    local.start()
    ring.barrier()
    spread = Spread(ring, out, sems, 0, lin)
    spread.begin()
    for i, (source, rhs) in enumerate(((normed.at[0], lin), (grad_attn, vals))):
        target = products.at[:, pl.ds(i * width, width)]
        weight_product(source, rhs, target, blocks, tiles_out, load_sems, store_sems)
    spread.relay()
    spread.arrive()
    spread.finish()
    local.wait()


def spread_dq(lin, normed, grad_attn, vals):
    rows, width = lin.shape
    feats = grad_attn.shape[1]
    return pl.pallas_call(
        spread_dq_kernel,
        in_specs=[VMEM, ANY, ANY, VMEM],
        out_specs=[ANY, ANY],
        out_shape=[
            jax.ShapeDtypeStruct((RING, rows, width), BF),
            jax.ShapeDtypeStruct((feats, 2 * width), BF),
        ],
        scratch_shapes=[
            pltpu.VMEM((2, rows, 256), BF),
            pltpu.VMEM((2, 256, width), BF),
            pltpu.SemaphoreType.DMA((2, 4)),
            pltpu.SemaphoreType.DMA,
            pltpu.SemaphoreType.DMA((2,)),
            pltpu.SemaphoreType.DMA((2,)),
        ],
        compiler_params=params(40, 3),
        cost_estimate=cost(70),
        name="spread_dq",
    )(lin, normed, grad_attn, vals)


class Line:
    def __init__(self, chunk):
        me = lax.axis_index("tensor")
        self.me, self.chunk = me, chunk
        self.low = me < 2
        self.outer = (me == 0) | (me == RING - 1)
        self.inner = (me == 1) | (me == RING - 2)
        self.up = jnp.where(self.low, me + 1, me - 1)
        self.down = jnp.where(self.low, lax.max(me - 1, 0), lax.min(me + 1, RING - 1))

    def at(self, number):
        index = jnp.where(self.low, number, RING - 1 - number)
        return pl.ds(pl.multiple_of(index * self.chunk, self.chunk), self.chunk)

    def barrier(self):
        gate = pltpu.get_barrier_semaphore()
        pl.semaphore_signal(gate, inc=1, device_id={"tensor": self.up}, device_id_type=MESH)

        @pl.when(self.inner)
        def _():
            pl.semaphore_signal(
                gate, inc=1, device_id={"tensor": self.down}, device_id_type=MESH
            )
            pl.semaphore_wait(gate, 2)

        @pl.when(self.outer)
        def _():
            pl.semaphore_wait(gate, 1)


class LineSum:
    def __init__(self, line, lhs, rhs, outbound, inbound, sems, base):
        self.line, self.lhs, self.rhs = line, lhs, rhs
        self.outbound, self.inbound = outbound, inbound
        copy = lambda slot, target, device: remote(
            outbound.at[slot], inbound.at[target], sems, base + target, device
        )
        self.inward = [copy(i, i, line.up) for i in range(3)]
        self.across = [copy(i, 3 + i, line.up) for i in range(2)]
        self.outward = remote(outbound.at[2], inbound.at[5], sems, base + 5, line.down)

    def partial(self, number, slot, arrived=None):
        rows = self.line.at(number)

        def write(cols, value):
            if arrived is not None:
                value = value + self.inbound[arrived, :, cols].astype(F32)
            self.outbound[slot, :, cols] = value.astype(BF)

        product(self.lhs, self.rhs, rows.start, self.line.chunk, write)

    def own(self, total):
        index = self.line.me * self.line.chunk

        def write(cols, value):
            total[:, cols] = value

        product(
            self.lhs, self.rhs, pl.multiple_of(index, self.line.chunk), self.line.chunk, write
        )

    def send_inward(self):
        for slot, copy in enumerate(self.inward):
            self.partial(3 - slot, slot)
            copy.start()

    def send_across(self, i):
        self.inward[i].wait_recv()
        self.partial(3 - i, i, i)
        self.across[i].start()

    def send_outward(self):
        self.across[0].wait_recv()
        self.partial(0, 2, 3)
        self.outward.start()

    def arrive(self):
        line = self.line

        @pl.when(line.inner)
        def _():
            self.inward[2].wait_recv()
            self.across[1].wait_recv()

        @pl.when(line.outer)
        def _():
            self.outward.wait_recv()

    def sent(self):
        line = self.line

        @pl.when(line.inner)
        def _():
            for copy in self.across + [self.outward]:
                copy.wait_send()

        @pl.when(line.outer)
        def _():
            for copy in self.inward:
                copy.wait_send()

    def clear(self):
        @pl.when(self.line.outer)
        def _():
            self.inbound[2] = jnp.zeros_like(self.inbound[2])

    def whole(self, total, part):
        last = jnp.where(self.line.outer, 5, 4)
        return (
            total[part, :]
            + self.inbound[2, part, :].astype(F32)
            + self.inbound[last, part, :].astype(F32)
        )


def mlp_back_kernel(
    lhs, rhs, acts, down, hidden, cot, mlp_in, lg, down_bias,
    grad_out, small_out, rows_out, grad_up, grad_down,
    outbound, inbound, total, cot_rows, own, sums, blocks, stage,
    sems, gather_sems, local_sems, load_sems, store_sems,
):
    chunk, feats = total.shape
    line = Line(chunk)
    mine = pl.ds(pl.multiple_of(line.me * chunk, chunk), chunk)
    fetch = pltpu.make_async_copy(cot.at[mine, :], cot_rows, local_sems.at[0])
    fetch.start()
    line.barrier()
    first = LineSum(line, lhs, rhs, outbound, inbound.at[0], sems.at[0], 0)
    second = LineSum(line, acts, down, outbound, inbound.at[1], sems.at[1], 0)
    first.clear()
    second.clear()

    @pl.when(line.outer)
    def _():
        first.send_inward()

    first.own(total)
    sums[...] = jnp.zeros_like(sums)
    weight_product(mlp_in, lhs, grad_up, blocks, stage, load_sems, store_sems)

    @pl.when(line.inner)
    def _():
        first.send_across(0)
        first.send_across(1)
        first.send_outward()

    weight_product(cot, acts, grad_down, blocks, stage, load_sems, store_sems)
    fetch.wait()
    first.arrive()

    def back(part):
        grads = first.whole(total, part)
        step, normed = norm_back(hidden[part, :], grads, lg[...])
        low = (cot_rows[part, :].astype(F32) + step).astype(BF)
        own[part, :] = low
        sums[0] += fold(grads * normed)
        sums[1] += fold(grads)
        sums[2] += fold(low.astype(F32))

    rows_loop(chunk, 64, back)
    local = pltpu.make_async_copy(own, grad_out.at[mine, :], local_sems.at[1])
    local.start()
    first.sent()

    def chunk_copy(number, index, device, source=None):
        rows = grad_out.at[line.at(number), :]
        return remote(rows if source is None else source, rows, gather_sems, index, device)

    @pl.when(line.outer)
    def _():
        onward = chunk_copy(0, 0, line.up, own)
        onward.start()
        second.send_inward()
        second.own(total)
        for number in range(1, RING):
            chunk_copy(number, 2 + number, line.up).wait_recv()
        onward.wait_send()

    @pl.when(line.inner)
    def _():
        inward = [chunk_copy(1, 1, line.up, own), chunk_copy(1, 3, line.down, own)]
        for copy in inward:
            copy.start()
        second.own(total)
        chunk_copy(0, 0, line.up).wait_recv()
        relay = chunk_copy(0, 2, line.up)
        relay.start()
        chunk_copy(2, 1, line.up).wait_recv()
        near = chunk_copy(2, 4, line.down)
        near.start()
        second.send_across(0)
        chunk_copy(3, 2, line.up).wait_recv()
        far = chunk_copy(3, 5, line.down)
        far.start()
        second.send_across(1)
        second.send_outward()
        for copy in inward + [relay, near, far]:
            copy.wait_send()

    for i in range(3):
        small_out[i : i + 1, :] = jnp.sum(sums[i], axis=0, keepdims=True)
    second.arrive()

    def add(part):
        value = hidden[part, :] + (second.whole(total, part) + down_bias[...])
        rows_out[part, :] = value.astype(BF)

    rows_loop(chunk, 64, add)
    second.sent()
    local.wait()


def mlp_back(lhs, rhs, acts, down, hidden, cot, mlp_in, lg, down_bias):
    rows, feats = cot.shape
    width = lhs.shape[1]
    chunk = rows // RING
    block = 256
    return pl.pallas_call(
        mlp_back_kernel,
        in_specs=[VMEM, VMEM, VMEM, VMEM, VMEM, ANY, ANY, VMEM, VMEM],
        out_specs=[ANY, VMEM, VMEM, ANY, ANY],
        out_shape=[
            jax.ShapeDtypeStruct((rows, feats), BF),
            jax.ShapeDtypeStruct((3, feats), F32),
            jax.ShapeDtypeStruct((chunk, feats), BF),
            jax.ShapeDtypeStruct((feats, width), BF),
            jax.ShapeDtypeStruct((feats, width), BF),
        ],
        scratch_shapes=[
            pltpu.VMEM((3, chunk, feats), BF),
            pltpu.VMEM((2, 6, chunk, feats), BF),
            pltpu.VMEM((chunk, feats), F32),
            pltpu.VMEM((chunk, feats), BF),
            pltpu.VMEM((chunk, feats), BF),
            pltpu.VMEM((3, 8, feats), F32),
            pltpu.VMEM((2, rows, block), BF),
            pltpu.VMEM((2, block, width), BF),
            pltpu.SemaphoreType.DMA((2, 2, 6)),
            pltpu.SemaphoreType.DMA((2, 6)),
            pltpu.SemaphoreType.DMA((2,)),
            pltpu.SemaphoreType.DMA((2,)),
            pltpu.SemaphoreType.DMA((2,)),
        ],
        compiler_params=params(60, 1),
        cost_estimate=cost(175),
        name="mlp_back",
    )(lhs, rhs, acts, down, hidden, cot, mlp_in, lg, down_bias)


class Spread:
    def __init__(self, ring, slots, sems, base, source):
        half = slots.shape[1] // 2
        mine = slots.at[ring.me]
        self.first = [
            remote(source, mine, sems, base, ring.right),
            remote(source, mine, sems, base + 1, ring.left),
        ]
        up = slots.at[ring.left, pl.ds(0, half), :]
        down = slots.at[ring.right, pl.ds(half, half), :]
        self.second = [
            remote(up, up, sems, base + 2, ring.right),
            remote(down, down, sems, base + 3, ring.left),
        ]

    def begin(self):
        for copy in self.first:
            copy.start()

    def relay(self):
        for arrived, onward in zip(self.first, self.second):
            arrived.wait_recv()
            onward.start()

    def arrive(self):
        for copy in self.second:
            copy.wait_recv()

    def finish(self):
        for copy in self.first + self.second:
            copy.wait_send()


def streams_back_kernel(
    first, lin, weight, hist, mix, lg, normed_in, own_rows,
    grads_out, small_out, products, rows_out,
    slots, weights, total, layers, stage, sums, blocks, tiles_out,
    sems, weight_sems, layer_sem, stage_sems, own_sems, load_sems, store_sems,
):
    tile, feats = total.shape
    depth = layers.shape[0]
    whole_load = pltpu.make_async_copy(hist, layers, layer_sem)
    whole_load.start()
    rows, width = lin.shape[1], lin.shape[2]
    tiles = rows // tile
    ring = Ring(rows)

    def fetch(stream):
        return weight_copies(
            weight, weights.at[stream % 2], weight_sems.at[stream % 2], stream
        )

    local = [
        pltpu.make_async_copy(lin.at[i], slots.at[i, ring.me], own_sems.at[i])
        for i in range(2)
    ]
    local.append(
        pltpu.make_async_copy(own_rows, rows_out.at[ring.me], own_sems.at[2])
    )
    for copy in local:
        copy.start()
    for stream in range(2):
        fetch(stream)(lambda copy: copy.start())
    sums[...] = jnp.zeros_like(sums)
    ring.barrier()
    spreads = [Spread(ring, slots.at[i], sems.at[i], 0, lin.at[i]) for i in range(2)]
    spreads.append(Spread(ring, rows_out, sems.at[2], 0, own_rows))

    def write_out(stream, index, slot):
        part = pl.ds(pl.multiple_of(index * tile, tile), tile)
        return pltpu.make_async_copy(
            stage.at[slot], grads_out.at[stream, part, :], stage_sems.at[slot]
        )

    def flush(stream):
        for index in range(tiles):
            write_out(stream, index, index).wait()

    def compute(stream):
        fetch(stream)(lambda copy: copy.wait())
        if stream == 0:
            whole_load.wait()
        else:
            flush(stream - 1)

        def one(index, carry):
            part = pl.ds(pl.multiple_of(index * tile, tile), tile)

            gathered = first if stream == 0 else slots.at[stream - 1]
            ring_product(gathered, weights.at[stream % 2], part, total)
            def back(sub):
                grads = total[sub, :]
                here = pl.ds(pl.multiple_of(index * tile + sub.start, 64), 64)
                latest = layers[depth - 1, here, :].astype(F32)
                share = mix[here, :]
                mixture = latest
                for j in range(depth):
                    col = stream * depth + j
                    mixture = mixture + share[:, col : col + 1] * layers[j, here, :].astype(F32)
                step, normed = norm_back(mixture, grads, lg[stream : stream + 1, :])
                stage[index, sub, :] = step.astype(BF)
                sums[stream, 0] += fold(grads * normed)
                sums[stream, 1] += fold(grads)

            rows_loop(tile, 64, back)
            write_out(stream, index, index).start()
            return carry

        lax.fori_loop(0, tiles, one, 0)
        if stream == 0:
            fetch(2)(lambda copy: copy.start())

    for copy in local:
        copy.wait()
    spreads[0].begin()
    compute(0)
    spreads[0].relay()
    for i in range(2):
        source, target = normed_in.at[i + 1], products.at[:, pl.ds(i * width, width)]
        weight_product(source, lin.at[i], target, blocks, tiles_out, load_sems, store_sems)
    spreads[0].arrive()
    spreads[1].begin()
    compute(1)
    spreads[1].relay()
    spreads[1].arrive()
    spreads[2].begin()
    compute(2)
    spreads[2].relay()
    spreads[2].arrive()
    flush(2)
    for i in range(3):
        for j in range(2):
            small_out[j, i : i + 1, :] = jnp.sum(sums[i, j], axis=0, keepdims=True)
    for spread in spreads:
        spread.finish()


def streams_back(first, lin, weight, hist, mix, lg, normed, own_rows):
    depth, rows, feats = hist.shape
    width = lin.shape[2]
    tile = min(256, rows)
    return pl.pallas_call(
        streams_back_kernel,
        in_specs=[VMEM, VMEM, ANY, ANY, VMEM, VMEM, ANY, ANY],
        out_specs=[ANY, VMEM, ANY, ANY],
        out_shape=[
            jax.ShapeDtypeStruct((3, rows, feats), BF),
            jax.ShapeDtypeStruct((2, 3, feats), F32),
            jax.ShapeDtypeStruct((feats, 2 * width), BF),
            jax.ShapeDtypeStruct((RING,) + own_rows.shape, BF),
        ],
        scratch_shapes=[
            pltpu.VMEM((2, RING, rows, width), BF),
            pltpu.VMEM((2, RING, feats, width), BF),
            pltpu.VMEM((tile, feats), F32),
            pltpu.VMEM((depth, rows, feats), BF),
            pltpu.VMEM((rows // tile, tile, feats), BF),
            pltpu.VMEM((3, 2, 8, feats), F32),
            pltpu.VMEM((2, rows, 256), BF),
            pltpu.VMEM((2, 256, width), BF),
            pltpu.SemaphoreType.DMA((3, 2, 4)),
            pltpu.SemaphoreType.DMA((2, weight.shape[0])),
            pltpu.SemaphoreType.DMA,
            pltpu.SemaphoreType.DMA((rows // tile,)),
            pltpu.SemaphoreType.DMA((3,)),
            pltpu.SemaphoreType.DMA((2,)),
            pltpu.SemaphoreType.DMA((2,)),
        ],
        compiler_params=params(60, 2),
        cost_estimate=cost(240),
        name="streams_back",
    )(first, lin, weight, hist, mix, lg, normed, own_rows)


def small_kernel(seqs, owners, ours, share, out, share_out, near, all_ours, all_shares, near_sems, sems):
    ring = Ring(2)
    near_rows = near.shape[1]
    rank, peers, places = owner_places(seqs, owners)
    mates = [ring.right, ring.far, ring.left]
    enter(places + [{"tensor": z} for z in mates])

    near[ring.me] = ours[0:near_rows, :]
    shares = [
        push(share.at[p], all_shares.at[rank], sems.at[0], k, place)
        for k, (p, place) in enumerate(zip(peers, places))
    ]
    first = [
        push(near.at[ring.me], near.at[ring.me], near_sems, k, {"tensor": z})
        for k, z in enumerate(mates)
    ]
    for copy in first + shares:
        copy.start()
    for copy in first:
        copy.wait()
    all_ours[rank, 0:near_rows, :] = (near[0] + near[1]) + (near[2] + near[3])
    all_ours[rank, near_rows:, :] = ours[near_rows:, :]
    all_shares[rank] = share[rank]
    second = [
        push(all_ours.at[rank], all_ours.at[rank], sems.at[1], k, place)
        for k, place in enumerate(places)
    ]
    for copy in second:
        copy.start()
    for copy in shares + second:
        copy.wait()
    total, part = all_ours[0], all_shares[0]
    for index in range(1, owners):
        total += all_ours[index]
        part += all_shares[index]
    out[...] = total
    share_out[...] = part


def small_sums(ours, share, seqs):
    owners = share.shape[0]
    rows, feats = ours.shape
    return pl.pallas_call(
        functools.partial(small_kernel, seqs, owners),
        in_specs=[VMEM, VMEM],
        out_specs=[VMEM, VMEM],
        out_shape=[
            jax.ShapeDtypeStruct(ours.shape, F32),
            jax.ShapeDtypeStruct(share.shape[1:], F32),
        ],
        scratch_shapes=[
            pltpu.VMEM((RING, 8, feats), F32),
            pltpu.VMEM((owners,) + ours.shape, F32),
            pltpu.VMEM(share.shape, F32),
            pltpu.SemaphoreType.DMA((2, 3)),
            pltpu.SemaphoreType.DMA((2, 2, owners - 1)),
        ],
        compiler_params=params(40, 4),
        cost_estimate=cost(12),
        name="small_sums",
    )(ours, share)


def mlp_kernel(mlp_in, cot, up, down, bias, act_out, grad_out, sum_out):
    lin = dot(mlp_in[...], up[...]) + bias[...]
    grad_act = dot(cot[...], down[...])
    cdf = normal_cdf(lin)
    act_out[...] = (lin * cdf).astype(BF)
    grad = (grad_act * gelu_slope(lin, cdf)).astype(BF)
    grad_out[...] = grad

    @pl.when(pl.program_id(1) == 0)
    def _():
        sum_out[...] = jnp.zeros_like(sum_out)

    sum_out[...] += jnp.sum(grad.astype(F32), axis=0, keepdims=True)


def mlp(mlp_in, cot, up, down, bias):
    rows, feats = mlp_in.shape
    width = up.shape[1]
    tile, cols = min(256, rows), 512
    return pl.pallas_call(
        mlp_kernel,
        grid=(width // cols, rows // tile),
        in_specs=[
            pl.BlockSpec((tile, feats), lambda n, r: (r, 0)),
            pl.BlockSpec((tile, feats), lambda n, r: (r, 0)),
            pl.BlockSpec((feats, cols), lambda n, r: (0, n)),
            pl.BlockSpec((feats, cols), lambda n, r: (0, n)),
            pl.BlockSpec((1, cols), lambda n, r: (0, n)),
        ],
        out_specs=[
            pl.BlockSpec((tile, cols), lambda n, r: (r, n)),
            pl.BlockSpec((tile, cols), lambda n, r: (r, n)),
            pl.BlockSpec((1, cols), lambda n, r: (0, n)),
        ],
        out_shape=[
            jax.ShapeDtypeStruct((rows, width), BF),
            jax.ShapeDtypeStruct((rows, width), BF),
            jax.ShapeDtypeStruct((1, width), F32),
        ],
        compiler_params=params(48),
        cost_estimate=cost(25),
        name="mlp",
    )(mlp_in, cot, up, down, bias)


def turn_back_kernel(dkv, tables, dk_out, sum_out):
    tabs = (tables[0], tables[1], tables[2])
    for head in range(dk_out.shape[1] // HEAD_DIM):
        cols = slice(head * HEAD_DIM, (head + 1) * HEAD_DIM)
        dk_out[:, cols] = turn(dkv[0, :, cols].astype(F32), tabs, -1.0).astype(BF)


def last_kernel(
    hist, streams, attn, mix, pre, gain, w1, w2, grad_out, gain_out, w1_out, w2_out,
    normed, grad_mix, grad_normed, gain_sum,
):
    depth, rows, feats = hist.shape
    step_index = pl.program_id(0)

    @pl.when(step_index == 0)
    def _():
        gain_sum[...] = jnp.zeros_like(gain_sum)
        w1_out[...] = jnp.zeros_like(w1_out)
        w2_out[...] = jnp.zeros_like(w2_out)

    def reduce(part):
        layers = [hist[j, part, :].astype(F32) for j in range(depth)]
        latest = layers[depth - 1]
        scale = lax.rsqrt(mean_last(latest * latest) + RMS_EPSILON)
        normed[part, :] = (latest * scale * gain[...]).astype(BF)
        for m in range(STREAMS):
            grads = (attn[part, :] if m == STREAMS - 1 else streams[m, part, :]).astype(F32)
            for j in range(depth):
                at = m * depth + j
                grad_mix[part, at : at + 1] = jnp.sum(grads * layers[j], axis=-1, keepdims=True)

    rows_loop(rows, 64, reduce)
    pre_value = pre[...]
    cdf = normal_cdf(pre_value)
    grads = grad_mix[...]
    w2_out[...] += dot(pre_value * cdf, grads, TN, EXACT)
    grad_act = dot(grads, w2[...], NT, EXACT)
    grad_pre = (grad_act * gelu_slope(pre_value, cdf)).astype(BF)
    w1_out[...] += dot(grad_pre, normed[...], TN)
    grad_normed[...] = dot(grad_pre, w1[...], NT)

    def write(part):
        layers = [hist[depth - 1, part, :].astype(F32)]
        latest = layers[0]
        scale = lax.rsqrt(mean_last(latest * latest) + RMS_EPSILON)
        value = grad_normed[part, :]
        gain_sum[...] += fold(value * latest * scale)
        value = value * gain[...]
        back = scale * value - latest * (scale * scale * scale * mean_last(latest * value))
        weight = mix[part, :]
        grads = [streams[m, part, :].astype(F32) for m in range(STREAMS - 1)]
        grads.append(attn[part, :].astype(F32))
        for j in range(depth):
            total = weight[:, j : j + 1] * grads[0]
            for m in range(1, STREAMS):
                at = m * depth + j
                total = total + weight[:, at : at + 1] * grads[m]
            if j == depth - 1:
                total = total + (grads[0] + grads[1] + grads[2] + grads[3]) + back
            grad_out[j, part, :] = total

    rows_loop(rows, 64, write)

    @pl.when(step_index == pl.num_programs(0) - 1)
    def _():
        gain_out[...] = jnp.sum(gain_sum[...], axis=0, keepdims=True)


def last(hist, streams, attn, mix, pre, gain, w1, w2):
    depth, rows, feats = hist.shape
    hidden = w1.shape[1]
    tile = min(64, rows)
    full = lambda shape: pl.BlockSpec(shape, lambda i: (0,) * len(shape))
    return pl.pallas_call(
        last_kernel,
        grid=(rows // tile,),
        in_specs=[
            pl.BlockSpec((depth, tile, feats), lambda i: (0, i, 0)),
            pl.BlockSpec((3, tile, feats), lambda i: (0, i, 0)),
            pl.BlockSpec((tile, feats), lambda i: (i, 0)),
            pl.BlockSpec((tile, STREAMS * depth), lambda i: (i, 0)),
            pl.BlockSpec((tile, hidden), lambda i: (i, 0)),
            full((1, feats)),
            full(w1.shape),
            full(w2.shape),
        ],
        out_specs=[
            pl.BlockSpec((depth, tile, feats), lambda i: (0, i, 0)),
            full((1, feats)),
            full((hidden, feats)),
            full(w2.shape),
        ],
        out_shape=[
            jax.ShapeDtypeStruct((depth, rows, feats), F32),
            jax.ShapeDtypeStruct((1, feats), F32),
            jax.ShapeDtypeStruct((hidden, feats), F32),
            jax.ShapeDtypeStruct(w2.shape, F32),
        ],
        scratch_shapes=[
            pltpu.VMEM((tile, feats), BF),
            pltpu.VMEM((tile, STREAMS * depth), F32),
            pltpu.VMEM((tile, feats), F32),
            pltpu.VMEM((8, feats), F32),
        ],
        compiler_params=params(40),
        cost_estimate=cost(30),
        name="last",
    )(hist, streams, attn, mix, pre, gain.reshape(1, feats), w1, w2)


def turn_back(dkv, tables):
    _, rows, width = dkv.shape
    return pl.pallas_call(
        lambda d, t, o: turn_back_kernel(d, t, o, None),
        grid=(1,),
        in_specs=[
            pl.BlockSpec((1, rows, width), lambda i: (0, 0, 0)),
            pl.BlockSpec(tables.shape, lambda i: (0, 0, 0)),
        ],
        out_specs=pl.BlockSpec((rows, width), lambda i: (0, 0)),
        out_shape=jax.ShapeDtypeStruct((rows, width), BF),
        compiler_params=params(40),
        cost_estimate=cost(3),
        name="turn_back",
    )(dkv, tables)


def row_product(left, right):
    return dot(left, right, TN).astype(BF)


def shards(
    history,
    positions,
    lengths,
    cotangent,
    mix_gain,
    mix_w1,
    mix_w2,
    ln_gain,
    ln_bias,
    qkv_weight,
    qkv_bias,
    out_weight,
    out_bias,
    up_weight,
    up_bias,
    down_weight,
    down_bias,
):
    depth, slots, block_len, feats = history.shape
    rows = slots * block_len
    width = qkv_weight.shape[2]
    heads = width // HEAD_DIM
    owners = ("dp", "seq")
    layers = history.reshape(depth, rows, feats)

    seqs = lax.axis_size("seq")
    count = lax.axis_size("dp") * seqs
    tie = lax.optimization_barrier
    gather = functools.partial(lax.all_gather, axis_name=owners, axis=0)
    w_kv = gather(jnp.concatenate([qkv_weight[1], qkv_weight[2]], axis=1), tiled=True)
    w_q = gather(qkv_weight[0], tiled=True)

    offset = lax.axis_index("seq") * block_len
    query_place = offset + jnp.arange(block_len, dtype=jnp.int32)
    valid = (query_place[None, :] < lengths[:, None]).reshape(rows, 1)
    cot = jnp.where(valid, cotangent.reshape(rows, feats), jnp.zeros((), BF))
    scalars = jnp.concatenate([lengths, offset[None].astype(jnp.int32)])
    tables = rotary_tables(positions.reshape(rows))

    normed, resid, mix, pre, w_mix = front(
        layers, mix_gain, mix_w1, mix_w2, ln_gain, ln_bias, seqs, count
    )
    w_up = gather(up_weight, tiled=True)
    kv = project(normed, w_kv, qkv_bias[1:], tables, 1)
    kv_all, ring_out, ring_qkv = share(kv, out_weight, qkv_weight.reshape(-1, width), seqs)
    q = project(normed, w_q, qkv_bias[:1], tables, 0)[0]
    w_out_all = gather(ring_out)
    kv_all = kv_all.reshape(seqs, 2, slots, block_len, width)
    attn_vals = attend(scalars, q, kv_all, heads).reshape(rows, width)
    attn_vals, w_up, down_weight = tie((attn_vals, w_up, down_weight))
    w_down = gather(down_weight, tiled=True)
    vals_all = spread_vals(attn_vals)
    vals_all, ring_qkv = tie((vals_all, ring_qkv))
    w_qkv = gather(ring_qkv.reshape((RING,) + qkv_weight.shape))
    hidden, mlp_in = attn_out(
        vals_all, w_out_all, resid, out_bias[None, :], ln_gain[3:4], ln_bias[3:4]
    )
    w_out = lax.dynamic_index_in_dim(
        w_out_all, lax.axis_index("tensor"), 1, keepdims=False
    ).reshape(feats, width)
    up_act, grad_up, grad_up_bias = mlp(mlp_in, cot, w_up, w_down, up_bias[None, :])
    scatter = functools.partial(
        lax.psum_scatter, axis_name=owners, scatter_dimension=0, tiled=True
    )
    grad_attn, small_mlp, out_rows, grad_upw, grad_down = mlp_back(
        grad_up, w_up, up_act, w_down, hidden, cot, mlp_in, ln_gain[3:4], down_bias[None, :]
    )
    grad_vals = dot(grad_attn, w_out).astype(BF)
    dq, dkv = attend_back(scalars, q, kv_all, grad_vals, tables, heads)
    w_qkv, dq, dkv = tie((w_qkv, dq, dkv))
    dkv_own = lax.psum_scatter(dkv, "seq", scatter_dimension=0).reshape(2, rows, width)
    dq = dq.reshape(rows, width)
    dq_all, grad_qo = spread_dq(dq, normed, grad_attn, attn_vals)
    dq_all, dkv_own, grad_down, grad_upw, grad_qo = tie(
        (dq_all, dkv_own, grad_down, grad_upw, grad_qo)
    )
    shard_down, shard_up, shard_qo = scatter(grad_down), scatter(grad_upw), scatter(grad_qo)
    lin_kv = jnp.stack([turn_back(dkv_own, tables), dkv_own[1]])
    grads, small_qkv, grad_kv, layer_out = streams_back(
        dq_all, lin_kv, w_qkv, layers, mix, ln_gain, normed, out_rows
    )
    shard_down, shard_up, shard_qo, grads, grad_kv = tie(
        (shard_down, shard_up, shard_qo, grads, grad_kv)
    )
    shard_kv = scatter(grad_kv)
    shard_down, shard_up = shard_down.astype(F32), shard_up.astype(F32)
    shard_qkv = jnp.stack([shard_qo[:, :width], shard_kv[:, :width], shard_kv[:, width:]])
    shard_qkv, shard_out = shard_qkv.astype(F32), shard_qo[:, width:].astype(F32)
    grad_layers, grad_gain, grad_w1, grad_w2 = last(
        layers, grads, grad_attn, mix, pre, mix_gain, w_mix, mix_w2
    )
    grad_history = grad_layers.reshape(depth, slots, block_len, feats)
    hidden_count = mix_w1.shape[1]
    w1_share = grad_w1.reshape(hidden_count, count, feats // count).transpose(1, 0, 2)

    def as_row(values):
        flat = values.reshape(1, -1)
        return jnp.pad(flat, ((0, 0), (0, feats - flat.shape[1])))

    grad_qkv_bias = jnp.concatenate(
        [jnp.sum(dq.astype(F32), axis=0)[None], jnp.sum(lin_kv.astype(F32), axis=1)]
    )
    ours = jnp.concatenate(
        [small_mlp, jnp.zeros((5, feats), F32), small_qkv.reshape(6, feats)]
        + [
            as_row(values)
            for values in (
                grad_gain, grad_w2, grad_qkv_bias, grad_up_bias, jnp.sum(cot.astype(F32), axis=0)
            )
        ]
        + [jnp.zeros((5, feats), F32)],
        axis=0,
    )
    summed, shard_w1 = small_sums(ours, w1_share.reshape(count, -1, 128), seqs)
    return (
        layer_out.reshape(slots, block_len, feats),
        grad_history,
        summed[14],
        shard_w1.reshape(hidden_count, feats // count).T,
        summed[15, : grad_w2.size].reshape(grad_w2.shape),
        jnp.concatenate([summed[8:11], summed[0:1]], axis=0),
        jnp.concatenate([summed[11:14], summed[1:2]], axis=0),
        shard_qkv,
        summed[16, : grad_qkv_bias.size].reshape(grad_qkv_bias.shape),
        shard_out,
        summed[2],
        shard_up,
        summed[17, : up_bias.size],
        shard_down,
        summed[18],
    )


def solution(mesh):
    in_specs = (
        P(None, "dp", "seq", None),
        P("dp", "seq"),
        P("dp"),
        P("dp", "seq", None),
        P(),
        P(("dp", "seq"), None),
        P(),
        P(),
        P(),
        P(None, ("dp", "seq"), "tensor"),
        P(None, "tensor"),
        P(("dp", "seq"), "tensor"),
        P(),
        P(("dp", "seq"), "tensor"),
        P("tensor"),
        P(("dp", "seq"), "tensor"),
        P(),
    )
    out_specs = (
        P("dp", "seq", None),
        P(None, "dp", "seq", None),
        P(),
        P(("dp", "seq"), None),
        P(),
        P(),
        P(),
        P(None, ("dp", "seq"), "tensor"),
        P(None, "tensor"),
        P(("dp", "seq"), "tensor"),
        P(),
        P(("dp", "seq"), "tensor"),
        P("tensor"),
        P(("dp", "seq"), "tensor"),
        P(),
    )
    return jax.shard_map(shards, mesh=mesh, in_specs=in_specs, out_specs=out_specs, check_vma=False)
```

```python
import functools
import math

import jax
import jax.numpy as jnp
from jax import lax
from jax.experimental import pallas as pl
from jax.experimental.pallas import tpu as pltpu
from jax.sharding import PartitionSpec as P

HEAD_DIM = 128
ROT = 32
STREAMS = 4
EXACT = lax.Precision.HIGHEST
RMS_EPSILON = 1e-06
NORM_EPSILON = 1e-05
BF = jnp.bfloat16
F32 = jnp.float32
MESH = pl.DeviceIdType.MESH
ANY = pl.BlockSpec(memory_space=pl.ANY)
VMEM = pl.BlockSpec(memory_space=pltpu.VMEM)
RING = 4
NN = (((1,), (0,)), ((), ()))
NT = (((1,), (1,)), ((), ()))
TN = (((0,), (0,)), ((), ()))


def dot(left, right, dims=NN, precision=None):
    return lax.dot_general(left, right, dims, precision=precision, preferred_element_type=F32)


def normal_cdf(values):
    return 0.5 * (1.0 + lax.erf(values * math.sqrt(0.5)))


def gelu_slope(values, cdf):
    return cdf + values * (jnp.exp(-0.5 * values * values) * (1.0 / math.sqrt(2.0 * math.pi)))


def mean_last(values):
    return jnp.mean(values, axis=-1, keepdims=True)


def rows_loop(total, step, body):
    def one(index, carry):
        body(pl.ds(pl.multiple_of(index * step, step), step))
        return carry

    lax.fori_loop(0, total // step, one, 0)


def params(limit_mib, collective_id=None):
    if collective_id is None:
        return pltpu.CompilerParams(vmem_limit_bytes=limit_mib << 20)
    return pltpu.CompilerParams(
        vmem_limit_bytes=limit_mib << 20, collective_id=collective_id, has_side_effects=True
    )


def cost(micros):
    return pl.CostEstimate(flops=0, bytes_accessed=int(micros * 3.0e6), transcendentals=0)


def owner_places(seqs, owners):
    rank = lax.axis_index("dp") * seqs + lax.axis_index("seq")
    peers = [lax.rem(rank + k, owners) for k in range(1, owners)]
    return rank, peers, [{"dp": lax.div(p, seqs), "seq": lax.rem(p, seqs)} for p in peers]


def push(source, target, sems, index, place):
    return pltpu.make_async_remote_copy(
        src_ref=source,
        dst_ref=target,
        send_sem=sems.at[0, index],
        recv_sem=sems.at[1, index],
        device_id=place,
        device_id_type=MESH,
    )


def enter(places):
    gate = pltpu.get_barrier_semaphore()
    for place in places:
        pl.semaphore_signal(gate, inc=1, device_id=place, device_id_type=MESH)
    pl.semaphore_wait(gate, len(places))


def front_kernel(
    seqs, owners,
    hist, gain, w1, w2, lg, lb, normed_out, resid_out, mix_out, pre_out, w1_out,
    scratch, w1_all, w1_sems,
):
    depth, rows, _ = hist.shape
    index = pl.program_id(0)
    rank, _, places = owner_places(seqs, owners)
    w1_copies = [push(w1, w1_all.at[rank], w1_sems, k, p) for k, p in enumerate(places)]

    @pl.when(index == 0)
    def _():
        enter(places)
        for copy in w1_copies:
            copy.start()
        w1_all[rank] = w1[...]
        for copy in w1_copies:
            copy.wait()
        w1_out[...] = w1_all[...].reshape(w1_out.shape)

    def rms(part):
        wide = hist[depth - 1, part, :].astype(F32)
        scale = lax.rsqrt(mean_last(wide * wide) + RMS_EPSILON)
        scratch[part, :] = (wide * scale * gain[...]).astype(BF)

    rows_loop(rows, 16, rms)
    pre = dot(scratch[...], w1_out[...])
    pre_out[...] = pre
    mix_out[...] = dot(pre * normal_cdf(pre), w2[...], precision=EXACT)

    def combine(part):
        layers = [hist[j, part, :].astype(F32) for j in range(depth)]
        mix = mix_out[part, :]
        for m in range(STREAMS):
            running = layers[depth - 1]
            for j in range(depth):
                running = running + mix[:, m * depth + j : m * depth + j + 1] * layers[j]
            if m == STREAMS - 1:
                resid_out[part, :] = running
            else:
                centred = running - mean_last(running)
                inverse = lax.rsqrt(mean_last(centred * centred) + NORM_EPSILON)
                normed = centred * inverse * lg[m : m + 1, :] + lb[m : m + 1, :]
                normed_out[m, part, :] = normed.astype(BF)

    rows_loop(rows, 32, combine)


def front(layers, gain, w1, w2, lg, lb, seqs, owners):
    depth, rows, feats = layers.shape
    tile = min(128, rows)
    hidden = w1.shape[1]
    full = lambda shape: pl.BlockSpec(shape, lambda i: (0,) * len(shape))
    return pl.pallas_call(
        functools.partial(front_kernel, seqs, owners),
        grid=(rows // tile,),
        in_specs=[
            pl.BlockSpec((depth, tile, feats), lambda i: (0, i, 0)),
            full((1, feats)),
            full(w1.shape),
            full(w2.shape),
            full(lg.shape),
            full(lb.shape),
        ],
        out_specs=[
            pl.BlockSpec((3, tile, feats), lambda i: (0, i, 0)),
            pl.BlockSpec((tile, feats), lambda i: (i, 0)),
            pl.BlockSpec((tile, STREAMS * depth), lambda i: (i, 0)),
            pl.BlockSpec((tile, hidden), lambda i: (i, 0)),
            full((feats, hidden)),
        ],
        out_shape=[
            jax.ShapeDtypeStruct((3, rows, feats), BF),
            jax.ShapeDtypeStruct((rows, feats), F32),
            jax.ShapeDtypeStruct((rows, STREAMS * depth), F32),
            jax.ShapeDtypeStruct((rows, hidden), F32),
            jax.ShapeDtypeStruct((feats, hidden), BF),
        ],
        scratch_shapes=[
            pltpu.VMEM((tile, feats), BF),
            pltpu.VMEM((owners,) + w1.shape, BF),
            pltpu.SemaphoreType.DMA((2, owners - 1)),
        ],
        compiler_params=params(48, 5),
        cost_estimate=cost(45),
        name="front",
    )(layers, gain.reshape(1, feats), w1, w2, lg, lb)


def turn(values, tables, sign):
    cosines, low, high = tables
    return values * cosines + sign * (
        pltpu.roll(values, HEAD_DIM - ROT // 2, 1) * low + pltpu.roll(values, ROT // 2, 1) * high
    )


def rotary_tables(positions):
    exponents = jnp.arange(0, ROT, 2).astype(F32) / ROT
    inverse = jnp.power(10000.0, -exponents)
    phases = positions.astype(F32)[:, None] * inverse[None, :]
    cosines, sines = jnp.cos(phases), jnp.sin(phases)
    rows, half = phases.shape
    ones = jnp.ones((rows, HEAD_DIM - 2 * half), F32)
    none = jnp.zeros((rows, HEAD_DIM - 2 * half), F32)
    zero = jnp.zeros((rows, half), F32)
    return jnp.stack(
        [
            jnp.concatenate([cosines, cosines, ones], axis=1),
            jnp.concatenate([-sines, zero, none], axis=1),
            jnp.concatenate([zero, sines, none], axis=1),
        ]
    )


def proj_kernel(first, lhs, weight, bias, tables, out):
    branch = pl.program_id(0) + first
    value = dot(lhs[0], weight[...]) + bias[0]

    @pl.when(branch < 2)
    def _():
        tabs = (tables[0], tables[1], tables[2])
        for head in range(value.shape[1] // HEAD_DIM):
            cols = slice(head * HEAD_DIM, (head + 1) * HEAD_DIM)
            out[0, :, cols] = turn(value[:, cols], tabs, 1.0).astype(BF)

    @pl.when(branch >= 2)
    def _():
        out[0] = value.astype(BF)


def project(normed, weight, bias, tables, first):
    _, rows, feats = normed.shape
    count, width = bias.shape
    tile = min(256, rows)
    return pl.pallas_call(
        functools.partial(proj_kernel, first),
        grid=(count, rows // tile),
        in_specs=[
            pl.BlockSpec((1, tile, feats), lambda b, r: (b + first, r, 0)),
            pl.BlockSpec((feats, width), lambda b, r: (0, b)),
            pl.BlockSpec((1, 1, width), lambda b, r: (b, 0, 0)),
            pl.BlockSpec((3, tile, HEAD_DIM), lambda b, r: (0, r, 0)),
        ],
        out_specs=pl.BlockSpec((1, tile, width), lambda b, r: (b, r, 0)),
        out_shape=jax.ShapeDtypeStruct((count, rows, width), BF),
        compiler_params=params(40),
        cost_estimate=cost(4 * count),
        name="project",
    )(normed, weight, bias.reshape(count, 1, width), tables)


def share_kernel(
    kv, shard_out, shard_qkv, kv_out, ring_out, ring_qkv, sems, ring_sems, own_sems
):
    seqs = kv_out.shape[0]
    me = lax.axis_index("seq")
    ring = Ring(16)
    places = [{"seq": lax.rem(me + k, seqs)} for k in range(1, seqs)]
    local = [
        pltpu.make_async_copy(kv, kv_out.at[me], own_sems.at[0]),
        pltpu.make_async_copy(shard_out, ring_out.at[ring.me], own_sems.at[1]),
        pltpu.make_async_copy(shard_qkv, ring_qkv.at[ring.me], own_sems.at[2]),
    ]
    for copy in local:
        copy.start()
    enter(places + [{"tensor": ring.left}, {"tensor": ring.right}])
    copies = [push(kv, kv_out.at[me], sems, k, place) for k, place in enumerate(places)]
    spreads = [
        Spread(ring, slots, ring_sems.at[i], 0, source)
        for i, (slots, source) in enumerate(((ring_out, shard_out), (ring_qkv, shard_qkv)))
    ]
    for copy in copies:
        copy.start()
    for spread in spreads:
        spread.begin()

    for spread in spreads:
        spread.relay()
    for copy in copies:
        copy.wait()
    for spread in spreads:
        spread.arrive()
        spread.finish()
    for copy in local:
        copy.wait()


def share(kv, shard_out, shard_qkv, seqs):
    return pl.pallas_call(
        share_kernel,
        in_specs=[ANY, ANY, ANY],
        out_specs=[ANY, ANY, ANY],
        out_shape=[
            jax.ShapeDtypeStruct((seqs,) + kv.shape, BF),
            jax.ShapeDtypeStruct((RING,) + shard_out.shape, BF),
            jax.ShapeDtypeStruct((RING,) + shard_qkv.shape, BF),
        ],
        scratch_shapes=[
            pltpu.SemaphoreType.DMA((2, seqs - 1)),
            pltpu.SemaphoreType.DMA((2, 2, 4)),
            pltpu.SemaphoreType.DMA((3,)),
        ],
        compiler_params=params(48, 6),
        cost_estimate=cost(72),
        name="share",
    )(kv, shard_out, shard_qkv)


def attend_kernel(scalars, q, k, v, out):
    keys = k[...].reshape(-1, HEAD_DIM)
    values = v[...].reshape(-1, HEAD_DIM)
    length = scalars[pl.program_id(0)]
    offset = scalars[pl.num_programs(0)]
    scores = dot(q[0], keys, NT) * (1.0 / math.sqrt(HEAD_DIM))
    key_place = lax.broadcasted_iota(jnp.int32, scores.shape, 1)
    query_place = lax.broadcasted_iota(jnp.int32, scores.shape, 0) + offset
    scores = jnp.where((key_place <= query_place) & (key_place < length), scores, -1e30)
    weights = jnp.exp(scores - jnp.max(scores, axis=-1, keepdims=True))
    total = jnp.sum(weights, axis=-1, keepdims=True)
    probs = (weights * (1.0 / total)).astype(BF)
    out[0] = dot(probs, values).astype(BF)


def attend(scalars, q, kv, heads):
    seqs, _, slots, length, width = kv.shape
    block = (1, length, HEAD_DIM)
    return pl.pallas_call(
        attend_kernel,
        grid_spec=pltpu.PrefetchScalarGridSpec(
            num_scalar_prefetch=1,
            grid=(slots, heads),
            in_specs=[
                pl.BlockSpec(block, lambda s, h, _: (s, 0, h)),
                pl.BlockSpec((seqs, 1, 1, length, HEAD_DIM), lambda s, h, _: (0, 0, s, 0, h)),
                pl.BlockSpec((seqs, 1, 1, length, HEAD_DIM), lambda s, h, _: (0, 1, s, 0, h)),
            ],
            out_specs=pl.BlockSpec(block, lambda s, h, _: (s, 0, h)),
        ),
        out_shape=jax.ShapeDtypeStruct((slots, length, width), BF),
        compiler_params=params(40),
        cost_estimate=cost(15),
        name="attend",
    )(scalars, q.reshape(slots, length, width), kv, kv)


def attend_back_kernel(scalars, q, k, v, g, tables, dq_out, dkv_out):
    seqs = k.shape[0]
    scaling = 1.0 / math.sqrt(HEAD_DIM)
    keys = k[...].reshape(-1, HEAD_DIM)
    values = v[...].reshape(-1, HEAD_DIM)
    length = scalars[pl.program_id(0)]
    offset = scalars[pl.num_programs(0)]
    queries, grads = q[0], g[0]
    scores = dot(keys, queries, NT) * scaling
    key_place = lax.broadcasted_iota(jnp.int32, scores.shape, 0)
    query_place = lax.broadcasted_iota(jnp.int32, scores.shape, 1) + offset
    scores = jnp.where((key_place <= query_place) & (key_place < length), scores, -1e30)
    weights = jnp.exp(scores - jnp.max(scores, axis=0, keepdims=True))
    probs = weights * (1.0 / jnp.sum(weights, axis=0, keepdims=True))
    grad_probs = dot(values, grads, NT)
    mixed = jnp.sum(probs * grad_probs, axis=0, keepdims=True)
    grad_scores = (probs * (grad_probs - mixed)).astype(BF)
    grad_values = dot(probs.astype(BF), grads)
    grad_keys = dot(grad_scores, queries) * scaling
    shape = (seqs, -1, HEAD_DIM)
    dkv_out[:, 0, 0] = grad_keys.astype(BF).reshape(shape)
    dkv_out[:, 1, 0] = grad_values.astype(BF).reshape(shape)
    grad_queries = dot(grad_scores, keys, TN) * scaling
    tabs = (tables[0], tables[1], tables[2])
    dq_out[0] = turn(grad_queries, tabs, -1.0).astype(BF)


def attend_back(scalars, q, kv, g, tables, heads):
    seqs, _, slots, length, width = kv.shape
    block = (1, length, HEAD_DIM)
    own = pl.BlockSpec(block, lambda s, h, _: (s, 0, h))
    return pl.pallas_call(
        attend_back_kernel,
        grid_spec=pltpu.PrefetchScalarGridSpec(
            num_scalar_prefetch=1,
            grid=(slots, heads),
            in_specs=[
                own,
                pl.BlockSpec((seqs, 1, 1, length, HEAD_DIM), lambda s, h, _: (0, 0, s, 0, h)),
                pl.BlockSpec((seqs, 1, 1, length, HEAD_DIM), lambda s, h, _: (0, 1, s, 0, h)),
                own,
                pl.BlockSpec((3, length, HEAD_DIM), lambda s, h, _: (0, s, 0)),
            ],
            out_specs=[
                own,
                pl.BlockSpec((seqs, 2, 1, length, HEAD_DIM), lambda s, h, _: (0, 0, s, 0, h)),
            ],
        ),
        out_shape=[
            jax.ShapeDtypeStruct((slots, length, width), BF),
            jax.ShapeDtypeStruct((seqs, 2, slots, length, width), BF),
        ],
        compiler_params=params(48),
        cost_estimate=cost(25),
        name="attend_back",
    )(scalars, q.reshape(slots, length, width), kv, kv, g.reshape(slots, length, width), tables)


class Ring:
    def __init__(self, chunk):
        me = lax.axis_index("tensor")
        self.chunk, self.half = chunk, chunk // 2
        self.me = me
        self.right = lax.rem(me + 1, RING)
        self.left = lax.rem(me + RING - 1, RING)
        self.far = lax.rem(me + 2, RING)

    def at(self, index, shift=0):
        return pl.multiple_of(index * self.chunk + shift, self.half)

    def barrier(self):
        gate = pltpu.get_barrier_semaphore()
        for near in (self.left, self.right):
            pl.semaphore_signal(gate, inc=1, device_id={"tensor": near}, device_id_type=MESH)
        pl.semaphore_wait(gate, 2)


def remote(source, target, sems, index, device):
    return pltpu.make_async_remote_copy(
        src_ref=source,
        dst_ref=target,
        send_sem=sems.at[0, index],
        recv_sem=sems.at[1, index],
        device_id={"tensor": device},
        device_id_type=MESH,
    )


def product(lhs, rhs, start, count, write, step=256):
    total = rhs.shape[0]

    def one(cols):
        write(cols, dot(lhs[pl.ds(start, count), :], rhs[cols, :], NT))

    rows_loop(total, min(step, total), one)


class Scatter:
    def __init__(self, ring, lhs, rhs, far, near, far_in, near_in, sems):
        self.ring, self.lhs, self.rhs = ring, lhs, rhs
        self.far, self.near, self.far_in, self.near_in = far, near, far_in, near_in
        half = ring.half
        up, down = pl.ds(0, half), pl.ds(half, half)
        self.copies = [
            remote(far.at[0], far_in.at[0], sems, 0, ring.right),
            remote(far.at[1], far_in.at[1], sems, 1, ring.left),
            remote(near.at[0, down], near_in.at[0, down], sems, 2, ring.right),
            remote(near.at[1, up], near_in.at[1, up], sems, 3, ring.left),
            remote(near.at[0, up], near_in.at[0, up], sems, 4, ring.right),
            remote(near.at[1, down], near_in.at[1, down], sems, 5, ring.left),
        ]

    def begin(self):
        ring, half = self.ring, self.ring.half

        def far_half(which):
            def write(cols, value):
                self.far[which, :, cols] = value.astype(BF)

            product(self.lhs, self.rhs, ring.at(ring.far, which * half), half, write)
            self.copies[which].start()

        def near_half(which, device, part, copy):
            def write(cols, value):
                self.near[which, pl.ds(part * half, half), cols] = value.astype(BF)

            product(self.lhs, self.rhs, ring.at(device, part * half), half, write)
            self.copies[copy].start()

        far_half(0)
        far_half(1)
        near_half(0, ring.right, 1, 2)
        near_half(1, ring.left, 0, 3)

    def relay(self):
        ring, half = self.ring, self.ring.half

        def add_half(which, device, part, copy):
            self.copies[which].wait_recv()

            def write(cols, value):
                arrived = self.far_in[which, :, cols].astype(F32)
                self.near[which, pl.ds(part * half, half), cols] = (value + arrived).astype(BF)

            product(self.lhs, self.rhs, ring.at(device, part * half), half, write)
            self.copies[copy].start()

        add_half(0, ring.right, 0, 4)
        add_half(1, ring.left, 1, 5)

    def arrive(self):
        for copy in self.copies[2:]:
            copy.wait_recv()

    def finish(self):
        for copy in self.copies:
            copy.wait_send()


class Gather:
    def __init__(self, ring, own, out, sems, base, local_sem):
        half = ring.half

        def rows(index, shift=0, count=ring.chunk):
            return out.at[pl.ds(ring.at(index, shift), count), :]

        mine = rows(ring.me)
        self.local = pltpu.make_async_copy(own, mine, local_sem)
        self.first = [
            remote(own, mine, sems, base, ring.right),
            remote(own, mine, sems, base + 1, ring.left),
        ]
        up, down = rows(ring.left, 0, half), rows(ring.right, half, half)
        self.second = [
            remote(up, up, sems, base + 2, ring.right),
            remote(down, down, sems, base + 3, ring.left),
        ]

    def begin(self):
        for copy in self.first:
            copy.start()
        self.local.start()

    def relay(self):
        for arrived, onward in zip(self.first, self.second):
            arrived.wait_recv()
            onward.start()

    def finish(self):
        for copy in self.second:
            copy.wait_recv()
        for copy in self.first + self.second:
            copy.wait_send()
        self.local.wait()


def scatter_scratch(chunk, feats, count=1):
    half = chunk // 2
    lead = () if count == 1 else (count,)
    return [
        pltpu.VMEM(lead + (2, half, feats), BF),
        pltpu.VMEM(lead + (2, chunk, feats), BF),
        pltpu.VMEM(lead + (2, half, feats), BF),
        pltpu.VMEM(lead + (2, chunk, feats), BF),
    ]


def own_sum(scatter, total):
    ring = scatter.ring

    def write(cols, value):
        total[:, cols] = value

    product(scatter.lhs, scatter.rhs, ring.at(ring.me), ring.chunk, write)


def whole_sum(scatter, total, part):
    near = scatter.near_in
    return total[part, :] + near[0, part, :].astype(F32) + near[1, part, :].astype(F32)


def weight_copies(weight, target, sems, index):
    count = weight.shape[-2]

    def one(owner):
        source = weight.at[owner] if index is None else weight.at[owner, :, index]
        return pltpu.make_async_copy(
            source,
            target.at[:, pl.ds(pl.multiple_of(owner * count, count), count), :],
            sems.at[owner],
        )

    def every(act):
        def step(owner, carry):
            act(one(owner))
            return carry

        lax.fori_loop(0, weight.shape[0], step, 0)

    return every


def ring_product(slots, weight, part, total):
    def columns(cols):
        value = dot(slots[0, part, :], weight[0, cols, :], NT)
        for z in range(1, RING):
            value += dot(slots[z, part, :], weight[z, cols, :], NT)
        total[:, cols] = value

    rows_loop(total.shape[1], 256, columns)


def spread_kernel(vals, out, sems, own_sem):
    ring = Ring(16)
    local = pltpu.make_async_copy(vals, out.at[ring.me], own_sem)
    local.start()
    ring.barrier()
    spread = Spread(ring, out, sems, 0, vals)
    spread.begin()
    spread.relay()
    spread.arrive()
    spread.finish()
    local.wait()


def spread_vals(vals):
    return pl.pallas_call(
        spread_kernel,
        in_specs=[ANY],
        out_specs=ANY,
        out_shape=jax.ShapeDtypeStruct((RING,) + vals.shape, BF),
        scratch_shapes=[pltpu.SemaphoreType.DMA((2, 4)), pltpu.SemaphoreType.DMA],
        compiler_params=params(32, 0),
        cost_estimate=cost(70),
        name="spread_vals",
    )(vals)


def attn_out_kernel(
    slots, weight, resid, bias, lg, lb, hidden_out, mlp_out,
    weights, total, base_rows, stage, weight_sems, base_sem, stage_sems,
):
    chunk, feats = total.shape
    me = lax.axis_index("tensor")
    load = weight_copies(weight, weights, weight_sems, None)
    load(lambda copy: copy.start())
    load(lambda copy: copy.wait())

    def write_out(index, slot):
        part = pl.ds(pl.multiple_of(index * chunk, chunk), chunk)
        return pltpu.make_async_copy(stage.at[slot], mlp_out.at[part, :], stage_sems.at[slot])

    def one(index, carry):
        part = pl.ds(pl.multiple_of(index * chunk, chunk), chunk)
        fetch = pltpu.make_async_copy(resid.at[part, :], base_rows, base_sem)
        fetch.start()
        slot = lax.rem(index, 2)
        ring_product(slots, weights, part, total)
        fetch.wait()

        @pl.when(index >= 2)
        def _():
            write_out(index - 2, slot).wait()

        def norm(sub):
            value = base_rows[sub, :] + (total[sub, :] + bias[...])
            total[sub, :] = value
            centred = value - mean_last(value)
            inverse = lax.rsqrt(mean_last(centred * centred) + NORM_EPSILON)
            stage[slot, sub, :] = (centred * inverse * lg[...] + lb[...]).astype(BF)

        rows_loop(chunk, 64, norm)
        write_out(index, slot).start()

        @pl.when(index == me)
        def _():
            hidden_out[...] = total[...]

        return carry

    lax.fori_loop(0, RING, one, 0)
    for index in range(RING - 2, RING):
        write_out(index, index % 2).wait()


def attn_out(slots, weight, resid, bias, lg, lb):
    rows, feats = resid.shape
    width = slots.shape[2]
    chunk = rows // RING
    return pl.pallas_call(
        attn_out_kernel,
        in_specs=[VMEM, ANY, ANY, VMEM, VMEM, VMEM],
        out_specs=[VMEM, ANY],
        out_shape=[
            jax.ShapeDtypeStruct((chunk, feats), F32),
            jax.ShapeDtypeStruct((rows, feats), BF),
        ],
        scratch_shapes=[
            pltpu.VMEM((RING, feats, width), BF),
            pltpu.VMEM((chunk, feats), F32),
            pltpu.VMEM((chunk, feats), F32),
            pltpu.VMEM((2, chunk, feats), BF),
            pltpu.SemaphoreType.DMA((weight.shape[0],)),
            pltpu.SemaphoreType.DMA,
            pltpu.SemaphoreType.DMA((2,)),
        ],
        compiler_params=params(48),
        cost_estimate=cost(30),
        name="attn_out",
    )(slots, weight, resid, bias, lg, lb)


def norm_back(values, grads, gain):
    centred = values - mean_last(values)
    inverse = lax.rsqrt(mean_last(centred * centred) + NORM_EPSILON)
    normed = centred * inverse
    inner = grads * gain
    back = inverse * (inner - mean_last(inner) - normed * mean_last(inner * normed))
    return back, normed


def fold(values):
    rows, feats = values.shape
    return jnp.sum(values.reshape(rows // 8, 8, feats), axis=0)


def weight_product(source, rhs, out, blocks, stage, load_sems, store_sems):
    width = blocks.shape[2]
    count = source.shape[1] // width

    def load(n, slot):
        cols = pl.ds(pl.multiple_of(n * width, width), width)
        return pltpu.make_async_copy(source.at[:, cols], blocks.at[slot], load_sems.at[slot])

    def store(n, slot):
        part = pl.ds(pl.multiple_of(n * width, width), width)
        return pltpu.make_async_copy(stage.at[slot], out.at[part, :], store_sems.at[slot])

    load(0, 0).start()

    def one(n, carry):
        slot = lax.rem(n, 2)

        @pl.when(n + 1 < count)
        def _():
            load(n + 1, 1 - slot).start()

        load(n, slot).wait()

        @pl.when(n >= 2)
        def _():
            store(n - 2, slot).wait()

        def columns(cols):
            stage[slot, :, cols] = dot(blocks[slot], rhs[:, cols], TN).astype(BF)

        rows_loop(rhs.shape[1], 256, columns)
        store(n, slot).start()
        return carry

    lax.fori_loop(0, count, one, 0)
    for n in range(count - 2, count):
        store(n, n % 2).wait()


def spread_dq_kernel(
    lin, normed, grad_attn, vals, out, products,
    blocks, tiles_out, sems, own_sem, load_sems, store_sems,
):
    ring = Ring(16)
    width = lin.shape[1]
    local = pltpu.make_async_copy(lin, out.at[ring.me], own_sem)
    local.start()
    ring.barrier()
    spread = Spread(ring, out, sems, 0, lin)
    spread.begin()
    for i, (source, rhs) in enumerate(((normed.at[0], lin), (grad_attn, vals))):
        target = products.at[:, pl.ds(i * width, width)]
        weight_product(source, rhs, target, blocks, tiles_out, load_sems, store_sems)
    spread.relay()
    spread.arrive()
    spread.finish()
    local.wait()


def spread_dq(lin, normed, grad_attn, vals):
    rows, width = lin.shape
    feats = grad_attn.shape[1]
    return pl.pallas_call(
        spread_dq_kernel,
        in_specs=[VMEM, ANY, ANY, VMEM],
        out_specs=[ANY, ANY],
        out_shape=[
            jax.ShapeDtypeStruct((RING, rows, width), BF),
            jax.ShapeDtypeStruct((feats, 2 * width), BF),
        ],
        scratch_shapes=[
            pltpu.VMEM((2, rows, 256), BF),
            pltpu.VMEM((2, 256, width), BF),
            pltpu.SemaphoreType.DMA((2, 4)),
            pltpu.SemaphoreType.DMA,
            pltpu.SemaphoreType.DMA((2,)),
            pltpu.SemaphoreType.DMA((2,)),
        ],
        compiler_params=params(40, 3),
        cost_estimate=cost(70),
        name="spread_dq",
    )(lin, normed, grad_attn, vals)


class Line:
    def __init__(self, chunk):
        me = lax.axis_index("tensor")
        self.me, self.chunk = me, chunk
        self.low = me < 2
        self.outer = (me == 0) | (me == RING - 1)
        self.inner = (me == 1) | (me == RING - 2)
        self.up = jnp.where(self.low, me + 1, me - 1)
        self.down = jnp.where(self.low, lax.max(me - 1, 0), lax.min(me + 1, RING - 1))

    def at(self, number):
        index = jnp.where(self.low, number, RING - 1 - number)
        return pl.ds(pl.multiple_of(index * self.chunk, self.chunk), self.chunk)

    def barrier(self):
        gate = pltpu.get_barrier_semaphore()
        pl.semaphore_signal(gate, inc=1, device_id={"tensor": self.up}, device_id_type=MESH)

        @pl.when(self.inner)
        def _():
            pl.semaphore_signal(
                gate, inc=1, device_id={"tensor": self.down}, device_id_type=MESH
            )
            pl.semaphore_wait(gate, 2)

        @pl.when(self.outer)
        def _():
            pl.semaphore_wait(gate, 1)


class LineSum:
    def __init__(self, line, lhs, rhs, outbound, inbound, sems, base):
        self.line, self.lhs, self.rhs = line, lhs, rhs
        self.outbound, self.inbound = outbound, inbound
        copy = lambda slot, target, device: remote(
            outbound.at[slot], inbound.at[target], sems, base + target, device
        )
        self.inward = [copy(i, i, line.up) for i in range(3)]
        self.across = [copy(i, 3 + i, line.up) for i in range(2)]
        self.outward = remote(outbound.at[2], inbound.at[5], sems, base + 5, line.down)

    def partial(self, number, slot, arrived=None):
        rows = self.line.at(number)

        def write(cols, value):
            if arrived is not None:
                value = value + self.inbound[arrived, :, cols].astype(F32)
            self.outbound[slot, :, cols] = value.astype(BF)

        product(self.lhs, self.rhs, rows.start, self.line.chunk, write)

    def own(self, total):
        index = self.line.me * self.line.chunk

        def write(cols, value):
            total[:, cols] = value

        product(
            self.lhs, self.rhs, pl.multiple_of(index, self.line.chunk), self.line.chunk, write
        )

    def send_inward(self):
        for slot, copy in enumerate(self.inward):
            self.partial(3 - slot, slot)
            copy.start()

    def send_across(self, i):
        self.inward[i].wait_recv()
        self.partial(3 - i, i, i)
        self.across[i].start()

    def send_outward(self):
        self.across[0].wait_recv()
        self.partial(0, 2, 3)
        self.outward.start()

    def arrive(self):
        line = self.line

        @pl.when(line.inner)
        def _():
            self.inward[2].wait_recv()
            self.across[1].wait_recv()

        @pl.when(line.outer)
        def _():
            self.outward.wait_recv()

    def sent(self):
        line = self.line

        @pl.when(line.inner)
        def _():
            for copy in self.across + [self.outward]:
                copy.wait_send()

        @pl.when(line.outer)
        def _():
            for copy in self.inward:
                copy.wait_send()

    def clear(self):
        @pl.when(self.line.outer)
        def _():
            self.inbound[2] = jnp.zeros_like(self.inbound[2])

    def whole(self, total, part):
        last = jnp.where(self.line.outer, 5, 4)
        return (
            total[part, :]
            + self.inbound[2, part, :].astype(F32)
            + self.inbound[last, part, :].astype(F32)
        )


def mlp_back_kernel(
    lhs, rhs, acts, down, hidden, cot, mlp_in, lg, down_bias,
    grad_out, small_out, rows_out, grad_up, grad_down,
    outbound, inbound, total, cot_rows, own, sums, blocks, stage,
    sems, gather_sems, local_sems, load_sems, store_sems,
):
    chunk, feats = total.shape
    line = Line(chunk)
    mine = pl.ds(pl.multiple_of(line.me * chunk, chunk), chunk)
    fetch = pltpu.make_async_copy(cot.at[mine, :], cot_rows, local_sems.at[0])
    fetch.start()
    line.barrier()
    first = LineSum(line, lhs, rhs, outbound, inbound.at[0], sems.at[0], 0)
    second = LineSum(line, acts, down, outbound, inbound.at[1], sems.at[1], 0)
    first.clear()
    second.clear()

    @pl.when(line.outer)
    def _():
        first.send_inward()

    first.own(total)
    sums[...] = jnp.zeros_like(sums)
    weight_product(mlp_in, lhs, grad_up, blocks, stage, load_sems, store_sems)

    @pl.when(line.inner)
    def _():
        first.send_across(0)
        first.send_across(1)
        first.send_outward()

    weight_product(cot, acts, grad_down, blocks, stage, load_sems, store_sems)
    fetch.wait()
    first.arrive()

    def back(part):
        grads = first.whole(total, part)
        step, normed = norm_back(hidden[part, :], grads, lg[...])
        low = (cot_rows[part, :].astype(F32) + step).astype(BF)
        own[part, :] = low
        sums[0] += fold(grads * normed)
        sums[1] += fold(grads)
        sums[2] += fold(low.astype(F32))

    rows_loop(chunk, 16, back)
    local = pltpu.make_async_copy(own, grad_out.at[mine, :], local_sems.at[1])
    local.start()
    first.sent()

    def chunk_copy(number, index, device, source=None):
        rows = grad_out.at[line.at(number), :]
        return remote(rows if source is None else source, rows, gather_sems, index, device)

    @pl.when(line.outer)
    def _():
        onward = chunk_copy(0, 0, line.up, own)
        onward.start()
        second.send_inward()
        second.own(total)
        for number in range(1, RING):
            chunk_copy(number, 2 + number, line.up).wait_recv()
        onward.wait_send()

    @pl.when(line.inner)
    def _():
        inward = [chunk_copy(1, 1, line.up, own), chunk_copy(1, 3, line.down, own)]
        for copy in inward:
            copy.start()
        second.own(total)
        chunk_copy(0, 0, line.up).wait_recv()
        relay = chunk_copy(0, 2, line.up)
        relay.start()
        chunk_copy(2, 1, line.up).wait_recv()
        near = chunk_copy(2, 4, line.down)
        near.start()
        second.send_across(0)
        chunk_copy(3, 2, line.up).wait_recv()
        far = chunk_copy(3, 5, line.down)
        far.start()
        second.send_across(1)
        second.send_outward()
        for copy in inward + [relay, near, far]:
            copy.wait_send()

    for i in range(3):
        small_out[i : i + 1, :] = jnp.sum(sums[i], axis=0, keepdims=True)
    second.arrive()

    def add(part):
        value = hidden[part, :] + (second.whole(total, part) + down_bias[...])
        rows_out[part, :] = value.astype(BF)

    rows_loop(chunk, 16, add)
    second.sent()
    local.wait()


def mlp_back(lhs, rhs, acts, down, hidden, cot, mlp_in, lg, down_bias):
    rows, feats = cot.shape
    width = lhs.shape[1]
    chunk = rows // RING
    block = 256
    return pl.pallas_call(
        mlp_back_kernel,
        in_specs=[VMEM, VMEM, VMEM, VMEM, VMEM, ANY, ANY, VMEM, VMEM],
        out_specs=[ANY, VMEM, VMEM, ANY, ANY],
        out_shape=[
            jax.ShapeDtypeStruct((rows, feats), BF),
            jax.ShapeDtypeStruct((3, feats), F32),
            jax.ShapeDtypeStruct((chunk, feats), BF),
            jax.ShapeDtypeStruct((feats, width), BF),
            jax.ShapeDtypeStruct((feats, width), BF),
        ],
        scratch_shapes=[
            pltpu.VMEM((3, chunk, feats), BF),
            pltpu.VMEM((2, 6, chunk, feats), BF),
            pltpu.VMEM((chunk, feats), F32),
            pltpu.VMEM((chunk, feats), BF),
            pltpu.VMEM((chunk, feats), BF),
            pltpu.VMEM((3, 8, feats), F32),
            pltpu.VMEM((2, rows, block), BF),
            pltpu.VMEM((2, block, width), BF),
            pltpu.SemaphoreType.DMA((2, 2, 6)),
            pltpu.SemaphoreType.DMA((2, 6)),
            pltpu.SemaphoreType.DMA((2,)),
            pltpu.SemaphoreType.DMA((2,)),
            pltpu.SemaphoreType.DMA((2,)),
        ],
        compiler_params=params(60, 1),
        cost_estimate=cost(175),
        name="mlp_back",
    )(lhs, rhs, acts, down, hidden, cot, mlp_in, lg, down_bias)


class Spread:
    def __init__(self, ring, slots, sems, base, source):
        half = slots.shape[1] // 2
        mine = slots.at[ring.me]
        self.first = [
            remote(source, mine, sems, base, ring.right),
            remote(source, mine, sems, base + 1, ring.left),
        ]
        up = slots.at[ring.left, pl.ds(0, half), :]
        down = slots.at[ring.right, pl.ds(half, half), :]
        self.second = [
            remote(up, up, sems, base + 2, ring.right),
            remote(down, down, sems, base + 3, ring.left),
        ]

    def begin(self):
        for copy in self.first:
            copy.start()

    def relay(self):
        for arrived, onward in zip(self.first, self.second):
            arrived.wait_recv()
            onward.start()

    def arrive(self):
        for copy in self.second:
            copy.wait_recv()

    def finish(self):
        for copy in self.first + self.second:
            copy.wait_send()


def streams_back_kernel(
    first, lin, weight, hist, mix, lg, normed_in, own_rows,
    grads_out, small_out, products, rows_out,
    slots, weights, total, layers, stage, sums, blocks, tiles_out,
    sems, weight_sems, layer_sem, stage_sems, own_sems, load_sems, store_sems,
):
    tile, feats = total.shape
    depth = layers.shape[0]
    whole_load = pltpu.make_async_copy(hist, layers, layer_sem)
    whole_load.start()
    rows, width = lin.shape[1], lin.shape[2]
    tiles = rows // tile
    ring = Ring(rows)

    def fetch(stream):
        return weight_copies(
            weight, weights.at[stream % 2], weight_sems.at[stream % 2], stream
        )

    local = [
        pltpu.make_async_copy(lin.at[i], slots.at[i, ring.me], own_sems.at[i])
        for i in range(2)
    ]
    local.append(
        pltpu.make_async_copy(own_rows, rows_out.at[ring.me], own_sems.at[2])
    )
    for copy in local:
        copy.start()
    for stream in range(2):
        fetch(stream)(lambda copy: copy.start())
    sums[...] = jnp.zeros_like(sums)
    ring.barrier()
    spreads = [Spread(ring, slots.at[i], sems.at[i], 0, lin.at[i]) for i in range(2)]
    spreads.append(Spread(ring, rows_out, sems.at[2], 0, own_rows))

    def write_out(stream, index, slot):
        part = pl.ds(pl.multiple_of(index * tile, tile), tile)
        return pltpu.make_async_copy(
            stage.at[slot], grads_out.at[stream, part, :], stage_sems.at[slot]
        )

    def flush(stream):
        for index in range(tiles):
            write_out(stream, index, index).wait()

    def compute(stream):
        fetch(stream)(lambda copy: copy.wait())
        if stream == 0:
            whole_load.wait()
        else:
            flush(stream - 1)

        def one(index, carry):
            part = pl.ds(pl.multiple_of(index * tile, tile), tile)

            gathered = first if stream == 0 else slots.at[stream - 1]
            ring_product(gathered, weights.at[stream % 2], part, total)
            def back(sub):
                grads = total[sub, :]
                here = pl.ds(pl.multiple_of(index * tile + sub.start, 16), 16)
                latest = layers[depth - 1, here, :].astype(F32)
                share = mix[here, :]
                mixture = latest
                for j in range(depth):
                    col = stream * depth + j
                    mixture = mixture + share[:, col : col + 1] * layers[j, here, :].astype(F32)
                step, normed = norm_back(mixture, grads, lg[stream : stream + 1, :])
                stage[index, sub, :] = step.astype(BF)
                sums[stream, 0] += fold(grads * normed)
                sums[stream, 1] += fold(grads)

            rows_loop(tile, 16, back)
            write_out(stream, index, index).start()
            return carry

        lax.fori_loop(0, tiles, one, 0)
        if stream == 0:
            fetch(2)(lambda copy: copy.start())

    for copy in local:
        copy.wait()
    spreads[0].begin()
    compute(0)
    spreads[0].relay()
    for i in range(2):
        source, target = normed_in.at[i + 1], products.at[:, pl.ds(i * width, width)]
        weight_product(source, lin.at[i], target, blocks, tiles_out, load_sems, store_sems)
    spreads[0].arrive()
    spreads[1].begin()
    compute(1)
    spreads[1].relay()
    spreads[1].arrive()
    spreads[2].begin()
    compute(2)
    spreads[2].relay()
    spreads[2].arrive()
    flush(2)
    for i in range(3):
        for j in range(2):
            small_out[j, i : i + 1, :] = jnp.sum(sums[i, j], axis=0, keepdims=True)
    for spread in spreads:
        spread.finish()


def streams_back(first, lin, weight, hist, mix, lg, normed, own_rows):
    depth, rows, feats = hist.shape
    width = lin.shape[2]
    tile = min(256, rows)
    return pl.pallas_call(
        streams_back_kernel,
        in_specs=[VMEM, VMEM, ANY, ANY, VMEM, VMEM, ANY, ANY],
        out_specs=[ANY, VMEM, ANY, ANY],
        out_shape=[
            jax.ShapeDtypeStruct((3, rows, feats), BF),
            jax.ShapeDtypeStruct((2, 3, feats), F32),
            jax.ShapeDtypeStruct((feats, 2 * width), BF),
            jax.ShapeDtypeStruct((RING,) + own_rows.shape, BF),
        ],
        scratch_shapes=[
            pltpu.VMEM((2, RING, rows, width), BF),
            pltpu.VMEM((2, RING, feats, width), BF),
            pltpu.VMEM((tile, feats), F32),
            pltpu.VMEM((depth, rows, feats), BF),
            pltpu.VMEM((rows // tile, tile, feats), BF),
            pltpu.VMEM((3, 2, 8, feats), F32),
            pltpu.VMEM((2, rows, 256), BF),
            pltpu.VMEM((2, 256, width), BF),
            pltpu.SemaphoreType.DMA((3, 2, 4)),
            pltpu.SemaphoreType.DMA((2, weight.shape[0])),
            pltpu.SemaphoreType.DMA,
            pltpu.SemaphoreType.DMA((rows // tile,)),
            pltpu.SemaphoreType.DMA((3,)),
            pltpu.SemaphoreType.DMA((2,)),
            pltpu.SemaphoreType.DMA((2,)),
        ],
        compiler_params=params(60, 2),
        cost_estimate=cost(240),
        name="streams_back",
    )(first, lin, weight, hist, mix, lg, normed, own_rows)


def small_kernel(seqs, owners, ours, share, out, share_out, near, all_ours, all_shares, near_sems, sems):
    ring = Ring(2)
    near_rows = near.shape[1]
    rank, peers, places = owner_places(seqs, owners)
    mates = [ring.right, ring.far, ring.left]
    enter(places + [{"tensor": z} for z in mates])

    near[ring.me] = ours[0:near_rows, :]
    shares = [
        push(share.at[p], all_shares.at[rank], sems.at[0], k, place)
        for k, (p, place) in enumerate(zip(peers, places))
    ]
    first = [
        push(near.at[ring.me], near.at[ring.me], near_sems, k, {"tensor": z})
        for k, z in enumerate(mates)
    ]
    for copy in first + shares:
        copy.start()
    for copy in first:
        copy.wait()
    all_ours[rank, 0:near_rows, :] = (near[0] + near[1]) + (near[2] + near[3])
    all_ours[rank, near_rows:, :] = ours[near_rows:, :]
    all_shares[rank] = share[rank]
    second = [
        push(all_ours.at[rank], all_ours.at[rank], sems.at[1], k, place)
        for k, place in enumerate(places)
    ]
    for copy in second:
        copy.start()
    for copy in shares + second:
        copy.wait()
    total, part = all_ours[0], all_shares[0]
    for index in range(1, owners):
        total += all_ours[index]
        part += all_shares[index]
    out[...] = total
    share_out[...] = part


def small_sums(ours, share, seqs):
    owners = share.shape[0]
    rows, feats = ours.shape
    return pl.pallas_call(
        functools.partial(small_kernel, seqs, owners),
        in_specs=[VMEM, VMEM],
        out_specs=[VMEM, VMEM],
        out_shape=[
            jax.ShapeDtypeStruct(ours.shape, F32),
            jax.ShapeDtypeStruct(share.shape[1:], F32),
        ],
        scratch_shapes=[
            pltpu.VMEM((RING, 8, feats), F32),
            pltpu.VMEM((owners,) + ours.shape, F32),
            pltpu.VMEM(share.shape, F32),
            pltpu.SemaphoreType.DMA((2, 3)),
            pltpu.SemaphoreType.DMA((2, 2, owners - 1)),
        ],
        compiler_params=params(40, 4),
        cost_estimate=cost(12),
        name="small_sums",
    )(ours, share)


def mlp_kernel(mlp_in, cot, up, down, bias, act_out, grad_out, sum_out):
    lin = dot(mlp_in[...], up[...]) + bias[...]
    grad_act = dot(cot[...], down[...])
    cdf = normal_cdf(lin)
    act_out[...] = (lin * cdf).astype(BF)
    grad = (grad_act * gelu_slope(lin, cdf)).astype(BF)
    grad_out[...] = grad

    @pl.when(pl.program_id(1) == 0)
    def _():
        sum_out[...] = jnp.zeros_like(sum_out)

    sum_out[...] += jnp.sum(grad.astype(F32), axis=0, keepdims=True)


def mlp(mlp_in, cot, up, down, bias):
    rows, feats = mlp_in.shape
    width = up.shape[1]
    tile, cols = min(256, rows), 512
    return pl.pallas_call(
        mlp_kernel,
        grid=(width // cols, rows // tile),
        in_specs=[
            pl.BlockSpec((tile, feats), lambda n, r: (r, 0)),
            pl.BlockSpec((tile, feats), lambda n, r: (r, 0)),
            pl.BlockSpec((feats, cols), lambda n, r: (0, n)),
            pl.BlockSpec((feats, cols), lambda n, r: (0, n)),
            pl.BlockSpec((1, cols), lambda n, r: (0, n)),
        ],
        out_specs=[
            pl.BlockSpec((tile, cols), lambda n, r: (r, n)),
            pl.BlockSpec((tile, cols), lambda n, r: (r, n)),
            pl.BlockSpec((1, cols), lambda n, r: (0, n)),
        ],
        out_shape=[
            jax.ShapeDtypeStruct((rows, width), BF),
            jax.ShapeDtypeStruct((rows, width), BF),
            jax.ShapeDtypeStruct((1, width), F32),
        ],
        compiler_params=params(48),
        cost_estimate=cost(25),
        name="mlp",
    )(mlp_in, cot, up, down, bias)


def turn_back_kernel(dkv, tables, dk_out, sum_out):
    tabs = (tables[0], tables[1], tables[2])
    for head in range(dk_out.shape[1] // HEAD_DIM):
        cols = slice(head * HEAD_DIM, (head + 1) * HEAD_DIM)
        dk_out[:, cols] = turn(dkv[0, :, cols].astype(F32), tabs, -1.0).astype(BF)


def last_kernel(
    hist, streams, attn, mix, pre, gain, w1, w2, grad_out, gain_out, w1_out, w2_out,
    normed, grad_mix, grad_normed, gain_sum,
):
    depth, rows, feats = hist.shape
    step_index = pl.program_id(0)

    @pl.when(step_index == 0)
    def _():
        gain_sum[...] = jnp.zeros_like(gain_sum)
        w1_out[...] = jnp.zeros_like(w1_out)
        w2_out[...] = jnp.zeros_like(w2_out)

    def reduce(part):
        layers = [hist[j, part, :].astype(F32) for j in range(depth)]
        latest = layers[depth - 1]
        scale = lax.rsqrt(mean_last(latest * latest) + RMS_EPSILON)
        normed[part, :] = (latest * scale * gain[...]).astype(BF)
        for m in range(STREAMS):
            grads = (attn[part, :] if m == STREAMS - 1 else streams[m, part, :]).astype(F32)
            for j in range(depth):
                at = m * depth + j
                grad_mix[part, at : at + 1] = jnp.sum(grads * layers[j], axis=-1, keepdims=True)

    rows_loop(rows, 64, reduce)
    pre_value = pre[...]
    cdf = normal_cdf(pre_value)
    grads = grad_mix[...]
    w2_out[...] += dot(pre_value * cdf, grads, TN, EXACT)
    grad_act = dot(grads, w2[...], NT, EXACT)
    grad_pre = (grad_act * gelu_slope(pre_value, cdf)).astype(BF)
    w1_out[...] += dot(grad_pre, normed[...], TN)
    grad_normed[...] = dot(grad_pre, w1[...], NT)

    def write(part):
        layers = [hist[depth - 1, part, :].astype(F32)]
        latest = layers[0]
        scale = lax.rsqrt(mean_last(latest * latest) + RMS_EPSILON)
        value = grad_normed[part, :]
        gain_sum[...] += fold(value * latest * scale)
        value = value * gain[...]
        back = scale * value - latest * (scale * scale * scale * mean_last(latest * value))
        weight = mix[part, :]
        grads = [streams[m, part, :].astype(F32) for m in range(STREAMS - 1)]
        grads.append(attn[part, :].astype(F32))
        for j in range(depth):
            total = weight[:, j : j + 1] * grads[0]
            for m in range(1, STREAMS):
                at = m * depth + j
                total = total + weight[:, at : at + 1] * grads[m]
            if j == depth - 1:
                total = total + (grads[0] + grads[1] + grads[2] + grads[3]) + back
            grad_out[j, part, :] = total

    rows_loop(rows, 64, write)

    @pl.when(step_index == pl.num_programs(0) - 1)
    def _():
        gain_out[...] = jnp.sum(gain_sum[...], axis=0, keepdims=True)


def last(hist, streams, attn, mix, pre, gain, w1, w2):
    depth, rows, feats = hist.shape
    hidden = w1.shape[1]
    tile = min(64, rows)
    full = lambda shape: pl.BlockSpec(shape, lambda i: (0,) * len(shape))
    return pl.pallas_call(
        last_kernel,
        grid=(rows // tile,),
        in_specs=[
            pl.BlockSpec((depth, tile, feats), lambda i: (0, i, 0)),
            pl.BlockSpec((3, tile, feats), lambda i: (0, i, 0)),
            pl.BlockSpec((tile, feats), lambda i: (i, 0)),
            pl.BlockSpec((tile, STREAMS * depth), lambda i: (i, 0)),
            pl.BlockSpec((tile, hidden), lambda i: (i, 0)),
            full((1, feats)),
            full(w1.shape),
            full(w2.shape),
        ],
        out_specs=[
            pl.BlockSpec((depth, tile, feats), lambda i: (0, i, 0)),
            full((1, feats)),
            full((hidden, feats)),
            full(w2.shape),
        ],
        out_shape=[
            jax.ShapeDtypeStruct((depth, rows, feats), F32),
            jax.ShapeDtypeStruct((1, feats), F32),
            jax.ShapeDtypeStruct((hidden, feats), F32),
            jax.ShapeDtypeStruct(w2.shape, F32),
        ],
        scratch_shapes=[
            pltpu.VMEM((tile, feats), BF),
            pltpu.VMEM((tile, STREAMS * depth), F32),
            pltpu.VMEM((tile, feats), F32),
            pltpu.VMEM((8, feats), F32),
        ],
        compiler_params=params(40),
        cost_estimate=cost(30),
        name="last",
    )(hist, streams, attn, mix, pre, gain.reshape(1, feats), w1, w2)


def turn_back(dkv, tables):
    _, rows, width = dkv.shape
    return pl.pallas_call(
        lambda d, t, o: turn_back_kernel(d, t, o, None),
        grid=(1,),
        in_specs=[
            pl.BlockSpec((1, rows, width), lambda i: (0, 0, 0)),
            pl.BlockSpec(tables.shape, lambda i: (0, 0, 0)),
        ],
        out_specs=pl.BlockSpec((rows, width), lambda i: (0, 0)),
        out_shape=jax.ShapeDtypeStruct((rows, width), BF),
        compiler_params=params(40),
        cost_estimate=cost(3),
        name="turn_back",
    )(dkv, tables)


def row_product(left, right):
    return dot(left, right, TN).astype(BF)


def shards(
    history,
    positions,
    lengths,
    cotangent,
    mix_gain,
    mix_w1,
    mix_w2,
    ln_gain,
    ln_bias,
    qkv_weight,
    qkv_bias,
    out_weight,
    out_bias,
    up_weight,
    up_bias,
    down_weight,
    down_bias,
):
    depth, slots, block_len, feats = history.shape
    rows = slots * block_len
    width = qkv_weight.shape[2]
    heads = width // HEAD_DIM
    owners = ("dp", "seq")
    layers = history.reshape(depth, rows, feats)

    seqs = lax.axis_size("seq")
    count = lax.axis_size("dp") * seqs
    tie = lax.optimization_barrier
    gather = functools.partial(lax.all_gather, axis_name=owners, axis=0)
    w_kv = gather(jnp.concatenate([qkv_weight[1], qkv_weight[2]], axis=1), tiled=True)
    w_q = gather(qkv_weight[0], tiled=True)

    offset = lax.axis_index("seq") * block_len
    query_place = offset + jnp.arange(block_len, dtype=jnp.int32)
    valid = (query_place[None, :] < lengths[:, None]).reshape(rows, 1)
    cot = jnp.where(valid, cotangent.reshape(rows, feats), jnp.zeros((), BF))
    scalars = jnp.concatenate([lengths, offset[None].astype(jnp.int32)])
    tables = rotary_tables(positions.reshape(rows))

    normed, resid, mix, pre, w_mix = front(
        layers, mix_gain, mix_w1, mix_w2, ln_gain, ln_bias, seqs, count
    )
    w_up = gather(up_weight, tiled=True)
    kv = project(normed, w_kv, qkv_bias[1:], tables, 1)
    kv_all, ring_out, ring_qkv = share(kv, out_weight, qkv_weight.reshape(-1, width), seqs)
    q = project(normed, w_q, qkv_bias[:1], tables, 0)[0]
    w_out_all = gather(ring_out)
    kv_all = kv_all.reshape(seqs, 2, slots, block_len, width)
    attn_vals = attend(scalars, q, kv_all, heads).reshape(rows, width)
    attn_vals, w_up, down_weight = tie((attn_vals, w_up, down_weight))
    w_down = gather(down_weight, tiled=True)
    vals_all = spread_vals(attn_vals)
    vals_all, ring_qkv = tie((vals_all, ring_qkv))
    w_qkv = gather(ring_qkv.reshape((RING,) + qkv_weight.shape))
    hidden, mlp_in = attn_out(
        vals_all, w_out_all, resid, out_bias[None, :], ln_gain[3:4], ln_bias[3:4]
    )
    w_out = lax.dynamic_index_in_dim(
        w_out_all, lax.axis_index("tensor"), 1, keepdims=False
    ).reshape(feats, width)
    up_act, grad_up, grad_up_bias = mlp(mlp_in, cot, w_up, w_down, up_bias[None, :])
    scatter = functools.partial(
        lax.psum_scatter, axis_name=owners, scatter_dimension=0, tiled=True
    )
    grad_attn, small_mlp, out_rows, grad_upw, grad_down = mlp_back(
        grad_up, w_up, up_act, w_down, hidden, cot, mlp_in, ln_gain[3:4], down_bias[None, :]
    )
    grad_vals = dot(grad_attn, w_out).astype(BF)
    dq, dkv = attend_back(scalars, q, kv_all, grad_vals, tables, heads)
    w_qkv, dq, dkv = tie((w_qkv, dq, dkv))
    dkv_own = lax.psum_scatter(dkv, "seq", scatter_dimension=0).reshape(2, rows, width)
    dq = dq.reshape(rows, width)
    dq_all, grad_qo = spread_dq(dq, normed, grad_attn, attn_vals)
    dq_all, dkv_own, grad_down, grad_upw, grad_qo = tie(
        (dq_all, dkv_own, grad_down, grad_upw, grad_qo)
    )
    shard_down, shard_up, shard_qo = scatter(grad_down), scatter(grad_upw), scatter(grad_qo)
    lin_kv = jnp.stack([turn_back(dkv_own, tables), dkv_own[1]])
    grads, small_qkv, grad_kv, layer_out = streams_back(
        dq_all, lin_kv, w_qkv, layers, mix, ln_gain, normed, out_rows
    )
    shard_down, shard_up, shard_qo, grads, grad_kv = tie(
        (shard_down, shard_up, shard_qo, grads, grad_kv)
    )
    shard_kv = scatter(grad_kv)
    shard_down, shard_up = shard_down.astype(F32), shard_up.astype(F32)
    shard_qkv = jnp.stack([shard_qo[:, :width], shard_kv[:, :width], shard_kv[:, width:]])
    shard_qkv, shard_out = shard_qkv.astype(F32), shard_qo[:, width:].astype(F32)
    grad_layers, grad_gain, grad_w1, grad_w2 = last(
        layers, grads, grad_attn, mix, pre, mix_gain, w_mix, mix_w2
    )
    grad_history = grad_layers.reshape(depth, slots, block_len, feats)
    hidden_count = mix_w1.shape[1]
    w1_share = grad_w1.reshape(hidden_count, count, feats // count).transpose(1, 0, 2)

    def as_row(values):
        flat = values.reshape(1, -1)
        return jnp.pad(flat, ((0, 0), (0, feats - flat.shape[1])))

    grad_qkv_bias = jnp.concatenate(
        [jnp.sum(dq.astype(F32), axis=0)[None], jnp.sum(lin_kv.astype(F32), axis=1)]
    )
    ours = jnp.concatenate(
        [small_mlp, jnp.zeros((5, feats), F32), small_qkv.reshape(6, feats)]
        + [
            as_row(values)
            for values in (
                grad_gain, grad_w2, grad_qkv_bias, grad_up_bias, jnp.sum(cot.astype(F32), axis=0)
            )
        ]
        + [jnp.zeros((5, feats), F32)],
        axis=0,
    )
    summed, shard_w1 = small_sums(ours, w1_share.reshape(count, -1, 128), seqs)
    return (
        layer_out.reshape(slots, block_len, feats),
        grad_history,
        summed[14],
        shard_w1.reshape(hidden_count, feats // count).T,
        summed[15, : grad_w2.size].reshape(grad_w2.shape),
        jnp.concatenate([summed[8:11], summed[0:1]], axis=0),
        jnp.concatenate([summed[11:14], summed[1:2]], axis=0),
        shard_qkv,
        summed[16, : grad_qkv_bias.size].reshape(grad_qkv_bias.shape),
        shard_out,
        summed[2],
        shard_up,
        summed[17, : up_bias.size],
        shard_down,
        summed[18],
    )


def solution(mesh):
    in_specs = (
        P(None, "dp", "seq", None),
        P("dp", "seq"),
        P("dp"),
        P("dp", "seq", None),
        P(),
        P(("dp", "seq"), None),
        P(),
        P(),
        P(),
        P(None, ("dp", "seq"), "tensor"),
        P(None, "tensor"),
        P(("dp", "seq"), "tensor"),
        P(),
        P(("dp", "seq"), "tensor"),
        P("tensor"),
        P(("dp", "seq"), "tensor"),
        P(),
    )
    out_specs = (
        P("dp", "seq", None),
        P(None, "dp", "seq", None),
        P(),
        P(("dp", "seq"), None),
        P(),
        P(),
        P(),
        P(None, ("dp", "seq"), "tensor"),
        P(None, "tensor"),
        P(("dp", "seq"), "tensor"),
        P(),
        P(("dp", "seq"), "tensor"),
        P("tensor"),
        P(("dp", "seq"), "tensor"),
        P(),
    )
    return jax.shard_map(shards, mesh=mesh, in_specs=in_specs, out_specs=out_specs, check_vma=False)
```
